32 devices in a mesh: dp: 4 (over x, core), mem: 8 (over z, y).
Axes of the slice: x: 2, y: 2, z: 4, core: 2. Of those that a mesh axis runs over, the one named last changes fastest.
Arguments:
- text: bfloat16 [256, 64, 768], P(('dp', 'mem')), may hold values from -6 to 6
- lengths: int32 [256], P(('dp', 'mem')), may hold values from 1 to 64, as said below
- memory: bfloat16 [256, 96, 768], P('dp', 'mem'), may hold values from -6 to 6
- out_grad: bfloat16 [256, 64, 768], P(('dp', 'mem')), may hold values from -6 to 6
- self_query: bfloat16 [768, 768], P('dp', 'mem'), may hold values from -0.21875 to 0.21875
- self_key: bfloat16 [768, 768], P('dp', 'mem'), may hold values from -0.21875 to 0.21875
- self_value: bfloat16 [768, 768], P('dp', 'mem'), may hold values from -0.21875 to 0.21875
- self_output: bfloat16 [768, 768], P('dp', 'mem'), may hold values from -0.5 to 0.5
- cross_query: bfloat16 [768, 768], P('dp', 'mem'), may hold values from -0.21875 to 0.21875
- cross_key: bfloat16 [768, 768], P('dp', 'mem'), may hold values from -0.21875 to 0.21875
- cross_value: bfloat16 [768, 768], P('dp', 'mem'), may hold values from -0.21875 to 0.21875
- cross_output: bfloat16 [768, 768], P('dp', 'mem'), may hold values from -0.75 to 0.75
- hidden_in: bfloat16 [768, 3072], P('dp', 'mem'), may hold values from -0.21875 to 0.21875
- hidden_out: bfloat16 [3072, 768], P('dp', 'mem'), may hold values from -0.109375 to 0.109375
- first_gain: float32 [768], replicated, may hold values from 0.5 to 1.5
- first_shift: float32 [768], replicated, may hold values from -3 to 3
- second_gain: float32 [768], replicated, may hold values from 0.5 to 1.5
- second_shift: float32 [768], replicated, may hold values from -3 to 3
- third_gain: float32 [768], replicated, may hold values from 0.5 to 1.5
- third_shift: float32 [768], replicated, may hold values from -3 to 3
Outputs:
- layer_out: bfloat16 [256, 64, 768], P(('dp', 'mem'))
- text_grad: bfloat16 [256, 64, 768], P(('dp', 'mem'))
- memory_grad: bfloat16 [256, 96, 768], P('dp', 'mem')
- self_query_grad: float32 [768, 768], P('dp', 'mem')
- self_key_grad: float32 [768, 768], P('dp', 'mem')
- self_value_grad: float32 [768, 768], P('dp', 'mem')
- self_output_grad: float32 [768, 768], P('dp', 'mem')
- cross_query_grad: float32 [768, 768], P('dp', 'mem')
- cross_key_grad: float32 [768, 768], P('dp', 'mem')
- cross_value_grad: float32 [768, 768], P('dp', 'mem')
- cross_output_grad: float32 [768, 768], P('dp', 'mem')
- hidden_in_grad: float32 [768, 3072], P('dp', 'mem')
- hidden_out_grad: float32 [3072, 768], P('dp', 'mem')
- first_gain_grad: float32 [768], replicated
- first_shift_grad: float32 [768], replicated
- second_gain_grad: float32 [768], replicated
- second_shift_grad: float32 [768], replicated
- third_gain_grad: float32 [768], replicated
- third_shift_grad: float32 [768], replicated
The draws below stay inside these ranges and needn't reach their ends.
Inputs may be any that keep to these rules, and one draw needn't show every extreme that they name: `lengths`: each image's caption length; slots at and beyond it are padding; some image has 64 and some has 1.
All inputs are finite; a program needn't handle non-finite values.
Results may differ from the reference program's by a relative error of at most 0.023.
Values may be sent and summed in bfloat16 or wider, within the bound.
A program may use at most 192 MiB of HBM per device.

```python
import jax
import jax.numpy as jnp
from jax import lax

D = 768
HEADS = 12
HEAD = 64
FF = 3072
TXT = 64
IMG_DEV = 8
MEMLEN = 96
IMAGES = 256


def draw_lengths(key, part):
    first_key, second_key, third_key = jax.random.split(key, 3)
    divisor = jax.random.randint(first_key, (IMAGES,), 1, 3)
    reduction = jax.random.randint(second_key, (IMAGES,), 0, TXT // 4)
    base_len = jnp.maximum(TXT // divisor - reduction, 1)
    chosen = jax.random.randint(third_key, (), 0, IMAGES)
    places = jnp.arange(IMAGES)
    base_len = jnp.where(places == chosen, TXT, base_len)
    base_len = jnp.where(places == (chosen + 1) % IMAGES, 1, base_len)
    return base_len.astype(jnp.int32)


def levels(rng, dims, cuts, smallest, top_value):
    level, own = 1.0, jax.random.fold_in(rng, 6)
    for position, parts in cuts:
        heights = jnp.exp(jax.random.uniform(jax.random.fold_in(own, position), (parts,), jnp.float32, smallest / len(cuts), top_value / len(cuts)))
        level = level * jnp.repeat(heights, dims[position] // parts).reshape([-1 if axis == position else 1 for axis in range(len(dims))])
    return level


def gaussian(stream_key, extent, scale, limit, pieces=(), held_as=jnp.bfloat16):
    result = scale * jax.random.normal(stream_key, extent, jnp.float32)
    if pieces:
        result = result * levels(stream_key, extent, pieces, -0.22, 0.18)
    return jnp.clip(result, -limit, limit).astype(held_as)


def setup_inputs(seed: int = 0) -> dict:
    arg_keys = jax.random.split(jax.random.key(seed), 21)
    return {
        "text": gaussian(arg_keys[0], (IMAGES, TXT, D), 1.0, 6.0, ((0, 32),)),
        "lengths": draw_lengths(jax.random.fold_in(arg_keys[20], 71), 0),
        "memory": gaussian(arg_keys[2], (IMAGES, MEMLEN, D), 1.0, 6.0, ((0, 4), (1, 8))),
        "out_grad": gaussian(arg_keys[3], (IMAGES, TXT, D), 1.0, 6.0, ((0, 32),)),
        "self_query": gaussian(arg_keys[4], (D, D), D ** -0.5, 0.21875, ((0, 4), (1, 8))),
        "self_key": gaussian(arg_keys[5], (D, D), D ** -0.5, 0.21875, ((0, 4), (1, 8))),
        "self_value": gaussian(arg_keys[6], (D, D), D ** -0.5, 0.21875, ((0, 4), (1, 8))),
        "self_output": gaussian(arg_keys[7], (D, D), (2 * HEAD) ** -0.5, 0.5, ((0, 4), (1, 8))),
        "cross_query": gaussian(arg_keys[8], (D, D), D ** -0.5, 0.21875, ((0, 4), (1, 8))),
        "cross_key": gaussian(arg_keys[9], (D, D), D ** -0.5, 0.21875, ((0, 4), (1, 8))),
        "cross_value": gaussian(arg_keys[10], (D, D), D ** -0.5, 0.21875, ((0, 4), (1, 8))),
        "cross_output": gaussian(arg_keys[11], (D, D), HEAD ** -0.5, 0.75, ((0, 4), (1, 8))),
        "hidden_in": gaussian(arg_keys[12], (D, FF), D ** -0.5, 0.21875, ((0, 4), (1, 8))),
        "hidden_out": gaussian(arg_keys[13], (FF, D), FF ** -0.5, 0.109375, ((0, 4), (1, 8))),
        "first_gain": jnp.clip(1.0 + 0.1 * jax.random.normal(arg_keys[14], (D,), jnp.float32), 0.5, 1.5),
        "first_shift": gaussian(arg_keys[15], (D,), 0.5, 3.0, (), jnp.float32),
        "second_gain": jnp.clip(1.0 + 0.1 * jax.random.normal(arg_keys[16], (D,), jnp.float32), 0.5, 1.5),
        "second_shift": gaussian(arg_keys[17], (D,), 0.5, 3.0, (), jnp.float32),
        "third_gain": jnp.clip(1.0 + 0.1 * jax.random.normal(arg_keys[18], (D,), jnp.float32), 0.5, 1.5),
        "third_shift": gaussian(arg_keys[19], (D,), 0.5, 3.0, (), jnp.float32),
    }


@jax.custom_vjp
def low(v):
    return lax.optimization_barrier(v.astype(jnp.bfloat16)).astype(jnp.float32)

@jax.custom_vjp
def low_back(v):
    return v

def low_keep(v):
    return (low(v), None)

def low_pass(kept, grad):
    return (grad,)

def back_keep(v):
    return (v, None)

def back_low(kept, grad):
    return (low(grad),)
low.defvjp(low_keep, low_pass)
low_back.defvjp(back_keep, back_low)
EPS = 1e-06
NEG = -1e+30
HIGH = lax.Precision.HIGHEST

def layer_norm(values, scaling, offsets):
    center = values - lax.optimization_barrier(jnp.mean(values, axis=-1, keepdims=True))
    spread = lax.optimization_barrier(jnp.mean(center * center, axis=-1, keepdims=True))
    return center * lax.rsqrt(spread + EPS) * scaling + offsets

def apply_mat(acts, matrix):
    return jnp.einsum('bsd,de->bse', acts, matrix, precision=HIGH)

def split_heads(values):
    return values.reshape(values.shape[0], values.shape[1], HEADS, HEAD)

def attend(queries, keys, values, allowed):
    score_scale = HEAD ** (-0.5)
    scores = jnp.einsum('bshd,bthd->bhst', split_heads(queries), split_heads(keys), precision=HIGH) * score_scale
    if allowed is not None:
        scores = jnp.where(allowed, scores, NEG)
    scores = low_back(scores)
    weights = low(jax.nn.softmax(scores, axis=-1))
    mixed_heads = jnp.einsum('bhst,bthd->bshd', weights, split_heads(values), precision=HIGH)
    joined = mixed_heads.reshape(mixed_heads.shape[0], mixed_heads.shape[1], HEADS * HEAD)
    return low(low_back(joined))

def block(params, text_rows, memory_rows, length_rows):
    w_query, w_key, w_value, w_output, m_query, m_key, m_value, m_output, w_in, w_out, gain_one, shift_one, gain_two, shift_two, gain_three, shift_three = params
    places = jnp.arange(text_rows.shape[1])
    valid_row = places[None, :] < length_rows[:, None]
    allowed = (places[None, :] <= places[:, None])[None, None] & valid_row[:, None, None, :]
    first = low(layer_norm(text_rows, gain_one, shift_one))
    queries = low(low_back(apply_mat(first, w_query)))
    keys = low(low_back(apply_mat(first, w_key)))
    values = low(low_back(apply_mat(first, w_value)))
    after_self = text_rows + low_back(apply_mat(attend(queries, keys, values, allowed), w_output))
    second = low(layer_norm(after_self, gain_two, shift_two))
    cross_queries = low(low_back(apply_mat(second, m_query)))
    mem_keys = low(low_back(apply_mat(memory_rows, m_key)))
    mem_values = low(low_back(apply_mat(memory_rows, m_value)))
    after_cross = after_self + low_back(apply_mat(attend(cross_queries, mem_keys, mem_values, None), m_output))
    third = low(layer_norm(after_cross, gain_three, shift_three))
    before_act = low_back(apply_mat(third, w_in))
    activated = low(jax.nn.gelu(before_act))
    final = after_cross + low_back(apply_mat(activated, w_out))
    return jnp.where(valid_row[:, :, None], final, 0.0)

def reference(text, lengths, memory, out_grad, self_query, self_key, self_value, self_output, cross_query, cross_key, cross_value, cross_output, hidden_in, hidden_out, first_gain, first_shift, second_gain, second_shift, third_gain, third_shift):
    mats = (self_query, self_key, self_value, self_output, cross_query, cross_key, cross_value, cross_output, hidden_in, hidden_out)
    params = tuple((matrix.astype(jnp.float32) for matrix in mats)) + (first_gain, first_shift, second_gain, second_shift, third_gain, third_shift)
    groups = text.shape[0] // IMG_DEV

    def run(params_in, text_in, memory_in):
        items = (text_in.reshape(groups, IMG_DEV, TXT, D), memory_in.reshape(groups, IMG_DEV, MEMLEN, D), lengths.reshape(groups, IMG_DEV))

        def one_group(item):
            return block(params_in, item[0], item[1], item[2])
        results = lax.map(jax.checkpoint(one_group), items)
        return results.reshape(text_in.shape)
    final, pull_back = jax.vjp(run, params, text.astype(jnp.float32), memory.astype(jnp.float32))
    param_grads, text_grad, memory_grad = pull_back(out_grad.astype(jnp.float32))
    return (final.astype(jnp.bfloat16), text_grad.astype(jnp.bfloat16), memory_grad.astype(jnp.bfloat16), param_grads[0], param_grads[1], param_grads[2], param_grads[3], param_grads[4], param_grads[5], param_grads[6], param_grads[7], param_grads[8], param_grads[9], param_grads[10], param_grads[11], param_grads[12], param_grads[13], param_grads[14], param_grads[15])
```

```python
import functools

import jax
import jax.numpy as jnp
from jax import lax
from jax.experimental import pallas as pl
from jax.experimental.pallas import tpu as pltpu
from jax.sharding import PartitionSpec as P

HEADS = 12
HEAD = 64
MESH = pl.DeviceIdType.MESH
BF = jnp.bfloat16
F32 = jnp.float32


EPS = 1e-06
NEG = -1e30


def layer_norm(values, scaling, offsets):
    center = values - jnp.mean(values, axis=-1, keepdims=True)
    spread = jnp.mean(center * center, axis=-1, keepdims=True)
    return center * lax.rsqrt(spread + EPS) * scaling + offsets


def norm_back(values, scaling, offsets, upstream):
    _, pull_back = jax.vjp(layer_norm, values, scaling, offsets)
    return pull_back(upstream)


def split_heads(values):
    return values.reshape(values.shape[0], values.shape[1], HEADS, HEAD)


def join_heads(values):
    return values.reshape(values.shape[0], values.shape[1], HEADS * HEAD)


def apply_mat(acts, matrix):
    return jnp.einsum("bsd,de->bse", acts, matrix, preferred_element_type=jnp.float32)


def apply_back(grads, matrix):
    return jnp.einsum("bse,de->bsd", grads, matrix, preferred_element_type=jnp.float32)


def mat_grad(acts, grads):
    return jnp.einsum("bsd,bse->de", acts, grads, preferred_element_type=jnp.float32)


def score_rows(queries, keys, allowed):
    score_scale = HEAD ** (-0.5)
    scores = (
        jnp.einsum(
            "bshd,bthd->bhst",
            split_heads(queries),
            split_heads(keys),
            preferred_element_type=jnp.float32,
        )
        * score_scale
    )
    if allowed is not None:
        scores = jnp.where(allowed, scores, NEG)
    return scores


def attend_fwd(queries, keys, values, allowed):
    scores = score_rows(queries, keys, allowed)
    highest = jnp.max(scores, axis=-1, keepdims=True)
    powered = jnp.exp(scores - highest)
    expo_sum = jnp.sum(powered, axis=-1, keepdims=True)
    weights = (powered / expo_sum).astype(jnp.bfloat16)
    mixed_heads = jnp.einsum(
        "bhst,bthd->bshd", weights, split_heads(values), preferred_element_type=jnp.float32
    )
    return (join_heads(mixed_heads).astype(jnp.bfloat16), highest + jnp.log(expo_sum))


def attend_back(queries, keys, values, allowed, log_sum, upstream):
    score_scale = HEAD ** (-0.5)
    probs_full = jnp.exp(score_rows(queries, keys, allowed) - log_sum)
    heads_up = split_heads(upstream)
    prob_grad = jnp.einsum(
        "bshd,bthd->bhst", heads_up, split_heads(values), preferred_element_type=jnp.float32
    )
    score_low = (
        probs_full * (prob_grad - jnp.sum(prob_grad * probs_full, axis=-1, keepdims=True))
    ).astype(jnp.bfloat16)
    value_grad = jnp.einsum(
        "bhst,bshd->bthd",
        probs_full.astype(jnp.bfloat16),
        heads_up,
        preferred_element_type=jnp.float32,
    )
    query_grad = (
        jnp.einsum(
            "bhst,bthd->bshd", score_low, split_heads(keys), preferred_element_type=jnp.float32
        )
        * score_scale
    )
    key_grad = (
        jnp.einsum(
            "bhst,bshd->bthd", score_low, split_heads(queries), preferred_element_type=jnp.float32
        )
        * score_scale
    )
    return (
        join_heads(query_grad).astype(jnp.bfloat16),
        join_heads(key_grad).astype(jnp.bfloat16),
        join_heads(value_grad).astype(jnp.bfloat16),
    )


def fetch_weights(mats):
    columns = (
        lax.all_gather(mats[0], "mem", axis=1, tiled=True),
        lax.all_gather(mats[1], "mem", axis=1, tiled=True),
        lax.all_gather(mats[2], "mem", axis=1, tiled=True),
        lax.all_gather(mats[3], "mem", axis=1, tiled=True),
        lax.all_gather(mats[4], "mem", axis=1, tiled=True),
        lax.all_gather(mats[5], "mem", axis=1, tiled=True),
        lax.all_gather(mats[6], "mem", axis=1, tiled=True),
        lax.all_gather(mats[7], "mem", axis=1, tiled=True),
        lax.all_gather(mats[8], "mem", axis=1, tiled=True),
        lax.all_gather(mats[9], "mem", axis=1, tiled=True),
    )
    return (
        lax.all_gather(columns[0], "dp", axis=0, tiled=True),
        lax.all_gather(columns[1], "dp", axis=0, tiled=True),
        lax.all_gather(columns[2], "dp", axis=0, tiled=True),
        lax.all_gather(columns[3], "dp", axis=0, tiled=True),
        lax.all_gather(columns[4], "dp", axis=0, tiled=True),
        lax.all_gather(columns[5], "dp", axis=0, tiled=True),
        lax.all_gather(columns[6], "dp", axis=0, tiled=True),
        lax.all_gather(columns[7], "dp", axis=0, tiled=True),
        lax.all_gather(columns[8], "dp", axis=0, tiled=True),
        lax.all_gather(columns[9], "dp", axis=0, tiled=True),
    )


def reduce_all(grads):
    row_sums = (
        lax.psum_scatter(
            grads[0].astype(jnp.bfloat16), "dp", scatter_dimension=0, tiled=True
        ).astype(jnp.float32),
        lax.psum_scatter(
            grads[1].astype(jnp.bfloat16), "dp", scatter_dimension=0, tiled=True
        ).astype(jnp.float32),
        lax.psum_scatter(
            grads[2].astype(jnp.bfloat16), "dp", scatter_dimension=0, tiled=True
        ).astype(jnp.float32),
        lax.psum_scatter(
            grads[3].astype(jnp.bfloat16), "dp", scatter_dimension=0, tiled=True
        ).astype(jnp.float32),
        lax.psum_scatter(
            grads[4].astype(jnp.bfloat16), "dp", scatter_dimension=0, tiled=True
        ).astype(jnp.float32),
        lax.psum_scatter(
            grads[5].astype(jnp.bfloat16), "dp", scatter_dimension=0, tiled=True
        ).astype(jnp.float32),
        lax.psum_scatter(
            grads[6].astype(jnp.bfloat16), "dp", scatter_dimension=0, tiled=True
        ).astype(jnp.float32),
        lax.psum_scatter(
            grads[7].astype(jnp.bfloat16), "dp", scatter_dimension=0, tiled=True
        ).astype(jnp.float32),
        lax.psum_scatter(
            grads[8].astype(jnp.bfloat16), "dp", scatter_dimension=0, tiled=True
        ).astype(jnp.float32),
        lax.psum_scatter(
            grads[9].astype(jnp.bfloat16), "dp", scatter_dimension=0, tiled=True
        ).astype(jnp.float32),
    )
    return (
        lax.psum_scatter(
            row_sums[0].astype(jnp.bfloat16), "mem", scatter_dimension=1, tiled=True
        ).astype(jnp.float32),
        lax.psum_scatter(
            row_sums[1].astype(jnp.bfloat16), "mem", scatter_dimension=1, tiled=True
        ).astype(jnp.float32),
        lax.psum_scatter(
            row_sums[2].astype(jnp.bfloat16), "mem", scatter_dimension=1, tiled=True
        ).astype(jnp.float32),
        lax.psum_scatter(
            row_sums[3].astype(jnp.bfloat16), "mem", scatter_dimension=1, tiled=True
        ).astype(jnp.float32),
        lax.psum_scatter(
            row_sums[4].astype(jnp.bfloat16), "mem", scatter_dimension=1, tiled=True
        ).astype(jnp.float32),
        lax.psum_scatter(
            row_sums[5].astype(jnp.bfloat16), "mem", scatter_dimension=1, tiled=True
        ).astype(jnp.float32),
        lax.psum_scatter(
            row_sums[6].astype(jnp.bfloat16), "mem", scatter_dimension=1, tiled=True
        ).astype(jnp.float32),
        lax.psum_scatter(
            row_sums[7].astype(jnp.bfloat16), "mem", scatter_dimension=1, tiled=True
        ).astype(jnp.float32),
        lax.psum_scatter(
            row_sums[8].astype(jnp.bfloat16), "mem", scatter_dimension=1, tiled=True
        ).astype(jnp.float32),
        lax.psum_scatter(
            row_sums[9].astype(jnp.bfloat16), "mem", scatter_dimension=1, tiled=True
        ).astype(jnp.float32),
    )


class Place:
    def __init__(self):
        self.d = lax.axis_index("dp")
        self.m = lax.axis_index("mem")
        self.c = lax.rem(self.d, 2)
        self.x = lax.div(self.d, 2)
        self.y = lax.rem(self.m, 2)
        self.z = lax.div(self.m, 2)
        self.oc, self.ox, self.oy = 1 - self.c, 1 - self.x, 1 - self.y
        self.sib = (self.x * 2 + self.oc, self.m)
        self.xn = (self.ox * 2 + self.c, self.m)
        self.yn = (self.d, self.z * 2 + self.oy)

    def zup(self, k):
        return lax.rem(self.z + k, 4)

    def zpeer(self, k):
        return (self.d, self.zup(k) * 2 + self.y)

    def mpeer(self, k):
        return (self.d, lax.rem(self.m + k, 8))


def greet(at):
    barrier = pltpu.get_barrier_semaphore()
    for peer in [at.sib, at.xn] + [at.mpeer(k) for k in range(1, 8)]:
        pl.semaphore_signal(barrier, inc=1, device_id=peer, device_id_type=MESH)
    pl.semaphore_wait(barrier, 9)


def remote(src, dst, sends, recvs, idx, peer):
    return pltpu.make_async_remote_copy(
        src_ref=src,
        dst_ref=dst,
        send_sem=sends.at[idx],
        recv_sem=recvs.at[idx],
        device_id=peer,
        device_id_type=MESH,
    )


class Gather:
    def __init__(self, at, full, span, stage, sends, recvs, base):
        self.at, self.full, self.span, self.stage = at, full, span, stage
        self.sends, self.recvs, self.base = sends, recvs, base
        self.lanes = full.shape[-1] // 2
        self.out = []

    def piece(self, z, y, h, x):
        lo = pl.multiple_of(x * self.lanes, 128)
        return self.full.at[self.span, z, y, h, :, pl.ds(lo, self.lanes)]

    def copy(self, slot, src, dst, peer):
        return remote(src, dst, self.sends, self.recvs, self.base + slot, peer)

    def send(self, slot, src, dst, peer):
        copy = self.copy(slot, src, dst, peer)
        copy.start()
        self.out.append(copy)

    def got(self, slot, ref):
        self.copy(slot, ref, ref, self.at.sib).wait_recv()

    def begin(self):
        at = self.at
        own = self.piece(at.z, at.y, at.c, at.x)
        for k in (1, 2, 3):
            self.send(k - 1, self.stage, own, at.zpeer(k))
        self.send(3, self.stage, own, at.xn)
        self.send(7, self.stage, own, at.yn)
        self.send(13, self.stage, own, at.sib)

    def second(self):
        at = self.at
        for k in (1, 2, 3):
            ref = self.piece(at.zup(4 - k), at.y, at.c, at.x)
            self.got(k - 1, ref)
            self.send(3 + k, ref, ref, at.xn)
            self.send(7 + k, ref, ref, at.yn)
            self.send(13 + k, ref, ref, at.sib)

    def third(self):
        at = self.at
        for k in range(4):
            self.got(3 + k, self.piece(at.zup(4 - k), at.y, at.c, at.ox))
        ref = self.piece(pl.ds(0, 2), at.y, at.c, at.ox)
        self.send(11, ref, ref, at.yn)
        ref = self.piece(slice(None), at.y, at.c, at.ox)
        self.send(17, ref, ref, at.sib)
        for k in range(4):
            self.got(7 + k, self.piece(at.zup(4 - k), at.oy, at.c, at.x))
        ref = self.piece(pl.ds(2, 2), at.oy, at.c, at.x)
        self.send(12, ref, ref, at.xn)
        ref = self.piece(slice(None), at.oy, at.c, at.x)
        self.send(18, ref, ref, at.sib)

    def fourth(self):
        at = self.at
        for half in range(2):
            ref = self.piece(pl.ds(2 * half, 2), at.oy, at.c, at.ox)
            self.got(11 + half, ref)
            self.send(19 + half, ref, ref, at.sib)

    def last(self):
        at = self.at
        for k in range(4):
            self.got(13 + k, self.piece(at.zup(4 - k), at.y, at.oc, at.x))
        self.got(17, self.piece(slice(None), at.y, at.oc, at.ox))
        self.got(18, self.piece(slice(None), at.oy, at.oc, at.x))
        for half in range(2):
            self.got(19 + half, self.piece(pl.ds(2 * half, 2), at.oy, at.oc, at.ox))

    def drain(self):
        for copy in self.out:
            copy.wait_send()
        self.out = []


GATHER_SLOTS = 21


class Reduce:
    def __init__(self, at, full, span, bufs, sends, recvs, base):
        self.at, self.full, self.span = at, full, span
        self.chip, self.rdiag, self.rx, self.ry, self.rz, self.fin = bufs
        self.sends, self.recvs, self.base = sends, recvs, base
        self.lanes = full.shape[-1] // 2
        self.count = self.chip.shape[0]
        self.out = []

    send, got, copy, drain = Gather.send, Gather.got, Gather.copy, Gather.drain

    def begin(self):
        at = self.at
        for x in range(2):
            src = self.full.at[
                self.span, :, :, at.oc, :, x * self.lanes : (x + 1) * self.lanes
            ]
            self.send(x, src, self.chip.at[:, x], at.sib)

    def second(self):
        at = self.at
        chip, full, lanes, w0 = self.chip, self.full, self.lanes, self.span.start
        for x in range(2):
            self.got(x, chip.at[:, x])

        def add(i, carry):
            w, r = lax.div(i, 8), lax.rem(i, 8)
            z, y = lax.div(r, 2), lax.rem(r, 2)
            for x in range(2):
                mine = full[w0 + w, z, y, at.c, :, x * lanes : (x + 1) * lanes]
                chip[w, x, z, y] = (
                    chip[w, x, z, y].astype(F32) + mine.astype(F32)
                ).astype(BF)
            return carry

        lax.fori_loop(0, 8 * self.count, add, 0)
        self.send(2, chip.at[:, at.ox, pl.ds(0, 2), at.oy], self.rdiag.at[0], at.yn)
        self.send(3, chip.at[:, at.ox, pl.ds(2, 2), at.oy], self.rdiag.at[1], at.xn)

    def third(self):
        at, chip = self.at, self.chip
        for half in range(2):
            self.got(2 + half, self.rdiag.at[half])
            x, y = ((at.ox, at.y), (at.x, at.oy))[half]

            def add(i, carry, x=x, y=y, half=half):
                w, z = lax.div(i, 2), lax.rem(i, 2)
                chip[w, x, 2 * half + z, y] = (
                    chip[w, x, 2 * half + z, y].astype(F32)
                    + self.rdiag[half, w, z].astype(F32)
                ).astype(BF)
                return carry

            lax.fori_loop(0, 2 * self.count, add, 0)
        self.send(4, chip.at[:, at.ox, :, at.y], self.rx, at.xn)
        self.send(5, chip.at[:, at.x, :, at.oy], self.ry, at.yn)

    def fourth(self):
        at, chip = self.at, self.chip
        self.got(4, self.rx)
        self.got(5, self.ry)

        def add(i, carry):
            w, z = lax.div(i, 4), lax.rem(i, 4)
            chip[w, at.x, z, at.y] = (
                chip[w, at.x, z, at.y].astype(F32)
                + self.rx[w, z].astype(F32)
                + self.ry[w, z].astype(F32)
            ).astype(BF)
            return carry

        lax.fori_loop(0, 4 * self.count, add, 0)
        for k in (1, 2, 3):
            self.send(
                5 + k, chip.at[:, at.x, at.zup(k), at.y], self.rz.at[k - 1], at.zpeer(k)
            )

    def fifth(self):
        at = self.at
        for k in (1, 2, 3):
            self.got(5 + k, self.rz.at[k - 1])

        def add(w, carry):
            total = self.chip[w, at.x, at.z, at.y].astype(F32)
            for k in range(3):
                total = total + self.rz[k, w].astype(F32)
            self.fin[at.c, w] = total.astype(BF)
            return carry

        lax.fori_loop(0, self.count, add, 0)
        self.send(9, self.fin.at[at.c], self.fin.at[at.c], at.sib)

    def last(self):
        self.got(9, self.fin.at[self.at.oc])


REDUCE_SLOTS = 10


def reduce_bufs(count, rows, lanes):
    return [
        pltpu.VMEM((count, 2, 4, 2, rows, lanes), BF),
        pltpu.VMEM((2, count, 2, rows, lanes), BF),
        pltpu.VMEM((count, 4, rows, lanes), BF),
        pltpu.VMEM((count, 4, rows, lanes), BF),
        pltpu.VMEM((3, count, rows, lanes), BF),
        pltpu.VMEM((2, count, rows, lanes), BF),
    ]


def pick(rows, cols, start):
    col = lax.broadcasted_iota(jnp.int32, (rows, cols), 1)
    row = lax.broadcasted_iota(jnp.int32, (rows, cols), 0)
    return jnp.where(col == row + start, 1.0, 0.0).astype(BF)


def dot_nt(a, b):
    return lax.dot_general(a, b, (((1,), (1,)), ((), ())), preferred_element_type=F32)


def gather_kernel(*refs):
    shards, rows = refs[:10], refs[10]
    out_s, out_in, out_out, out_rows = refs[11:15]
    (full_s, full_in, full_out, pair_s, pair_in, pair_out, stage_s, stage_in, stage_out,
     psend, precv, gsend, grecv, rsend, rrecv, local) = refs[15:]
    at = Place()
    greet(at)
    pairs = [pair_s.at[i] for i in range(8)] + [pair_in, pair_out]
    own, other = [], []
    for i in range(10):
        depth = shards[i].shape[0]
        mine = pairs[i].at[pl.ds(pl.multiple_of(at.c * depth, 8), depth), :]
        copy = remote(shards[i], mine, psend, precv, i, at.sib)
        copy.start()
        other.append(copy)
        copy = pltpu.make_async_copy(shards[i], mine, local.at[i])
        copy.start()
        own.append(copy)

    def ready(i):
        own[i].wait()
        depth = shards[i].shape[0]
        theirs = pairs[i].at[pl.ds(pl.multiple_of(at.oc * depth, 8), depth), :]
        remote(theirs, theirs, psend, precv, i, at.sib).wait_recv()

    groups = [
        Gather(at, full_s, slice(0, 3), stage_s.at[0:3], gsend, grecv, 0),
        Gather(at, full_s, slice(3, 8), stage_s.at[3:8], gsend, grecv, GATHER_SLOTS),
        Gather(at, full_in, slice(0, 1), stage_in, gsend, grecv, 2 * GATHER_SLOTS),
        Gather(at, full_out, slice(0, 1), stage_out, gsend, grecv, 3 * GATHER_SLOTS),
    ]
    locals_ = []
    for g, group in enumerate(groups):
        if g < 2:
            half = stage_s.shape[1]
            sel = pick(half, 2 * half, at.c * half)
            for i in range(group.span.start, group.span.stop):
                ready(i)
                stage_s[i] = dot_nt(sel, pair_s[i]).astype(BF)
        else:
            ready(6 + g)
            stage, pair = ((stage_in, pair_in), (stage_out, pair_out))[g - 2]
            half = stage.shape[1]
            stage[0] = dot_nt(pick(half, 2 * half, at.c * half), pair[...]).astype(BF)
        group.begin()
        copy = pltpu.make_async_copy(
            group.stage, group.piece(at.z, at.y, at.c, at.x), local.at[10 + g]
        )
        copy.start()
        locals_.append(copy)
    mems = []
    for k in range(1, 8):
        to = lax.rem(at.m + k, 8)
        copy = remote(rows.at[to], out_rows.at[at.m], rsend, rrecv, k - 1, at.mpeer(k))
        copy.start()
        mems.append(copy)
    copy = pltpu.make_async_copy(rows.at[at.m], out_rows.at[at.m], local.at[14])
    copy.start()
    locals_.append(copy)
    for group in groups:
        group.second()
    for group in groups:
        group.third()
    for group in groups:
        group.fourth()
    for group in groups:
        group.last()
    for k in range(1, 8):
        ref = out_rows.at[lax.rem(at.m + 8 - k, 8)]
        remote(ref, ref, rsend, rrecv, k - 1, at.sib).wait_recv()
    for copy in locals_:
        copy.wait()
    ends = []
    for i, (a, b) in enumerate(
        ((full_s, out_s), (full_in, out_in), (full_out, out_out))
    ):
        copy = pltpu.make_async_copy(a, b, local.at[i])
        copy.start()
        ends.append(copy)
    for copy in ends:
        copy.wait()
    for copy in other + mems:
        copy.wait_send()
    for group in groups:
        group.drain()


def gather_all(shards, rows):
    depth, width = shards[0].shape
    dmodel = depth * 4
    half = width // 2
    half_in = shards[8].shape[1] // 2
    ff = half_in * 16
    shapes = [
        (8, 4, 2, 2, half, dmodel),
        (1, 4, 2, 2, half_in, dmodel),
        (1, 4, 2, 2, half, ff),
    ]
    any_ = pl.BlockSpec(memory_space=pl.ANY)
    return pl.pallas_call(
        gather_kernel,
        out_shape=[jax.ShapeDtypeStruct(s, BF) for s in shapes]
        + [jax.ShapeDtypeStruct(rows.shape, BF)],
        in_specs=[any_] * 11,
        out_specs=[any_] * 4,
        scratch_shapes=[pltpu.VMEM(s, BF) for s in shapes]
        + [
            pltpu.VMEM((8, 2 * depth, width), BF),
            pltpu.VMEM((2 * depth, 2 * half_in), BF),
            pltpu.VMEM((ff // 2, width), BF),
            pltpu.VMEM((8, half, 2 * depth), BF),
            pltpu.VMEM((1, half_in, 2 * depth), BF),
            pltpu.VMEM((1, half, ff // 2), BF),
            pltpu.SemaphoreType.DMA((10,)),
            pltpu.SemaphoreType.DMA((10,)),
            pltpu.SemaphoreType.DMA((4 * GATHER_SLOTS,)),
            pltpu.SemaphoreType.DMA((4 * GATHER_SLOTS,)),
            pltpu.SemaphoreType.DMA((7,)),
            pltpu.SemaphoreType.DMA((7,)),
            pltpu.SemaphoreType.DMA((15,)),
        ],
        compiler_params=pltpu.CompilerParams(
            collective_id=0, has_side_effects=True, vmem_limit_bytes=60 << 20
        ),
    )(*shards, rows)


def reduce_kernel(*refs):
    in_s, in_in, in_out, rows = refs[:4]
    outs, out_rows = refs[4:14], refs[14]
    full_s, full_in, full_out = refs[15:18]
    bufs = [refs[18 + 6 * g : 24 + 6 * g] for g in range(3)]
    gsend, grecv, rsend, rrecv, local = refs[36:]
    at = Place()
    loads = []
    for i, (a, b) in enumerate(((in_out, full_out), (in_in, full_in), (in_s, full_s))):
        copy = pltpu.make_async_copy(a, b, local.at[i])
        copy.start()
        loads.append(copy)
    greet(at)
    groups = [
        Reduce(at, full_out, slice(0, 1), bufs[0], gsend, grecv, 0),
        Reduce(at, full_in, slice(0, 1), bufs[1], gsend, grecv, REDUCE_SLOTS),
        Reduce(at, full_s, slice(0, 8), bufs[2], gsend, grecv, 2 * REDUCE_SLOTS),
    ]
    for load, group in zip(loads, groups):
        load.wait()
        group.begin()
    mems = []
    for k in range(1, 8):
        to = lax.rem(at.m + k, 8)
        copy = remote(rows.at[to], out_rows.at[at.m], rsend, rrecv, k - 1, at.mpeer(k))
        copy.start()
        mems.append(copy)
    own = pltpu.make_async_copy(rows.at[at.m], out_rows.at[at.m], local.at[3])
    own.start()
    for group in groups:
        group.second()
    for group in groups:
        group.third()
    for group in groups:
        group.fourth()
    for group in groups:
        group.fifth()
    for group in groups:
        group.last()
    fin_out, fin_in, fin_s = (group.fin for group in groups)

    def lay(out, fin, w):
        both = jnp.concatenate([fin[0, w], fin[1, w]], axis=0)
        depth = out.shape[0]
        out[...] = dot_nt(pick(depth, 2 * depth, at.c * depth), both)

    for w in range(8):
        lay(outs[w], fin_s, w)
    lay(outs[8], fin_in, 0)
    lay(outs[9], fin_out, 0)
    own.wait()
    for k in range(1, 8):
        ref = out_rows.at[lax.rem(at.m + 8 - k, 8)]
        remote(ref, ref, rsend, rrecv, k - 1, at.sib).wait_recv()
    for copy in mems:
        copy.wait_send()
    for group in groups:
        group.drain()


def reduce_everything(full_s, full_in, full_out, rows, shapes):
    half, dmodel = full_s.shape[-2:]
    half_in = full_in.shape[-2]
    ff = full_out.shape[-1]
    any_ = pl.BlockSpec(memory_space=pl.ANY)
    vmem = pl.BlockSpec(memory_space=pltpu.VMEM)
    return pl.pallas_call(
        reduce_kernel,
        out_shape=[jax.ShapeDtypeStruct(s, F32) for s in shapes]
        + [jax.ShapeDtypeStruct(rows.shape, BF)],
        in_specs=[any_] * 4,
        out_specs=[vmem] * 10 + [any_],
        scratch_shapes=[pltpu.VMEM(a.shape, BF) for a in (full_s, full_in, full_out)]
        + reduce_bufs(1, half, ff // 2)
        + reduce_bufs(1, half_in, dmodel // 2)
        + reduce_bufs(8, half, dmodel // 2)
        + [
            pltpu.SemaphoreType.DMA((3 * REDUCE_SLOTS,)),
            pltpu.SemaphoreType.DMA((3 * REDUCE_SLOTS,)),
            pltpu.SemaphoreType.DMA((7,)),
            pltpu.SemaphoreType.DMA((7,)),
            pltpu.SemaphoreType.DMA((4,)),
        ],
        compiler_params=pltpu.CompilerParams(
            collective_id=1, has_side_effects=True, vmem_limit_bytes=60 << 20
        ),
    )(full_s, full_in, full_out, rows)


def apply_t(acts, matrix):
    return jnp.einsum("bsd,ed->bse", acts, matrix, preferred_element_type=F32)


def apply_back_t(grads, matrix):
    return jnp.einsum("bse,ed->bsd", grads, matrix, preferred_element_type=F32)


def mat_grad_t(acts, grads):
    return jnp.einsum("bse,bsd->ed", grads, acts, preferred_element_type=F32)

def shards_lean(
    text,
    lengths,
    memory,
    out_grad,
    self_query,
    self_key,
    self_value,
    self_output,
    cross_query,
    cross_key,
    cross_value,
    cross_output,
    hidden_in,
    hidden_out,
    first_gain,
    first_shift,
    second_gain,
    second_shift,
    third_gain,
    third_shift,
):
    mats = (
        self_query,
        self_key,
        self_value,
        self_output,
        cross_query,
        cross_key,
        cross_value,
        cross_output,
        hidden_in,
        hidden_out,
    )
    owners, length = memory.shape[0] // 8, memory.shape[1]
    dmodel = memory.shape[2]
    full_s, full_in, full_out, landed = gather_all(mats, memory.reshape(8, owners * length, dmodel))
    full_mats = tuple(full_s.reshape(8, dmodel, dmodel)) + (full_in.reshape(-1, dmodel), full_out.reshape(dmodel, -1))
    w_query, w_key, w_value, w_output, m_query, m_key, m_value, m_output, w_in, w_out = full_mats
    places = jnp.arange(text.shape[1])
    valid_row = places[None, :] < lengths[:, None]
    allowed = (places[None, :] <= places[:, None])[None, None] & valid_row[:, None, None, :]
    residual = text.astype(jnp.float32)
    first = layer_norm(residual, first_gain, first_shift).astype(jnp.bfloat16)
    queries = apply_t(first, w_query).astype(jnp.bfloat16)
    keys = apply_t(first, w_key).astype(jnp.bfloat16)
    values = apply_t(first, w_value).astype(jnp.bfloat16)
    self_mixed, self_lse = attend_fwd(queries, keys, values, allowed)
    after_self = residual + apply_t(self_mixed, w_output)
    memory_rows = landed.reshape(8, owners, length, dmodel).transpose(1, 0, 2, 3).reshape(owners, 8 * length, dmodel)
    second = layer_norm(after_self, second_gain, second_shift).astype(jnp.bfloat16)
    cross_queries = apply_t(second, m_query).astype(jnp.bfloat16)
    mem_keys = apply_t(memory_rows, m_key).astype(jnp.bfloat16)
    mem_values = apply_t(memory_rows, m_value).astype(jnp.bfloat16)
    cross_mixed, cross_lse = attend_fwd(cross_queries, mem_keys, mem_values, None)
    after_cross = after_self + apply_t(cross_mixed, m_output)
    third = layer_norm(after_cross, third_gain, third_shift).astype(jnp.bfloat16)
    before_act = apply_t(third, w_in)
    activated = jax.nn.gelu(before_act).astype(jnp.bfloat16)
    final = after_cross + apply_t(activated, w_out)
    layer_out = jnp.where(valid_row[:, :, None], final, 0.0).astype(jnp.bfloat16)
    b_query, b_key, b_value, b_output, n_query, n_key, n_value, n_output, b_in, b_out = full_mats
    grad_top = jnp.where(valid_row[:, :, None], out_grad.astype(jnp.float32), 0.0)
    top_low = grad_top.astype(jnp.bfloat16)
    hidden_out_grad = mat_grad_t(activated, top_low)
    _, gelu_pull = jax.vjp(jax.nn.gelu, before_act)
    act_low = gelu_pull(apply_back_t(top_low, b_out))[0].astype(jnp.bfloat16)
    hidden_in_grad = mat_grad_t(third, act_low)
    cross_input, third_gain_grad, third_shift_grad = norm_back(
        after_cross, third_gain, third_shift, apply_back_t(act_low, b_in)
    )
    grad_cross = grad_top + cross_input
    cross_low = grad_cross.astype(jnp.bfloat16)
    cross_output_grad = mat_grad_t(cross_mixed, cross_low)
    mixed_up = apply_back_t(cross_low, n_output).astype(jnp.bfloat16)
    cross_query_low, mem_key_low, mem_value_low = attend_back(
        cross_queries, mem_keys, mem_values, None, cross_lse, mixed_up
    )
    cross_query_grad = mat_grad_t(second, cross_query_low)
    cross_key_grad = mat_grad_t(memory_rows, mem_key_low)
    cross_value_grad = mat_grad_t(memory_rows, mem_value_low)
    mem_back = (apply_back_t(mem_key_low, n_key) + apply_back_t(mem_value_low, n_value)).astype(
        jnp.bfloat16
    )
    mem_back = mem_back.reshape(owners, 8, length, dmodel).transpose(1, 0, 2, 3).reshape(8, owners * length, dmodel)
    self_input, second_gain_grad, second_shift_grad = norm_back(
        after_self, second_gain, second_shift, apply_back_t(cross_query_low, n_query)
    )
    grad_self = grad_cross + self_input
    self_low = grad_self.astype(jnp.bfloat16)
    self_output_grad = mat_grad_t(self_mixed, self_low)
    self_up = apply_back_t(self_low, b_output).astype(jnp.bfloat16)
    query_low, key_low, value_low = attend_back(queries, keys, values, allowed, self_lse, self_up)
    self_query_grad = mat_grad_t(first, query_low)
    self_key_grad = mat_grad_t(first, key_low)
    self_value_grad = mat_grad_t(first, value_low)
    first_up = (
        apply_back_t(query_low, b_query) + apply_back_t(key_low, b_key) + apply_back_t(value_low, b_value)
    )
    text_input, first_gain_grad, first_shift_grad = norm_back(
        residual, first_gain, first_shift, first_up
    )
    text_grad = (grad_self + text_input).astype(jnp.bfloat16)
    small = jnp.stack(
        [
            self_query_grad,
            self_key_grad,
            self_value_grad,
            self_output_grad,
            cross_query_grad,
            cross_key_grad,
            cross_value_grad,
            cross_output_grad,
        ]
    ).astype(BF)
    *weight_sums, back = reduce_everything(
        small.reshape(full_s.shape),
        hidden_in_grad.astype(BF).reshape(full_in.shape),
        hidden_out_grad.astype(BF).reshape(full_out.shape),
        mem_back,
        [mat.shape for mat in mats],
    )
    memory_grad = back.reshape(memory.shape)
    norm_sums = lax.psum(
        (
            first_gain_grad,
            first_shift_grad,
            second_gain_grad,
            second_shift_grad,
            third_gain_grad,
            third_shift_grad,
        ),
        ("dp", "mem"),
    )
    return (
        layer_out,
        text_grad,
        memory_grad,
        weight_sums[0],
        weight_sums[1],
        weight_sums[2],
        weight_sums[3],
        weight_sums[4],
        weight_sums[5],
        weight_sums[6],
        weight_sums[7],
        weight_sums[8],
        weight_sums[9],
        norm_sums[0],
        norm_sums[1],
        norm_sums[2],
        norm_sums[3],
        norm_sums[4],
        norm_sums[5],
    )


def shards(
    text,
    lengths,
    memory,
    out_grad,
    self_query,
    self_key,
    self_value,
    self_output,
    cross_query,
    cross_key,
    cross_value,
    cross_output,
    hidden_in,
    hidden_out,
    first_gain,
    first_shift,
    second_gain,
    second_shift,
    third_gain,
    third_shift,
):
    mats = (
        self_query,
        self_key,
        self_value,
        self_output,
        cross_query,
        cross_key,
        cross_value,
        cross_output,
        hidden_in,
        hidden_out,
    )
    full_mats = fetch_weights(mats)
    w_query, w_key, w_value, w_output, m_query, m_key, m_value, m_output, w_in, w_out = full_mats
    places = jnp.arange(text.shape[1])
    valid_row = places[None, :] < lengths[:, None]
    allowed = (places[None, :] <= places[:, None])[None, None] & valid_row[:, None, None, :]
    residual = text.astype(jnp.float32)
    first = layer_norm(residual, first_gain, first_shift).astype(jnp.bfloat16)
    queries = apply_mat(first, w_query).astype(jnp.bfloat16)
    keys = apply_mat(first, w_key).astype(jnp.bfloat16)
    values = apply_mat(first, w_value).astype(jnp.bfloat16)
    self_mixed, self_lse = attend_fwd(queries, keys, values, allowed)
    after_self = residual + apply_mat(self_mixed, w_output)
    memory_rows = lax.all_to_all(memory, "mem", split_axis=0, concat_axis=1, tiled=True)
    second = layer_norm(after_self, second_gain, second_shift).astype(jnp.bfloat16)
    cross_queries = apply_mat(second, m_query).astype(jnp.bfloat16)
    mem_keys = apply_mat(memory_rows, m_key).astype(jnp.bfloat16)
    mem_values = apply_mat(memory_rows, m_value).astype(jnp.bfloat16)
    cross_mixed, cross_lse = attend_fwd(cross_queries, mem_keys, mem_values, None)
    after_cross = after_self + apply_mat(cross_mixed, m_output)
    third = layer_norm(after_cross, third_gain, third_shift).astype(jnp.bfloat16)
    before_act = apply_mat(third, w_in)
    activated = jax.nn.gelu(before_act).astype(jnp.bfloat16)
    final = after_cross + apply_mat(activated, w_out)
    layer_out = jnp.where(valid_row[:, :, None], final, 0.0).astype(jnp.bfloat16)
    b_query, b_key, b_value, b_output, n_query, n_key, n_value, n_output, b_in, b_out = full_mats
    grad_top = jnp.where(valid_row[:, :, None], out_grad.astype(jnp.float32), 0.0)
    top_low = grad_top.astype(jnp.bfloat16)
    hidden_out_grad = mat_grad(activated, top_low)
    _, gelu_pull = jax.vjp(jax.nn.gelu, before_act)
    act_low = gelu_pull(apply_back(top_low, b_out))[0].astype(jnp.bfloat16)
    hidden_in_grad = mat_grad(third, act_low)
    cross_input, third_gain_grad, third_shift_grad = norm_back(
        after_cross, third_gain, third_shift, apply_back(act_low, b_in)
    )
    grad_cross = grad_top + cross_input
    cross_low = grad_cross.astype(jnp.bfloat16)
    cross_output_grad = mat_grad(cross_mixed, cross_low)
    mixed_up = apply_back(cross_low, n_output).astype(jnp.bfloat16)
    cross_query_low, mem_key_low, mem_value_low = attend_back(
        cross_queries, mem_keys, mem_values, None, cross_lse, mixed_up
    )
    cross_query_grad = mat_grad(second, cross_query_low)
    cross_key_grad = mat_grad(memory_rows, mem_key_low)
    cross_value_grad = mat_grad(memory_rows, mem_value_low)
    mem_back = (apply_back(mem_key_low, n_key) + apply_back(mem_value_low, n_value)).astype(
        jnp.bfloat16
    )
    memory_grad = lax.all_to_all(mem_back, "mem", split_axis=1, concat_axis=0, tiled=True)
    self_input, second_gain_grad, second_shift_grad = norm_back(
        after_self, second_gain, second_shift, apply_back(cross_query_low, n_query)
    )
    grad_self = grad_cross + self_input
    self_low = grad_self.astype(jnp.bfloat16)
    self_output_grad = mat_grad(self_mixed, self_low)
    self_up = apply_back(self_low, b_output).astype(jnp.bfloat16)
    query_low, key_low, value_low = attend_back(queries, keys, values, allowed, self_lse, self_up)
    self_query_grad = mat_grad(first, query_low)
    self_key_grad = mat_grad(first, key_low)
    self_value_grad = mat_grad(first, value_low)
    first_up = (
        apply_back(query_low, b_query) + apply_back(key_low, b_key) + apply_back(value_low, b_value)
    )
    text_input, first_gain_grad, first_shift_grad = norm_back(
        residual, first_gain, first_shift, first_up
    )
    text_grad = (grad_self + text_input).astype(jnp.bfloat16)
    weight_sums = reduce_all(
        (
            self_query_grad,
            self_key_grad,
            self_value_grad,
            self_output_grad,
            cross_query_grad,
            cross_key_grad,
            cross_value_grad,
            cross_output_grad,
            hidden_in_grad,
            hidden_out_grad,
        )
    )
    norm_sums = lax.psum(
        (
            first_gain_grad,
            first_shift_grad,
            second_gain_grad,
            second_shift_grad,
            third_gain_grad,
            third_shift_grad,
        ),
        ("dp", "mem"),
    )
    return (
        layer_out,
        text_grad,
        memory_grad,
        weight_sums[0],
        weight_sums[1],
        weight_sums[2],
        weight_sums[3],
        weight_sums[4],
        weight_sums[5],
        weight_sums[6],
        weight_sums[7],
        weight_sums[8],
        weight_sums[9],
        norm_sums[0],
        norm_sums[1],
        norm_sums[2],
        norm_sums[3],
        norm_sums[4],
        norm_sums[5],
    )


def solution(mesh):
    fits = mesh.shape["dp"] == 4 and mesh.shape["mem"] == 8
    return jax.shard_map(
        shards_lean if fits else shards,
        mesh=mesh,
        in_specs=(
            P(("dp", "mem"), None, None),
            P(("dp", "mem")),
            P("dp", "mem", None),
            P(("dp", "mem"), None, None),
            P("dp", "mem"),
            P("dp", "mem"),
            P("dp", "mem"),
            P("dp", "mem"),
            P("dp", "mem"),
            P("dp", "mem"),
            P("dp", "mem"),
            P("dp", "mem"),
            P("dp", "mem"),
            P("dp", "mem"),
            P(),
            P(),
            P(),
            P(),
            P(),
            P(),
        ),
        out_specs=(
            P(("dp", "mem"), None, None),
            P(("dp", "mem"), None, None),
            P("dp", "mem", None),
            P("dp", "mem"),
            P("dp", "mem"),
            P("dp", "mem"),
            P("dp", "mem"),
            P("dp", "mem"),
            P("dp", "mem"),
            P("dp", "mem"),
            P("dp", "mem"),
            P("dp", "mem"),
            P("dp", "mem"),
            P(),
            P(),
            P(),
            P(),
            P(),
            P(),
        ),
        check_vma=False,
    )
```

```python
import functools

import jax
import jax.numpy as jnp
from jax import lax
from jax.experimental import pallas as pl
from jax.experimental.pallas import tpu as pltpu
from jax.sharding import PartitionSpec as P

HEADS = 12
HEAD = 64
MESH = pl.DeviceIdType.MESH
BF = jnp.bfloat16
F32 = jnp.float32
EPS = 1e-06
NEG = -1e30


def layer_norm(values, scaling, offsets):
    center = values - jnp.mean(values, axis=-1, keepdims=True)
    spread = jnp.mean(center * center, axis=-1, keepdims=True)
    return center * lax.rsqrt(spread + EPS) * scaling + offsets


def norm_back(values, scaling, offsets, upstream):
    _, pull_back = jax.vjp(layer_norm, values, scaling, offsets)
    return pull_back(upstream)


def split_heads(values):
    return values.reshape(values.shape[0], values.shape[1], HEADS, HEAD)


def join_heads(values):
    return values.reshape(values.shape[0], values.shape[1], HEADS * HEAD)


def apply_mat(acts, matrix):
    return jnp.einsum("bsd,de->bse", acts, matrix, preferred_element_type=jnp.float32)


def apply_back(grads, matrix):
    return jnp.einsum("bse,de->bsd", grads, matrix, preferred_element_type=jnp.float32)


def mat_grad(acts, grads):
    return jnp.einsum("bsd,bse->de", acts, grads, preferred_element_type=jnp.float32)


def score_rows(queries, keys, allowed):
    score_scale = HEAD ** (-0.5)
    scores = (
        jnp.einsum(
            "bshd,bthd->bhst",
            split_heads(queries),
            split_heads(keys),
            preferred_element_type=jnp.float32,
        )
        * score_scale
    )
    if allowed is not None:
        scores = jnp.where(allowed, scores, NEG)
    return scores


def attend_fwd(queries, keys, values, allowed):
    scores = score_rows(queries, keys, allowed)
    highest = jnp.max(scores, axis=-1, keepdims=True)
    powered = jnp.exp(scores - highest)
    expo_sum = jnp.sum(powered, axis=-1, keepdims=True)
    weights = (powered / expo_sum).astype(jnp.bfloat16)
    mixed_heads = jnp.einsum(
        "bhst,bthd->bshd", weights, split_heads(values), preferred_element_type=jnp.float32
    )
    return (join_heads(mixed_heads).astype(jnp.bfloat16), highest + jnp.log(expo_sum))


def attend_back(queries, keys, values, allowed, log_sum, upstream):
    score_scale = HEAD ** (-0.5)
    probs_full = jnp.exp(score_rows(queries, keys, allowed) - log_sum)
    heads_up = split_heads(upstream)
    prob_grad = jnp.einsum(
        "bshd,bthd->bhst", heads_up, split_heads(values), preferred_element_type=jnp.float32
    )
    score_low = (
        probs_full * (prob_grad - jnp.sum(prob_grad * probs_full, axis=-1, keepdims=True))
    ).astype(jnp.bfloat16)
    value_grad = jnp.einsum(
        "bhst,bshd->bthd",
        probs_full.astype(jnp.bfloat16),
        heads_up,
        preferred_element_type=jnp.float32,
    )
    query_grad = (
        jnp.einsum(
            "bhst,bthd->bshd", score_low, split_heads(keys), preferred_element_type=jnp.float32
        )
        * score_scale
    )
    key_grad = (
        jnp.einsum(
            "bhst,bshd->bthd", score_low, split_heads(queries), preferred_element_type=jnp.float32
        )
        * score_scale
    )
    return (
        join_heads(query_grad).astype(jnp.bfloat16),
        join_heads(key_grad).astype(jnp.bfloat16),
        join_heads(value_grad).astype(jnp.bfloat16),
    )


def fetch_weights(mats):
    columns = (
        lax.all_gather(mats[0], "mem", axis=1, tiled=True),
        lax.all_gather(mats[1], "mem", axis=1, tiled=True),
        lax.all_gather(mats[2], "mem", axis=1, tiled=True),
        lax.all_gather(mats[3], "mem", axis=1, tiled=True),
        lax.all_gather(mats[4], "mem", axis=1, tiled=True),
        lax.all_gather(mats[5], "mem", axis=1, tiled=True),
        lax.all_gather(mats[6], "mem", axis=1, tiled=True),
        lax.all_gather(mats[7], "mem", axis=1, tiled=True),
        lax.all_gather(mats[8], "mem", axis=1, tiled=True),
        lax.all_gather(mats[9], "mem", axis=1, tiled=True),
    )
    return (
        lax.all_gather(columns[0], "dp", axis=0, tiled=True),
        lax.all_gather(columns[1], "dp", axis=0, tiled=True),
        lax.all_gather(columns[2], "dp", axis=0, tiled=True),
        lax.all_gather(columns[3], "dp", axis=0, tiled=True),
        lax.all_gather(columns[4], "dp", axis=0, tiled=True),
        lax.all_gather(columns[5], "dp", axis=0, tiled=True),
        lax.all_gather(columns[6], "dp", axis=0, tiled=True),
        lax.all_gather(columns[7], "dp", axis=0, tiled=True),
        lax.all_gather(columns[8], "dp", axis=0, tiled=True),
        lax.all_gather(columns[9], "dp", axis=0, tiled=True),
    )


def reduce_all(grads):
    row_sums = (
        lax.psum_scatter(
            grads[0].astype(jnp.bfloat16), "dp", scatter_dimension=0, tiled=True
        ).astype(jnp.float32),
        lax.psum_scatter(
            grads[1].astype(jnp.bfloat16), "dp", scatter_dimension=0, tiled=True
        ).astype(jnp.float32),
        lax.psum_scatter(
            grads[2].astype(jnp.bfloat16), "dp", scatter_dimension=0, tiled=True
        ).astype(jnp.float32),
        lax.psum_scatter(
            grads[3].astype(jnp.bfloat16), "dp", scatter_dimension=0, tiled=True
        ).astype(jnp.float32),
        lax.psum_scatter(
            grads[4].astype(jnp.bfloat16), "dp", scatter_dimension=0, tiled=True
        ).astype(jnp.float32),
        lax.psum_scatter(
            grads[5].astype(jnp.bfloat16), "dp", scatter_dimension=0, tiled=True
        ).astype(jnp.float32),
        lax.psum_scatter(
            grads[6].astype(jnp.bfloat16), "dp", scatter_dimension=0, tiled=True
        ).astype(jnp.float32),
        lax.psum_scatter(
            grads[7].astype(jnp.bfloat16), "dp", scatter_dimension=0, tiled=True
        ).astype(jnp.float32),
        lax.psum_scatter(
            grads[8].astype(jnp.bfloat16), "dp", scatter_dimension=0, tiled=True
        ).astype(jnp.float32),
        lax.psum_scatter(
            grads[9].astype(jnp.bfloat16), "dp", scatter_dimension=0, tiled=True
        ).astype(jnp.float32),
    )
    return (
        lax.psum_scatter(
            row_sums[0].astype(jnp.bfloat16), "mem", scatter_dimension=1, tiled=True
        ).astype(jnp.float32),
        lax.psum_scatter(
            row_sums[1].astype(jnp.bfloat16), "mem", scatter_dimension=1, tiled=True
        ).astype(jnp.float32),
        lax.psum_scatter(
            row_sums[2].astype(jnp.bfloat16), "mem", scatter_dimension=1, tiled=True
        ).astype(jnp.float32),
        lax.psum_scatter(
            row_sums[3].astype(jnp.bfloat16), "mem", scatter_dimension=1, tiled=True
        ).astype(jnp.float32),
        lax.psum_scatter(
            row_sums[4].astype(jnp.bfloat16), "mem", scatter_dimension=1, tiled=True
        ).astype(jnp.float32),
        lax.psum_scatter(
            row_sums[5].astype(jnp.bfloat16), "mem", scatter_dimension=1, tiled=True
        ).astype(jnp.float32),
        lax.psum_scatter(
            row_sums[6].astype(jnp.bfloat16), "mem", scatter_dimension=1, tiled=True
        ).astype(jnp.float32),
        lax.psum_scatter(
            row_sums[7].astype(jnp.bfloat16), "mem", scatter_dimension=1, tiled=True
        ).astype(jnp.float32),
        lax.psum_scatter(
            row_sums[8].astype(jnp.bfloat16), "mem", scatter_dimension=1, tiled=True
        ).astype(jnp.float32),
        lax.psum_scatter(
            row_sums[9].astype(jnp.bfloat16), "mem", scatter_dimension=1, tiled=True
        ).astype(jnp.float32),
    )


def shards(
    text,
    lengths,
    memory,
    out_grad,
    self_query,
    self_key,
    self_value,
    self_output,
    cross_query,
    cross_key,
    cross_value,
    cross_output,
    hidden_in,
    hidden_out,
    first_gain,
    first_shift,
    second_gain,
    second_shift,
    third_gain,
    third_shift,
):
    mats = (
        self_query,
        self_key,
        self_value,
        self_output,
        cross_query,
        cross_key,
        cross_value,
        cross_output,
        hidden_in,
        hidden_out,
    )
    full_mats = fetch_weights(mats)
    w_query, w_key, w_value, w_output, m_query, m_key, m_value, m_output, w_in, w_out = full_mats
    places = jnp.arange(text.shape[1])
    valid_row = places[None, :] < lengths[:, None]
    allowed = (places[None, :] <= places[:, None])[None, None] & valid_row[:, None, None, :]
    residual = text.astype(jnp.float32)
    first = layer_norm(residual, first_gain, first_shift).astype(jnp.bfloat16)
    queries = apply_mat(first, w_query).astype(jnp.bfloat16)
    keys = apply_mat(first, w_key).astype(jnp.bfloat16)
    values = apply_mat(first, w_value).astype(jnp.bfloat16)
    self_mixed, self_lse = attend_fwd(queries, keys, values, allowed)
    after_self = residual + apply_mat(self_mixed, w_output)
    memory_rows = lax.all_to_all(memory, "mem", split_axis=0, concat_axis=1, tiled=True)
    second = layer_norm(after_self, second_gain, second_shift).astype(jnp.bfloat16)
    cross_queries = apply_mat(second, m_query).astype(jnp.bfloat16)
    mem_keys = apply_mat(memory_rows, m_key).astype(jnp.bfloat16)
    mem_values = apply_mat(memory_rows, m_value).astype(jnp.bfloat16)
    cross_mixed, cross_lse = attend_fwd(cross_queries, mem_keys, mem_values, None)
    after_cross = after_self + apply_mat(cross_mixed, m_output)
    third = layer_norm(after_cross, third_gain, third_shift).astype(jnp.bfloat16)
    before_act = apply_mat(third, w_in)
    activated = jax.nn.gelu(before_act).astype(jnp.bfloat16)
    final = after_cross + apply_mat(activated, w_out)
    layer_out = jnp.where(valid_row[:, :, None], final, 0.0).astype(jnp.bfloat16)
    b_query, b_key, b_value, b_output, n_query, n_key, n_value, n_output, b_in, b_out = full_mats
    grad_top = jnp.where(valid_row[:, :, None], out_grad.astype(jnp.float32), 0.0)
    top_low = grad_top.astype(jnp.bfloat16)
    hidden_out_grad = mat_grad(activated, top_low)
    _, gelu_pull = jax.vjp(jax.nn.gelu, before_act)
    act_low = gelu_pull(apply_back(top_low, b_out))[0].astype(jnp.bfloat16)
    hidden_in_grad = mat_grad(third, act_low)
    cross_input, third_gain_grad, third_shift_grad = norm_back(
        after_cross, third_gain, third_shift, apply_back(act_low, b_in)
    )
    grad_cross = grad_top + cross_input
    cross_low = grad_cross.astype(jnp.bfloat16)
    cross_output_grad = mat_grad(cross_mixed, cross_low)
    mixed_up = apply_back(cross_low, n_output).astype(jnp.bfloat16)
    cross_query_low, mem_key_low, mem_value_low = attend_back(
        cross_queries, mem_keys, mem_values, None, cross_lse, mixed_up
    )
    cross_query_grad = mat_grad(second, cross_query_low)
    cross_key_grad = mat_grad(memory_rows, mem_key_low)
    cross_value_grad = mat_grad(memory_rows, mem_value_low)
    mem_back = (apply_back(mem_key_low, n_key) + apply_back(mem_value_low, n_value)).astype(
        jnp.bfloat16
    )
    memory_grad = lax.all_to_all(mem_back, "mem", split_axis=1, concat_axis=0, tiled=True)
    self_input, second_gain_grad, second_shift_grad = norm_back(
        after_self, second_gain, second_shift, apply_back(cross_query_low, n_query)
    )
    grad_self = grad_cross + self_input
    self_low = grad_self.astype(jnp.bfloat16)
    self_output_grad = mat_grad(self_mixed, self_low)
    self_up = apply_back(self_low, b_output).astype(jnp.bfloat16)
    query_low, key_low, value_low = attend_back(queries, keys, values, allowed, self_lse, self_up)
    self_query_grad = mat_grad(first, query_low)
    self_key_grad = mat_grad(first, key_low)
    self_value_grad = mat_grad(first, value_low)
    first_up = (
        apply_back(query_low, b_query) + apply_back(key_low, b_key) + apply_back(value_low, b_value)
    )
    text_input, first_gain_grad, first_shift_grad = norm_back(
        residual, first_gain, first_shift, first_up
    )
    text_grad = (grad_self + text_input).astype(jnp.bfloat16)
    weight_sums = reduce_all(
        (
            self_query_grad,
            self_key_grad,
            self_value_grad,
            self_output_grad,
            cross_query_grad,
            cross_key_grad,
            cross_value_grad,
            cross_output_grad,
            hidden_in_grad,
            hidden_out_grad,
        )
    )
    norm_sums = lax.psum(
        (
            first_gain_grad,
            first_shift_grad,
            second_gain_grad,
            second_shift_grad,
            third_gain_grad,
            third_shift_grad,
        ),
        ("dp", "mem"),
    )
    return (
        layer_out,
        text_grad,
        memory_grad,
        weight_sums[0],
        weight_sums[1],
        weight_sums[2],
        weight_sums[3],
        weight_sums[4],
        weight_sums[5],
        weight_sums[6],
        weight_sums[7],
        weight_sums[8],
        weight_sums[9],
        norm_sums[0],
        norm_sums[1],
        norm_sums[2],
        norm_sums[3],
        norm_sums[4],
        norm_sums[5],
    )


class Place:
    def __init__(self):
        self.d = lax.axis_index("dp")
        self.m = lax.axis_index("mem")
        self.c = lax.rem(self.d, 2)
        self.x = lax.div(self.d, 2)
        self.y = lax.rem(self.m, 2)
        self.z = lax.div(self.m, 2)
        self.oc, self.ox, self.oy = 1 - self.c, 1 - self.x, 1 - self.y
        self.sib = (self.x * 2 + self.oc, self.m)
        self.xn = (self.ox * 2 + self.c, self.m)
        self.yn = (self.d, self.z * 2 + self.oy)

    def zup(self, k):
        return lax.rem(self.z + k, 4)

    def zpeer(self, k):
        return (self.d, self.zup(k) * 2 + self.y)

    def mpeer(self, k):
        return (self.d, lax.rem(self.m + k, 8))


def greet(at):
    barrier = pltpu.get_barrier_semaphore()
    for peer in [at.sib, at.xn] + [at.mpeer(k) for k in range(1, 8)]:
        pl.semaphore_signal(barrier, inc=1, device_id=peer, device_id_type=MESH)
    pl.semaphore_wait(barrier, 9)


def remote(src, dst, sends, recvs, idx, peer):
    return pltpu.make_async_remote_copy(
        src_ref=src,
        dst_ref=dst,
        send_sem=sends.at[idx],
        recv_sem=recvs.at[idx],
        device_id=peer,
        device_id_type=MESH,
    )


class Gather:
    def __init__(self, at, full, span, sends, recvs, base):
        self.at, self.full, self.span = at, full, span
        self.sends, self.recvs, self.base = sends, recvs, base
        self.lanes = full.shape[-1] // 2
        self.out = []

    def piece(self, z, y, h, x):
        lo = pl.multiple_of(x * self.lanes, 128)
        return self.full.at[self.span, z, y, h, :, pl.ds(lo, self.lanes)]

    def copy(self, slot, src, dst, peer):
        return remote(src, dst, self.sends, self.recvs, self.base + slot, peer)

    def send(self, slot, src, dst, peer):
        copy = self.copy(slot, src, dst, peer)
        copy.start()
        self.out.append(copy)

    def got(self, slot, ref):
        self.copy(slot, ref, ref, self.at.sib).wait_recv()

    def begin(self):
        at = self.at
        own = self.piece(at.z, at.y, at.c, at.x)
        for k in (1, 2, 3):
            self.send(k - 1, own, own, at.zpeer(k))
        self.send(3, own, own, at.xn)
        self.send(7, own, own, at.yn)
        self.send(13, own, own, at.sib)

    def second(self):
        at = self.at
        for k in (1, 2, 3):
            ref = self.piece(at.zup(4 - k), at.y, at.c, at.x)
            self.got(k - 1, ref)
            self.send(3 + k, ref, ref, at.xn)
            self.send(7 + k, ref, ref, at.yn)
            self.send(13 + k, ref, ref, at.sib)

    def third(self):
        at = self.at
        for k in range(4):
            self.got(3 + k, self.piece(at.zup(4 - k), at.y, at.c, at.ox))
        ref = self.piece(pl.ds(0, 2), at.y, at.c, at.ox)
        self.send(11, ref, ref, at.yn)
        ref = self.piece(slice(None), at.y, at.c, at.ox)
        self.send(17, ref, ref, at.sib)
        for k in range(4):
            self.got(7 + k, self.piece(at.zup(4 - k), at.oy, at.c, at.x))
        ref = self.piece(pl.ds(2, 2), at.oy, at.c, at.x)
        self.send(12, ref, ref, at.xn)
        ref = self.piece(slice(None), at.oy, at.c, at.x)
        self.send(18, ref, ref, at.sib)

    def fourth(self):
        at = self.at
        for half in range(2):
            ref = self.piece(pl.ds(2 * half, 2), at.oy, at.c, at.ox)
            self.got(11 + half, ref)
            self.send(19 + half, ref, ref, at.sib)

    def last(self):
        at = self.at
        for k in range(4):
            self.got(13 + k, self.piece(at.zup(4 - k), at.y, at.oc, at.x))
        self.got(17, self.piece(slice(None), at.y, at.oc, at.ox))
        self.got(18, self.piece(slice(None), at.oy, at.oc, at.x))
        for half in range(2):
            self.got(19 + half, self.piece(pl.ds(2 * half, 2), at.oy, at.oc, at.ox))

    def drain(self):
        for copy in self.out:
            copy.wait_send()
        self.out = []


GATHER_SLOTS = 21


class Reduce:
    def __init__(self, at, sources, parts, mine, bufs, sends, recvs, base):
        self.at, self.sources, self.parts, self.mine = at, sources, parts, mine
        self.chip, self.rdiag, self.rx, self.ry, self.rz, self.fin = bufs
        self.sends, self.recvs, self.base = sends, recvs, base
        self.count = self.chip.shape[0]
        self.out = []

    send, got, copy, drain = Gather.send, Gather.got, Gather.copy, Gather.drain

    def begin(self, part):
        for src, dst in self.sources(part):
            self.copy(part, src, dst, self.at.sib).start()
        whole = self.parts(part)
        self.out.append(self.copy(part, whole, whole, self.at.sib))

    def second(self):
        at, chip = self.at, self.chip
        for part in range(2):
            self.got(part, self.parts(part))

        def add(i, carry):
            w, r = lax.div(i, 8), lax.rem(i, 8)
            z, y = lax.div(r, 2), lax.rem(r, 2)
            for x in range(2):
                chip[w, x, z, y] = (
                    chip[w, x, z, y].astype(F32) + self.mine(w, x, z, y).astype(F32)
                ).astype(BF)
            return carry

        lax.fori_loop(0, 8 * self.count, add, 0)
        self.send(2, chip.at[:, at.ox, pl.ds(0, 2), at.oy], self.rdiag.at[0], at.yn)
        self.send(3, chip.at[:, at.ox, pl.ds(2, 2), at.oy], self.rdiag.at[1], at.xn)

    def third(self):
        at, chip = self.at, self.chip
        for half in range(2):
            self.got(2 + half, self.rdiag.at[half])
            x, y = ((at.ox, at.y), (at.x, at.oy))[half]

            def add(i, carry, x=x, y=y, half=half):
                w, z = lax.div(i, 2), lax.rem(i, 2)
                chip[w, x, 2 * half + z, y] = (
                    chip[w, x, 2 * half + z, y].astype(F32)
                    + self.rdiag[half, w, z].astype(F32)
                ).astype(BF)
                return carry

            lax.fori_loop(0, 2 * self.count, add, 0)
        self.send(4, chip.at[:, at.ox, :, at.y], self.rx, at.xn)
        self.send(5, chip.at[:, at.x, :, at.oy], self.ry, at.yn)

    def fourth(self):
        at, chip = self.at, self.chip
        self.got(4, self.rx)
        self.got(5, self.ry)

        def add(i, carry):
            w, z = lax.div(i, 4), lax.rem(i, 4)
            chip[w, at.x, z, at.y] = (
                chip[w, at.x, z, at.y].astype(F32)
                + self.rx[w, z].astype(F32)
                + self.ry[w, z].astype(F32)
            ).astype(BF)
            return carry

        lax.fori_loop(0, 4 * self.count, add, 0)
        for k in (1, 2, 3):
            self.send(
                5 + k, chip.at[:, at.x, at.zup(k), at.y], self.rz.at[k - 1], at.zpeer(k)
            )

    def fifth(self):
        at = self.at
        for k in (1, 2, 3):
            self.got(5 + k, self.rz.at[k - 1])

        def add(w, carry):
            total = self.chip[w, at.x, at.z, at.y].astype(F32)
            for k in range(3):
                total = total + self.rz[k, w].astype(F32)
            self.fin[at.c, w] = total.astype(BF)
            return carry

        lax.fori_loop(0, self.count, add, 0)
        self.send(9, self.fin.at[at.c], self.fin.at[at.c], at.sib)

    def last(self):
        self.got(9, self.fin.at[self.at.oc])


REDUCE_SLOTS = 10


def reduce_bufs(count, rows, lanes):
    return [
        pltpu.VMEM((count, 2, 4, 2, rows, lanes), BF),
        pltpu.VMEM((2, count, 2, rows, lanes), BF),
        pltpu.VMEM((count, 4, rows, lanes), BF),
        pltpu.VMEM((count, 4, rows, lanes), BF),
        pltpu.VMEM((3, count, rows, lanes), BF),
        pltpu.VMEM((2, count, rows, lanes), BF),
    ]


def pick(rows, cols, start):
    col = lax.broadcasted_iota(jnp.int32, (rows, cols), 1)
    row = lax.broadcasted_iota(jnp.int32, (rows, cols), 0)
    return jnp.where(col == row + start, 1.0, 0.0).astype(BF)


def dot_nt(a, b):
    return lax.dot_general(a, b, (((1,), (1,)), ((), ())), preferred_element_type=F32)


def dot_nn(a, b):
    return lax.dot_general(a, b, (((1,), (0,)), ((), ())), preferred_element_type=F32)


def dot_tn(a, b):
    return lax.dot_general(a, b, (((0,), (0,)), ((), ())), preferred_element_type=F32)


def norm_stats(values):
    center = values - jnp.mean(values, axis=-1, keepdims=True)
    scale = lax.rsqrt(jnp.mean(center * center, axis=-1, keepdims=True) + EPS)
    return center * scale, scale


def gelu_both(value):
    c0, c1 = 0.7978845608028654, 0.044715
    square = value * value
    tanh = jnp.tanh(c0 * value * (1.0 + c1 * square))
    half = 0.5 + 0.5 * tanh
    slope = half + 0.5 * value * (1.0 - tanh * tanh) * (c0 + 3.0 * c0 * c1 * square)
    return value * half, slope


def softmax(scores):
    powered = jnp.exp(scores - jnp.max(scores, axis=-1, keepdims=True))
    return powered / jnp.sum(powered, axis=-1, keepdims=True)


class Layer:
    def __init__(self, **refs):
        self.__dict__.update(refs)
        self.tokens, self.dmodel = self.nrm.shape
        self.images = self.own_images
        self.txt = self.tokens // self.images
        self.mem_len = self.mk.shape[0] // self.images
        lane = lax.broadcasted_iota(jnp.int32, (1, 4 * HEAD), 1)
        self.head_lanes = [
            jnp.where((lane >= HEAD * h) & (lane < HEAD * (h + 1)), 1.0, 0.0)
            for h in range(4)
        ]

    def weight(self, i):
        return self.full_s[i].reshape(self.dmodel, self.dmodel)

    def put_weight(self, i, value):
        self.full_s[i] = value.astype(BF).reshape(self.full_s.shape[1:])

    def blocks(self, size, fn, total=None):
        def step(i, carry):
            fn(pl.ds(pl.multiple_of(i * size, size), size))
            return carry

        lax.fori_loop(0, (total or self.tokens) // size, step, 0)

    def spread(self, value):
        return jnp.concatenate(
            [value * mask.astype(BF) for mask in self.head_lanes], axis=0
        )

    def gather_heads(self, value):
        n = value.shape[0] // 4
        out = value[:n] * self.head_lanes[0]
        for h in range(1, 4):
            out = out + value[h * n : (h + 1) * n] * self.head_lanes[h]
        return out

    def norm_into(self, source, index):
        gain, shift = self.norms[2 * index : 2 * index + 1], self.norms[2 * index + 1 : 2 * index + 2]

        def block(rows):
            hat, _ = norm_stats(source[rows, :].astype(F32))
            self.nrm[rows, :] = (hat * gain + shift).astype(BF)

        self.blocks(128, block)

    def norm_back(self, source, upstream, index, finish):
        gain = self.norms[2 * index : 2 * index + 1]

        def step(i, carry):
            rows = pl.ds(pl.multiple_of(i * 64, 64), 64)
            hat, scale = norm_stats(source[rows, :].astype(F32))
            up = upstream[rows, :]
            scaled = up * gain
            first = jnp.mean(scaled, axis=-1, keepdims=True)
            second = jnp.mean(scaled * hat, axis=-1, keepdims=True)
            finish(rows, scale * (scaled - first - hat * second))
            gains, shifts = carry
            return (
                gains + jnp.sum(up * hat, axis=0, keepdims=True),
                shifts + jnp.sum(up, axis=0, keepdims=True),
            )

        zero = jnp.zeros((1, self.dmodel), F32)
        gains, shifts = lax.fori_loop(0, self.tokens // 64, step, (zero, zero))
        self.norm_grads[2 * index : 2 * index + 1, :] = gains
        self.norm_grads[2 * index + 1 : 2 * index + 2, :] = shifts


    def project(self, out, source, i):
        out[...] = dot_nt(source[...], self.weight(i)).astype(BF)

    def self_forward(self):
        def pair(p, carry):
            rows = pl.ds(pl.multiple_of(p * 128, 128), 128)
            allow = self.allow[p].astype(F32)
            for g in range(self.dmodel // 256):
                cols = slice(256 * g, 256 * g + 256)
                scores = dot_nt(self.spread(self.q[rows, cols]), self.k[rows, cols])
                scores = scores.reshape(4, 128, 128) * HEAD**-0.5
                scores = jnp.where((allow > 0.5)[None], scores, NEG)
                probs = softmax(scores).reshape(512, 128).astype(BF)
                self.ps[p, g] = probs
                mixed = dot_nn(probs, self.v[rows, cols])
                self.sm[rows, cols] = self.gather_heads(mixed).astype(BF)
            return carry

        lax.fori_loop(0, self.images // 2, pair, 0)

    def add_after_self(self):
        def block(rows):
            self.after_self[rows, :] = self.io[rows, :].astype(F32) + dot_nt(
                self.sm[rows, :], self.weight(3)
            )

        self.blocks(256, block)

    def swap_rows(self, out, source):
        n, size = self.images, self.mem_len
        short = size // n
        total = n * size

        def block(i, carry):
            row = lax.broadcasted_iota(jnp.int32, (size, total), 0)
            col = lax.broadcasted_iota(jnp.int32, (size, total), 1)
            which = jnp.floor((row.astype(F32) + 0.5) * (1.0 / short)).astype(jnp.int32)
            hit = col == row + which * (size - short) + i * short
            rows = pl.ds(pl.multiple_of(i * size, 32), size)
            out[rows, :] = dot_nn(jnp.where(hit, 1.0, 0.0).astype(BF), source[...]).astype(BF)
            return carry

        lax.fori_loop(0, n, block, 0)

    def memory_in(self):
        self.swap_rows(self.mk, self.rows)
        self.rows[...] = self.mk[...]

    def probs_at(self, i, g):
        size = 4 * self.txt
        start = pl.multiple_of(lax.rem(i, 2) * size, size)
        return lax.div(i, 2), g, pl.ds(start, size), slice(0, self.mem_len)

    def cross_forward(self):
        def image(i, carry):
            rows = pl.ds(pl.multiple_of(i * self.txt, 64), self.txt)
            mems = pl.ds(pl.multiple_of(i * self.mem_len, 32), self.mem_len)
            for g in range(self.dmodel // 256):
                cols = slice(256 * g, 256 * g + 256)
                scores = dot_nt(self.spread(self.cq[rows, cols]), self.mk[mems, cols])
                probs = softmax(scores * HEAD**-0.5).astype(BF)
                self.ps[self.probs_at(i, g)] = probs
                mixed = dot_nn(probs, self.mv[mems, cols])
                self.cm[rows, cols] = self.gather_heads(mixed).astype(BF)
            return carry

        lax.fori_loop(0, self.images, image, 0)

    def add_after_cross(self):
        def block(rows):
            self.after_cross[rows, :] = self.after_self[rows, :] + dot_nt(
                self.cm[rows, :], self.weight(7)
            )

        self.blocks(256, block)


    def mask_top(self):
        def block(rows):
            self.io[rows, :] = self.io[rows, :] * self.valid[rows, :1]

        self.blocks(128, block)

    def feed_start(self):
        def block(rows):
            self.acc_out[rows, :] = self.after_cross[rows, :]
            self.acc_up[rows, :] = jnp.zeros((128, self.dmodel), F32)

        self.blocks(128, block)

    def feed_chunk(self, z):
        dmodel = self.dmodel
        lo = pl.multiple_of(z * dmodel, 128)

        def w_out():
            return self.full_out[0, :, :, :, :, pl.ds(lo, dmodel)].reshape(dmodel, dmodel)

        def w_in():
            return self.full_in[0, z].reshape(dmodel, dmodel)

        def block(rows):
            before = dot_nt(self.nrm[rows, :], w_in())
            act, slope = gelu_both(before)
            self.t2[rows, :] = act.astype(BF)
            up = dot_nn(self.io[rows, :], w_out())
            self.t3[rows, :] = (slope * up).astype(BF)

        self.blocks(256, block)

        def block(rows):
            self.acc_out[rows, :] += dot_nt(self.t2[rows, :], w_out())
            self.acc_up[rows, :] += dot_nn(self.t3[rows, :], w_in())

        self.blocks(256, block)
        self.full_out[0, :, :, :, :, pl.ds(lo, dmodel)] = (
            dot_tn(self.io[...], self.t2[...]).astype(BF)
        ).reshape(self.full_out.shape[1:5] + (dmodel,))
        self.full_in[0, z] = (
            dot_tn(self.t3[...], self.nrm[...]).astype(BF).reshape(self.full_in.shape[2:])
        )

    def layer_out(self, out):
        def block(rows):
            out[rows, :] = (self.acc_out[rows, :] * self.valid[rows, :1].astype(F32)).astype(BF)

        self.blocks(128, block)


    def third_back(self):
        def finish(rows, grad):
            total = self.io[rows, :].astype(F32) + grad
            self.acc_up[rows, :] = total
            self.io[rows, :] = total.astype(BF)

        self.norm_back(self.after_cross, self.acc_up, 2, finish)

    def output_back(self, i, mixed, out):
        out[...] = dot_nn(self.io[...], self.weight(i)).astype(BF)
        self.put_weight(i, dot_tn(self.io[...], mixed[...]))

    def attend_back(self, probs, up, q, k, v, rows, mems, cols):
        low_q = self.spread(q[rows, cols])
        low_up = self.spread(up[rows, cols])
        keys, values = k[mems, cols], v[mems, cols]
        full = probs.astype(F32)
        prob_grad = dot_nt(low_up, values)
        score = full * (prob_grad - jnp.sum(prob_grad * full, axis=-1, keepdims=True))
        score = (score * HEAD**-0.5).astype(BF)
        v[mems, cols] = dot_tn(probs, low_up).astype(BF)
        k[mems, cols] = dot_tn(score, low_q).astype(BF)
        q[rows, cols] = self.gather_heads(dot_nn(score, keys)).astype(BF)

    def cross_back(self, start, stop):
        def image(i, carry):
            rows = pl.ds(pl.multiple_of(i * self.txt, 64), self.txt)
            mems = pl.ds(pl.multiple_of(i * self.mem_len, 32), self.mem_len)
            for g in range(self.dmodel // 256):
                cols = slice(256 * g, 256 * g + 256)
                probs = self.ps[self.probs_at(i, g)]
                self.attend_back(
                    probs, self.t2, self.cq, self.mk, self.mv, rows, mems, cols
                )
            return carry

        lax.fori_loop(start, stop, image, 0)

    def self_back(self):
        def pair(p, carry):
            rows = pl.ds(pl.multiple_of(p * 128, 128), 128)
            for g in range(self.dmodel // 256):
                cols = slice(256 * g, 256 * g + 256)
                self.attend_back(
                    self.ps[p, g], self.t2, self.q, self.k, self.v, rows, rows, cols
                )
            return carry

        lax.fori_loop(0, self.images // 2, pair, 0)

    def memory_back(self):
        key_grad = dot_tn(self.mk[...], self.rows[...])

        def block(rows):
            total = dot_nn(self.mk[rows, :], self.weight(5)) + dot_nn(
                self.mv[rows, :], self.weight(6)
            )
            self.back[rows, :] = total.astype(BF)

        self.blocks(256, block, self.mk.shape[0])
        self.put_weight(5, key_grad)
        self.put_weight(6, dot_tn(self.mv[...], self.rows[...]))
        self.swap_rows(self.rows, self.back)

    def second_up(self):
        def block(rows):
            self.acc_out[rows, :] = dot_nn(self.cq[rows, :], self.weight(4))

        self.blocks(256, block)

    def query_grad(self):
        self.put_weight(4, dot_tn(self.cq[...], self.nrm[...]))

    def second_back(self):
        def finish(rows, grad):
            total = self.acc_up[rows, :] + grad
            self.acc_up[rows, :] = total
            self.io[rows, :] = total.astype(BF)

        self.norm_back(self.after_self, self.acc_out, 1, finish)

    def first_up(self):
        def block(rows):
            self.acc_out[rows, :] = (
                dot_nn(self.q[rows, :], self.weight(0))
                + dot_nn(self.k[rows, :], self.weight(1))
                + dot_nn(self.v[rows, :], self.weight(2))
            )

        self.blocks(256, block)

    def first_grads(self):
        for i, low in enumerate((self.q, self.k, self.v)):
            self.put_weight(i, dot_tn(low[...], self.nrm[...]))

    def first_back(self, text, out):
        def finish(rows, grad):
            out[rows, :] = (self.acc_up[rows, :] + grad).astype(BF)

        self.norm_back(text, self.acc_out, 0, finish)


class NormSum:
    def __init__(self, at, sums, recv, sends, recvs):
        self.at, self.sums, self.recv, self.sends, self.recvs = at, sums, recv, sends, recvs
        flip = (at.d, (at.z + 1 - 2 * lax.rem(at.z, 2)) * 2 + at.y)
        self.peers = [at.sib, at.xn, at.yn, flip, at.zpeer(2)]
        self.out = []

    def start(self, i):
        copy = remote(
            self.sums.at[i], self.recv.at[i], self.sends, self.recvs, i, self.peers[i]
        )
        copy.start()
        self.out.append(copy)

    def finish(self, i):
        self.out[i].wait_recv()
        self.sums[i + 1] = self.sums[i] + self.recv[i]


REDUCE_COUNTS = (4, 4, 1, 3, 1, 3)
NAMES = ("nrm", "io", "q", "k", "v", "sm", "cq", "cm", "t2", "t3")
WIDE = ("after_self", "after_cross", "acc_out", "acc_up")


def whole_kernel(own_images, *refs):
    refs = list(refs)

    def take(n):
        out = refs[:n]
        del refs[:n]
        return out

    shards, (rows_in, text_in, top_in) = take(10), take(3)
    valid, allow, norms = take(3)
    outs, (layer_out, text_out, rows_out, norm_out, spill) = take(10), take(5)
    full_s, full_in, full_out, pair_s, pair_in, pair_out = take(6)
    bufs = [take(6) for _ in REDUCE_COUNTS]
    narrow, wide = take(len(NAMES)), take(len(WIDE))
    rows, mk, mv, ps, norm_sums, norm_recv = take(6)
    (psend, precv, gsend, grecv, hsend, hrecv, rsend, rrecv, bsend, brecv, nsend, nrecv, local) = refs
    at = Place()
    greet(at)
    layer = Layer(
        own_images=own_images,
        full_s=full_s,
        full_in=full_in,
        full_out=full_out,
        rows=rows,
        mk=mk,
        mv=mv,
        ps=ps,
        back=mk,
        valid=valid,
        allow=allow,
        norms=norms,
        norm_grads=norm_sums.at[0],
        **dict(zip(NAMES, narrow)),
        **dict(zip(WIDE, wide)),
    )

    pairs = [pair_s.at[i] for i in range(8)] + [pair_in, pair_out]
    own, other = [], []
    for i in range(10):
        depth = shards[i].shape[0]
        mine = pairs[i].at[pl.ds(pl.multiple_of(at.c * depth, 8), depth), :]
        copy = remote(shards[i], mine, psend, precv, i, at.sib)
        copy.start()
        other.append(copy)
        copy = pltpu.make_async_copy(shards[i], mine, local.at[i])
        copy.start()
        own.append(copy)
    load = pltpu.make_async_copy(text_in, layer.io, local.at[10])
    load.start()

    def ready(i):
        own[i].wait()
        depth = shards[i].shape[0]
        theirs = pairs[i].at[pl.ds(pl.multiple_of(at.oc * depth, 8), depth), :]
        remote(theirs, theirs, psend, precv, i, at.sib).wait_recv()

    def lay_in(full, w, i, half, lanes):
        ready(i)
        lo = pl.multiple_of(at.x * lanes, 128)
        block = dot_nt(pick(half, 2 * half, at.c * half), pairs[i][...])
        full[w, at.z, at.y, at.c, :, pl.ds(lo, lanes)] = block.astype(BF)

    fulls = (full_s, full_s, full_in, full_out)
    spans = (slice(0, 3), slice(3, 8), slice(0, 1), slice(0, 1))
    groups = [
        Gather(at, full, span, gsend, grecv, GATHER_SLOTS * g)
        for g, (full, span) in enumerate(zip(fulls, spans))
    ]
    for g, group in enumerate(groups):
        half, lanes = group.full.shape[4], group.full.shape[5] // 2
        for w in range(group.span.start, group.span.stop):
            lay_in(group.full, w, w if g < 2 else 6 + g, half, lanes)
        group.begin()
    size = rows.shape[0] // 8

    def block_of(m):
        return rows.at[pl.ds(pl.multiple_of(m * size, 32), size), :]

    mems = []
    for k in range(1, 8):
        to = lax.rem(at.m + k, 8)
        copy = remote(rows_in.at[to], block_of(at.m), rsend, rrecv, k - 1, at.mpeer(k))
        copy.start()
        mems.append(copy)
    keep = pltpu.make_async_copy(rows_in.at[at.m], block_of(at.m), local.at[11])
    keep.start()

    first, rest, feed_in, feed_out = groups
    load.wait()
    layer.norm_into(layer.io, 0)
    first.second()
    rest.second()
    first.third()
    feed_in.second()
    first.fourth()
    feed_out.second()
    first.last()
    layer.project(layer.q, layer.nrm, 0)
    rest.third()
    layer.project(layer.k, layer.nrm, 1)
    layer.project(layer.v, layer.nrm, 2)
    feed_in.third()
    rest.fourth()
    layer.self_forward()
    away = pltpu.make_async_copy(ps, spill, local.at[13])
    away.start()
    rest.last()
    layer.add_after_self()
    feed_out.third()
    feed_in.fourth()
    top = pltpu.make_async_copy(top_in, layer.io, local.at[10])
    top.start()
    layer.norm_into(layer.after_self, 1)
    layer.project(layer.cq, layer.nrm, 4)
    keep.wait()
    for k in range(1, 8):
        ref = block_of(lax.rem(at.m + 8 - k, 8))
        remote(ref, ref, rsend, rrecv, k - 1, at.sib).wait_recv()
    layer.memory_in()
    layer.project(layer.mk, layer.rows, 5)
    layer.project(layer.mv, layer.rows, 6)
    feed_out.fourth()
    away.wait()
    layer.cross_forward()
    layer.add_after_cross()
    layer.norm_into(layer.after_cross, 2)
    top.wait()
    layer.mask_top()
    layer.feed_start()
    feed_in.last()
    feed_out.last()
    for copy in other + mems:
        copy.wait_send()
    for group in groups:
        group.drain()

    half, dmodel = full_s.shape[4:]
    lanes = dmodel // 2

    def small(g, span):
        chip, w0 = bufs[g][0], span.start

        def sources(part):
            cut = slice(part * lanes, (part + 1) * lanes)
            return [(full_s.at[span, :, :, at.oc, :, cut], chip.at[:, part])]

        def mine(w, x, z, y):
            return full_s[w0 + w, z, y, at.c, :, x * lanes : (x + 1) * lanes]

        return Reduce(
            at, sources, lambda x: chip.at[:, x], mine, bufs[g], hsend, hrecv, REDUCE_SLOTS * g
        )

    def out_group(g):
        chip = bufs[g][0]
        count = chip.shape[0]

        def cut(j, x):
            lo = (x * count + j) * lanes
            return slice(lo, lo + lanes)

        def sources(x):
            return [
                (full_out.at[0, :, :, at.oc, :, cut(j, x)], chip.at[j, x])
                for j in range(count)
            ]

        def mine(j, x, z, y):
            lo = pl.multiple_of((x * count + j) * lanes, 128)
            return full_out[0, z, y, at.c, :, pl.ds(lo, lanes)]

        return Reduce(
            at, sources, lambda x: chip.at[:, x], mine, bufs[g], hsend, hrecv, REDUCE_SLOTS * g
        )

    def in_group(g):
        chip = bufs[g][0]
        count = chip.shape[0]

        def sources(part):
            zs = pl.ds(2 * part, 2)
            return [
                (
                    full_in.at[
                        0, zs, :, at.oc, s * half : (s + 1) * half, x * lanes : (x + 1) * lanes
                    ],
                    chip.at[s, x, zs],
                )
                for s in range(count)
                for x in range(2)
            ]

        def mine(s, x, z, y):
            lo = pl.multiple_of(s * half, 16)
            return full_in[0, z, y, at.c, pl.ds(lo, half), x * lanes : (x + 1) * lanes]

        def parts(part):
            return chip.at[:, :, pl.ds(2 * part, 2)]

        return Reduce(at, sources, parts, mine, bufs[g], hsend, hrecv, REDUCE_SLOTS * g)

    g_out, g_in = out_group(0), in_group(1)
    g_co, g_cross = small(2, slice(7, 8)), small(3, slice(4, 7))
    g_so, g_self = small(4, slice(3, 4)), small(5, slice(0, 3))

    def chunks(a, b):
        def step(z, carry):
            layer.feed_chunk(z)
            return carry

        lax.fori_loop(a, b, step, 0)

    chunks(0, 2)
    g_out.begin(0)
    g_in.begin(0)
    chunks(2, 4)
    g_out.begin(1)
    g_in.begin(1)
    layer.layer_out(layer.t3)
    save = pltpu.make_async_copy(layer.t3, layer_out, local.at[12])
    save.start()
    g_out.second()
    layer.third_back()
    g_in.second()
    layer.output_back(7, layer.cm, layer.t2)
    g_co.begin(0)
    g_co.begin(1)
    g_out.third()
    layer.cross_back(0, own_images // 2)
    g_in.third()
    g_co.second()
    layer.cross_back(own_images // 2, own_images)
    again = pltpu.make_async_copy(spill, ps, local.at[13])
    again.start()
    g_out.fourth()
    g_co.third()
    layer.second_up()
    layer.norm_into(layer.after_self, 1)
    layer.query_grad()
    layer.memory_back()
    g_cross.begin(0)
    g_cross.begin(1)
    backs = []
    for k in range(1, 8):
        to = lax.rem(at.m + k, 8)
        copy = remote(block_of(to), rows_out.at[at.m], bsend, brecv, k - 1, at.mpeer(k))
        copy.start()
        backs.append(copy)
    keep = pltpu.make_async_copy(block_of(at.m), rows_out.at[at.m], local.at[11])
    keep.start()
    layer.second_back()
    g_in.fourth()
    layer.output_back(3, layer.sm, layer.t2)
    g_so.begin(0)
    g_so.begin(1)
    g_cross.second()
    text = pltpu.make_async_copy(text_in, layer.sm, local.at[10])
    text.start()
    again.wait()
    layer.self_back()
    g_so.second()
    g_co.fourth()
    g_cross.third()
    text.wait()
    layer.norm_into(layer.sm, 0)
    layer.first_up()
    layer.first_grads()
    g_self.begin(0)
    g_self.begin(1)
    g_so.third()
    save.wait()
    layer.first_back(layer.sm, layer.t3)
    save = pltpu.make_async_copy(layer.t3, text_out, local.at[12])
    save.start()
    norm = NormSum(at, norm_sums, norm_recv, nsend, nrecv)
    norm.start(0)
    g_self.second()
    norm.finish(0)
    norm.start(1)
    g_out.fifth()
    g_in.fifth()
    g_cross.fourth()
    norm.finish(1)
    norm.start(2)
    g_self.third()
    g_co.fifth()
    g_so.fourth()
    norm.finish(2)
    norm.start(3)
    depth = shards[0].shape[0]

    def lay(out, blocks):
        both = jnp.concatenate(blocks, axis=0)
        rows_ = out.shape[0]
        out[...] = dot_nt(pick(rows_, both.shape[1], at.c * rows_), both).astype(BF)

    def lay_small(group, start):
        group.last()
        for w in range(group.count):
            lay(outs[start + w], [group.fin[0, w], group.fin[1, w]])

    g_out.last()
    count = g_out.count
    lay(
        outs[9],
        [
            jnp.concatenate([g_out.fin[h, j] for j in range(count)], axis=1)
            for h in range(2)
        ],
    )
    g_in.last()
    lay(outs[8], [g_in.fin[h, s] for h in range(2) for s in range(count)])
    norm.finish(3)
    norm.start(4)
    g_cross.fifth()
    g_so.fifth()
    lay_small(g_co, 7)
    g_self.fourth()
    norm.finish(4)
    norm_out[...] = norm_sums[5]
    lay_small(g_cross, 4)
    lay_small(g_so, 3)
    g_self.fifth()
    lay_small(g_self, 0)
    save.wait()
    keep.wait()
    for k in range(1, 8):
        ref = rows_out.at[lax.rem(at.m + 8 - k, 8)]
        remote(ref, ref, bsend, brecv, k - 1, at.sib).wait_recv()
    for copy in backs + norm.out:
        copy.wait_send()
    for group in (g_out, g_in, g_co, g_cross, g_so, g_self):
        group.drain()


def whole(shards, rows, text, top, valid, allow, norms, own_images):
    depth, width = shards[0].shape
    dmodel = depth * 4
    half = width // 2
    half_in = shards[8].shape[1] // 2
    ff = half_in * 16
    shapes = [
        (8, 4, 2, 2, half, dmodel),
        (1, 4, 2, 2, half_in, dmodel),
        (1, 4, 2, 2, half, ff),
    ]
    tokens = text.shape[0]
    mem_rows = rows.shape[0] * rows.shape[1]
    groups = dmodel // 256
    any_ = pl.BlockSpec(memory_space=pl.ANY)
    vmem = pl.BlockSpec(memory_space=pltpu.VMEM)
    sems = pltpu.SemaphoreType.DMA
    scratch = [pltpu.VMEM(s, BF) for s in shapes]
    scratch += [
        pltpu.VMEM((8, 2 * depth, width), BF),
        pltpu.VMEM((2 * depth, 2 * half_in), BF),
        pltpu.VMEM((ff // 2, width), BF),
    ]
    for count in REDUCE_COUNTS:
        scratch += reduce_bufs(count, half, dmodel // 2)
    scratch += [pltpu.VMEM((tokens, dmodel), BF) for _ in NAMES]
    scratch += [pltpu.VMEM((tokens, dmodel), F32) for _ in WIDE]
    scratch += [
        pltpu.VMEM((mem_rows, dmodel), BF),
        pltpu.VMEM((mem_rows, dmodel), BF),
        pltpu.VMEM((mem_rows, dmodel), BF),
        pltpu.VMEM((own_images // 2, groups, 512, 128), BF),
        pltpu.VMEM((6, 8, dmodel), F32),
        pltpu.VMEM((5, 8, dmodel), F32),
    ]
    for n in (10, 4 * GATHER_SLOTS, len(REDUCE_COUNTS) * REDUCE_SLOTS, 7, 7, 5):
        scratch += [sems((n,)), sems((n,))]
    scratch += [sems((14,))]
    return pl.pallas_call(
        functools.partial(whole_kernel, own_images),
        out_shape=[jax.ShapeDtypeStruct(s.shape, BF) for s in shards]
        + [
            jax.ShapeDtypeStruct(text.shape, BF),
            jax.ShapeDtypeStruct(text.shape, BF),
            jax.ShapeDtypeStruct(rows.shape, BF),
            jax.ShapeDtypeStruct((8, dmodel), F32),
            jax.ShapeDtypeStruct((own_images // 2, groups, 512, 128), BF),
        ],
        in_specs=[any_] * 13 + [vmem] * 3,
        out_specs=[vmem] * 10 + [any_] * 3 + [vmem, any_],
        scratch_shapes=scratch,
        compiler_params=pltpu.CompilerParams(
            collective_id=0, has_side_effects=True, vmem_limit_bytes=63 << 20
        ),
    )(*shards, rows, text, top, valid, allow, norms)


def fits(mesh_shape, text, memory, mats):
    images, txt, dmodel = text.shape
    depth, width = mats[0].shape
    return (
        mesh_shape["dp"] == 4
        and mesh_shape["mem"] == 8
        and images == 8
        and txt == HEAD == 64
        and memory.shape[0] == 8 * images
        and (memory.shape[1] * 8) % 32 == 0
        and dmodel == HEADS * HEAD == 4 * depth == 8 * width
        and dmodel % 256 == 0
        and width % 32 == 0
        and mats[8].shape == (depth, 4 * width)
        and mats[9].shape == (4 * depth, width)
    )


def shards_lean(text, lengths, memory, out_grad, *params):
    mats, norms = params[:10], params[10:]
    images, txt, dmodel = text.shape
    tokens = images * txt
    valid = jnp.arange(txt)[None, :] < lengths[:, None]
    place = jnp.arange(2 * txt)
    causal = (place[None, :] // txt == place[:, None] // txt) & (
        place[None, :] <= place[:, None]
    )
    allow = causal[None] & valid.reshape(images // 2, 1, 2 * txt)
    spread = jnp.broadcast_to(valid.reshape(tokens, 1), (tokens, 128))
    rows = memory.reshape(8, -1, dmodel)
    *weight_sums, layer_out, text_grad, back, norm_sums, _ = whole(
        mats,
        rows,
        text.reshape(tokens, dmodel),
        out_grad.reshape(tokens, dmodel),
        spread.astype(BF),
        allow.astype(BF),
        jnp.stack(norms + norms[:2]),
        images,
    )
    return (
        layer_out.reshape(text.shape),
        text_grad.reshape(text.shape),
        back.reshape(memory.shape),
        *(total.astype(F32) for total in weight_sums),
        *(norm_sums[i] for i in range(6)),
    )


def solution(mesh):
    def pick_form(text, lengths, memory, out_grad, *params):
        lean = fits(mesh.shape, text, memory, params[:10])
        form = shards_lean if lean else shards
        return form(text, lengths, memory, out_grad, *params)

    return jax.shard_map(
        pick_form,
        mesh=mesh,
        in_specs=(
            P(("dp", "mem"), None, None),
            P(("dp", "mem")),
            P("dp", "mem", None),
            P(("dp", "mem"), None, None),
            P("dp", "mem"),
            P("dp", "mem"),
            P("dp", "mem"),
            P("dp", "mem"),
            P("dp", "mem"),
            P("dp", "mem"),
            P("dp", "mem"),
            P("dp", "mem"),
            P("dp", "mem"),
            P("dp", "mem"),
            P(),
            P(),
            P(),
            P(),
            P(),
            P(),
        ),
        out_specs=(
            P(("dp", "mem"), None, None),
            P(("dp", "mem"), None, None),
            P("dp", "mem", None),
            P("dp", "mem"),
            P("dp", "mem"),
            P("dp", "mem"),
            P("dp", "mem"),
            P("dp", "mem"),
            P("dp", "mem"),
            P("dp", "mem"),
            P("dp", "mem"),
            P("dp", "mem"),
            P("dp", "mem"),
            P(),
            P(),
            P(),
            P(),
            P(),
            P(),
        ),
        check_vma=False,
    )
```

```python
import functools

import jax
import jax.numpy as jnp
from jax import lax
from jax.experimental import pallas as pl
from jax.experimental.pallas import tpu as pltpu
from jax.sharding import PartitionSpec as P

HEADS = 12
HEAD = 64
MESH = pl.DeviceIdType.MESH
BF = jnp.bfloat16
F32 = jnp.float32
EPS = 1e-06
NEG = -1e30


def layer_norm(values, scaling, offsets):
    center = values - jnp.mean(values, axis=-1, keepdims=True)
    spread = jnp.mean(center * center, axis=-1, keepdims=True)
    return center * lax.rsqrt(spread + EPS) * scaling + offsets


def norm_back(values, scaling, offsets, upstream):
    _, pull_back = jax.vjp(layer_norm, values, scaling, offsets)
    return pull_back(upstream)


def split_heads(values):
    return values.reshape(values.shape[0], values.shape[1], HEADS, HEAD)


def join_heads(values):
    return values.reshape(values.shape[0], values.shape[1], HEADS * HEAD)


def apply_mat(acts, matrix):
    return jnp.einsum("bsd,de->bse", acts, matrix, preferred_element_type=jnp.float32)


def apply_back(grads, matrix):
    return jnp.einsum("bse,de->bsd", grads, matrix, preferred_element_type=jnp.float32)


def mat_grad(acts, grads):
    return jnp.einsum("bsd,bse->de", acts, grads, preferred_element_type=jnp.float32)


def score_rows(queries, keys, allowed):
    score_scale = HEAD ** (-0.5)
    scores = (
        jnp.einsum(
            "bshd,bthd->bhst",
            split_heads(queries),
            split_heads(keys),
            preferred_element_type=jnp.float32,
        )
        * score_scale
    )
    if allowed is not None:
        scores = jnp.where(allowed, scores, NEG)
    return scores


def attend_fwd(queries, keys, values, allowed):
    scores = score_rows(queries, keys, allowed)
    highest = jnp.max(scores, axis=-1, keepdims=True)
    powered = jnp.exp(scores - highest)
    expo_sum = jnp.sum(powered, axis=-1, keepdims=True)
    weights = (powered / expo_sum).astype(jnp.bfloat16)
    mixed_heads = jnp.einsum(
        "bhst,bthd->bshd", weights, split_heads(values), preferred_element_type=jnp.float32
    )
    return (join_heads(mixed_heads).astype(jnp.bfloat16), highest + jnp.log(expo_sum))


def attend_back(queries, keys, values, allowed, log_sum, upstream):
    score_scale = HEAD ** (-0.5)
    probs_full = jnp.exp(score_rows(queries, keys, allowed) - log_sum)
    heads_up = split_heads(upstream)
    prob_grad = jnp.einsum(
        "bshd,bthd->bhst", heads_up, split_heads(values), preferred_element_type=jnp.float32
    )
    score_low = (
        probs_full * (prob_grad - jnp.sum(prob_grad * probs_full, axis=-1, keepdims=True))
    ).astype(jnp.bfloat16)
    value_grad = jnp.einsum(
        "bhst,bshd->bthd",
        probs_full.astype(jnp.bfloat16),
        heads_up,
        preferred_element_type=jnp.float32,
    )
    query_grad = (
        jnp.einsum(
            "bhst,bthd->bshd", score_low, split_heads(keys), preferred_element_type=jnp.float32
        )
        * score_scale
    )
    key_grad = (
        jnp.einsum(
            "bhst,bshd->bthd", score_low, split_heads(queries), preferred_element_type=jnp.float32
        )
        * score_scale
    )
    return (
        join_heads(query_grad).astype(jnp.bfloat16),
        join_heads(key_grad).astype(jnp.bfloat16),
        join_heads(value_grad).astype(jnp.bfloat16),
    )


def fetch_weights(mats):
    columns = (
        lax.all_gather(mats[0], "mem", axis=1, tiled=True),
        lax.all_gather(mats[1], "mem", axis=1, tiled=True),
        lax.all_gather(mats[2], "mem", axis=1, tiled=True),
        lax.all_gather(mats[3], "mem", axis=1, tiled=True),
        lax.all_gather(mats[4], "mem", axis=1, tiled=True),
        lax.all_gather(mats[5], "mem", axis=1, tiled=True),
        lax.all_gather(mats[6], "mem", axis=1, tiled=True),
        lax.all_gather(mats[7], "mem", axis=1, tiled=True),
        lax.all_gather(mats[8], "mem", axis=1, tiled=True),
        lax.all_gather(mats[9], "mem", axis=1, tiled=True),
    )
    return (
        lax.all_gather(columns[0], "dp", axis=0, tiled=True),
        lax.all_gather(columns[1], "dp", axis=0, tiled=True),
        lax.all_gather(columns[2], "dp", axis=0, tiled=True),
        lax.all_gather(columns[3], "dp", axis=0, tiled=True),
        lax.all_gather(columns[4], "dp", axis=0, tiled=True),
        lax.all_gather(columns[5], "dp", axis=0, tiled=True),
        lax.all_gather(columns[6], "dp", axis=0, tiled=True),
        lax.all_gather(columns[7], "dp", axis=0, tiled=True),
        lax.all_gather(columns[8], "dp", axis=0, tiled=True),
        lax.all_gather(columns[9], "dp", axis=0, tiled=True),
    )


def reduce_all(grads):
    row_sums = (
        lax.psum_scatter(
            grads[0].astype(jnp.bfloat16), "dp", scatter_dimension=0, tiled=True
        ).astype(jnp.float32),
        lax.psum_scatter(
            grads[1].astype(jnp.bfloat16), "dp", scatter_dimension=0, tiled=True
        ).astype(jnp.float32),
        lax.psum_scatter(
            grads[2].astype(jnp.bfloat16), "dp", scatter_dimension=0, tiled=True
        ).astype(jnp.float32),
        lax.psum_scatter(
            grads[3].astype(jnp.bfloat16), "dp", scatter_dimension=0, tiled=True
        ).astype(jnp.float32),
        lax.psum_scatter(
            grads[4].astype(jnp.bfloat16), "dp", scatter_dimension=0, tiled=True
        ).astype(jnp.float32),
        lax.psum_scatter(
            grads[5].astype(jnp.bfloat16), "dp", scatter_dimension=0, tiled=True
        ).astype(jnp.float32),
        lax.psum_scatter(
            grads[6].astype(jnp.bfloat16), "dp", scatter_dimension=0, tiled=True
        ).astype(jnp.float32),
        lax.psum_scatter(
            grads[7].astype(jnp.bfloat16), "dp", scatter_dimension=0, tiled=True
        ).astype(jnp.float32),
        lax.psum_scatter(
            grads[8].astype(jnp.bfloat16), "dp", scatter_dimension=0, tiled=True
        ).astype(jnp.float32),
        lax.psum_scatter(
            grads[9].astype(jnp.bfloat16), "dp", scatter_dimension=0, tiled=True
        ).astype(jnp.float32),
    )
    return (
        lax.psum_scatter(
            row_sums[0].astype(jnp.bfloat16), "mem", scatter_dimension=1, tiled=True
        ).astype(jnp.float32),
        lax.psum_scatter(
            row_sums[1].astype(jnp.bfloat16), "mem", scatter_dimension=1, tiled=True
        ).astype(jnp.float32),
        lax.psum_scatter(
            row_sums[2].astype(jnp.bfloat16), "mem", scatter_dimension=1, tiled=True
        ).astype(jnp.float32),
        lax.psum_scatter(
            row_sums[3].astype(jnp.bfloat16), "mem", scatter_dimension=1, tiled=True
        ).astype(jnp.float32),
        lax.psum_scatter(
            row_sums[4].astype(jnp.bfloat16), "mem", scatter_dimension=1, tiled=True
        ).astype(jnp.float32),
        lax.psum_scatter(
            row_sums[5].astype(jnp.bfloat16), "mem", scatter_dimension=1, tiled=True
        ).astype(jnp.float32),
        lax.psum_scatter(
            row_sums[6].astype(jnp.bfloat16), "mem", scatter_dimension=1, tiled=True
        ).astype(jnp.float32),
        lax.psum_scatter(
            row_sums[7].astype(jnp.bfloat16), "mem", scatter_dimension=1, tiled=True
        ).astype(jnp.float32),
        lax.psum_scatter(
            row_sums[8].astype(jnp.bfloat16), "mem", scatter_dimension=1, tiled=True
        ).astype(jnp.float32),
        lax.psum_scatter(
            row_sums[9].astype(jnp.bfloat16), "mem", scatter_dimension=1, tiled=True
        ).astype(jnp.float32),
    )


def shards(
    text,
    lengths,
    memory,
    out_grad,
    self_query,
    self_key,
    self_value,
    self_output,
    cross_query,
    cross_key,
    cross_value,
    cross_output,
    hidden_in,
    hidden_out,
    first_gain,
    first_shift,
    second_gain,
    second_shift,
    third_gain,
    third_shift,
):
    mats = (
        self_query,
        self_key,
        self_value,
        self_output,
        cross_query,
        cross_key,
        cross_value,
        cross_output,
        hidden_in,
        hidden_out,
    )
    full_mats = fetch_weights(mats)
    w_query, w_key, w_value, w_output, m_query, m_key, m_value, m_output, w_in, w_out = full_mats
    places = jnp.arange(text.shape[1])
    valid_row = places[None, :] < lengths[:, None]
    allowed = (places[None, :] <= places[:, None])[None, None] & valid_row[:, None, None, :]
    residual = text.astype(jnp.float32)
    first = layer_norm(residual, first_gain, first_shift).astype(jnp.bfloat16)
    queries = apply_mat(first, w_query).astype(jnp.bfloat16)
    keys = apply_mat(first, w_key).astype(jnp.bfloat16)
    values = apply_mat(first, w_value).astype(jnp.bfloat16)
    self_mixed, self_lse = attend_fwd(queries, keys, values, allowed)
    after_self = residual + apply_mat(self_mixed, w_output)
    memory_rows = lax.all_to_all(memory, "mem", split_axis=0, concat_axis=1, tiled=True)
    second = layer_norm(after_self, second_gain, second_shift).astype(jnp.bfloat16)
    cross_queries = apply_mat(second, m_query).astype(jnp.bfloat16)
    mem_keys = apply_mat(memory_rows, m_key).astype(jnp.bfloat16)
    mem_values = apply_mat(memory_rows, m_value).astype(jnp.bfloat16)
    cross_mixed, cross_lse = attend_fwd(cross_queries, mem_keys, mem_values, None)
    after_cross = after_self + apply_mat(cross_mixed, m_output)
    third = layer_norm(after_cross, third_gain, third_shift).astype(jnp.bfloat16)
    before_act = apply_mat(third, w_in)
    activated = jax.nn.gelu(before_act).astype(jnp.bfloat16)
    final = after_cross + apply_mat(activated, w_out)
    layer_out = jnp.where(valid_row[:, :, None], final, 0.0).astype(jnp.bfloat16)
    b_query, b_key, b_value, b_output, n_query, n_key, n_value, n_output, b_in, b_out = full_mats
    grad_top = jnp.where(valid_row[:, :, None], out_grad.astype(jnp.float32), 0.0)
    top_low = grad_top.astype(jnp.bfloat16)
    hidden_out_grad = mat_grad(activated, top_low)
    _, gelu_pull = jax.vjp(jax.nn.gelu, before_act)
    act_low = gelu_pull(apply_back(top_low, b_out))[0].astype(jnp.bfloat16)
    hidden_in_grad = mat_grad(third, act_low)
    cross_input, third_gain_grad, third_shift_grad = norm_back(
        after_cross, third_gain, third_shift, apply_back(act_low, b_in)
    )
    grad_cross = grad_top + cross_input
    cross_low = grad_cross.astype(jnp.bfloat16)
    cross_output_grad = mat_grad(cross_mixed, cross_low)
    mixed_up = apply_back(cross_low, n_output).astype(jnp.bfloat16)
    cross_query_low, mem_key_low, mem_value_low = attend_back(
        cross_queries, mem_keys, mem_values, None, cross_lse, mixed_up
    )
    cross_query_grad = mat_grad(second, cross_query_low)
    cross_key_grad = mat_grad(memory_rows, mem_key_low)
    cross_value_grad = mat_grad(memory_rows, mem_value_low)
    mem_back = (apply_back(mem_key_low, n_key) + apply_back(mem_value_low, n_value)).astype(
        jnp.bfloat16
    )
    memory_grad = lax.all_to_all(mem_back, "mem", split_axis=1, concat_axis=0, tiled=True)
    self_input, second_gain_grad, second_shift_grad = norm_back(
        after_self, second_gain, second_shift, apply_back(cross_query_low, n_query)
    )
    grad_self = grad_cross + self_input
    self_low = grad_self.astype(jnp.bfloat16)
    self_output_grad = mat_grad(self_mixed, self_low)
    self_up = apply_back(self_low, b_output).astype(jnp.bfloat16)
    query_low, key_low, value_low = attend_back(queries, keys, values, allowed, self_lse, self_up)
    self_query_grad = mat_grad(first, query_low)
    self_key_grad = mat_grad(first, key_low)
    self_value_grad = mat_grad(first, value_low)
    first_up = (
        apply_back(query_low, b_query) + apply_back(key_low, b_key) + apply_back(value_low, b_value)
    )
    text_input, first_gain_grad, first_shift_grad = norm_back(
        residual, first_gain, first_shift, first_up
    )
    text_grad = (grad_self + text_input).astype(jnp.bfloat16)
    weight_sums = reduce_all(
        (
            self_query_grad,
            self_key_grad,
            self_value_grad,
            self_output_grad,
            cross_query_grad,
            cross_key_grad,
            cross_value_grad,
            cross_output_grad,
            hidden_in_grad,
            hidden_out_grad,
        )
    )
    norm_sums = lax.psum(
        (
            first_gain_grad,
            first_shift_grad,
            second_gain_grad,
            second_shift_grad,
            third_gain_grad,
            third_shift_grad,
        ),
        ("dp", "mem"),
    )
    return (
        layer_out,
        text_grad,
        memory_grad,
        weight_sums[0],
        weight_sums[1],
        weight_sums[2],
        weight_sums[3],
        weight_sums[4],
        weight_sums[5],
        weight_sums[6],
        weight_sums[7],
        weight_sums[8],
        weight_sums[9],
        norm_sums[0],
        norm_sums[1],
        norm_sums[2],
        norm_sums[3],
        norm_sums[4],
        norm_sums[5],
    )


class Place:
    def __init__(self):
        self.d = lax.axis_index("dp")
        self.m = lax.axis_index("mem")
        self.c = lax.rem(self.d, 2)
        self.x = lax.div(self.d, 2)
        self.y = lax.rem(self.m, 2)
        self.z = lax.div(self.m, 2)
        self.oc, self.ox, self.oy = 1 - self.c, 1 - self.x, 1 - self.y
        self.sib = (self.x * 2 + self.oc, self.m)
        self.xn = (self.ox * 2 + self.c, self.m)
        self.yn = (self.d, self.z * 2 + self.oy)

    def zup(self, k):
        return lax.rem(self.z + k, 4)

    def zpeer(self, k):
        return (self.d, self.zup(k) * 2 + self.y)

    def mpeer(self, k):
        return (self.d, lax.rem(self.m + k, 8))


def greet(at):
    barrier = pltpu.get_barrier_semaphore()
    for peer in [at.sib, at.xn] + [at.mpeer(k) for k in range(1, 8)]:
        pl.semaphore_signal(barrier, inc=1, device_id=peer, device_id_type=MESH)
    pl.semaphore_wait(barrier, 9)


def remote(src, dst, sends, recvs, idx, peer):
    return pltpu.make_async_remote_copy(
        src_ref=src,
        dst_ref=dst,
        send_sem=sends.at[idx],
        recv_sem=recvs.at[idx],
        device_id=peer,
        device_id_type=MESH,
    )


class Gather:
    def __init__(self, at, full, span, via_y, sends, recvs, base):
        self.at, self.full, self.span = at, full, span
        self.sends, self.recvs, self.base = sends, recvs, base
        self.lanes = full.shape[-1] // 2
        self.cuts = ((0, via_y), (via_y, self.lanes - via_y))
        self.out = []

    def piece(self, z, y, h, x, cut=None):
        start, size = cut or (0, self.lanes)
        lo = pl.multiple_of(x * self.lanes + start, 128)
        return self.full.at[self.span, z, y, h, :, pl.ds(lo, size)]

    def copy(self, slot, src, dst, peer):
        return remote(src, dst, self.sends, self.recvs, self.base + slot, peer)

    def send(self, slot, src, dst, peer):
        copy = self.copy(slot, src, dst, peer)
        copy.start()
        self.out.append(copy)

    def got(self, slot, ref):
        self.copy(slot, ref, ref, self.at.sib).wait_recv()

    def begin(self):
        at = self.at
        own = self.piece(at.z, at.y, at.c, at.x)
        for k in (1, 2, 3):
            self.send(k - 1, own, own, at.zpeer(k))
        self.send(3, own, own, at.xn)
        self.send(7, own, own, at.yn)
        self.send(13, own, own, at.sib)

    def second(self):
        at = self.at
        for k in (1, 2, 3):
            ref = self.piece(at.zup(4 - k), at.y, at.c, at.x)
            self.got(k - 1, ref)
            self.send(3 + k, ref, ref, at.xn)
            self.send(7 + k, ref, ref, at.yn)
            self.send(13 + k, ref, ref, at.sib)

    def third(self):
        at, every = self.at, slice(None)
        for k in range(4):
            self.got(3 + k, self.piece(at.zup(4 - k), at.y, at.c, at.ox))
        ref = self.piece(every, at.y, at.c, at.ox, self.cuts[0])
        self.send(11, ref, ref, at.yn)
        ref = self.piece(every, at.y, at.c, at.ox)
        self.send(17, ref, ref, at.sib)
        for k in range(4):
            self.got(7 + k, self.piece(at.zup(4 - k), at.oy, at.c, at.x))
        ref = self.piece(every, at.oy, at.c, at.x, self.cuts[1])
        self.send(12, ref, ref, at.xn)
        ref = self.piece(every, at.oy, at.c, at.x)
        self.send(18, ref, ref, at.sib)

    def fourth(self):
        at = self.at
        for part, cut in enumerate(self.cuts):
            ref = self.piece(slice(None), at.oy, at.c, at.ox, cut)
            self.got(11 + part, ref)
            self.send(19 + part, ref, ref, at.sib)

    def last(self):
        at, every = self.at, slice(None)
        for k in range(4):
            self.got(13 + k, self.piece(at.zup(4 - k), at.y, at.oc, at.x))
        self.got(17, self.piece(every, at.y, at.oc, at.ox))
        self.got(18, self.piece(every, at.oy, at.oc, at.x))
        for part, cut in enumerate(self.cuts):
            self.got(19 + part, self.piece(every, at.oy, at.oc, at.ox, cut))

    def drain(self):
        for copy in self.out:
            copy.wait_send()
        self.out = []


GATHER_SLOTS = 21


class Reduce:
    def __init__(self, at, full, span, bufs, sends, recvs, base):
        self.at, self.full, self.span = at, full, span
        self.chip, self.via_y, self.via_x, self.rx, self.ry, self.rz, self.fin = bufs
        self.sends, self.recvs, self.base = sends, recvs, base
        self.count, self.lanes = self.chip.shape[0], full.shape[-1] // 2
        cut = self.via_y.shape[-1]
        self.cuts = (slice(0, cut), slice(cut, self.lanes))
        self.out = []

    send, got, copy, drain = Gather.send, Gather.got, Gather.copy, Gather.drain

    def begin(self):
        at = self.at
        for x in range(2):
            lanes = slice(x * self.lanes, (x + 1) * self.lanes)
            src = self.full.at[self.span, :, :, at.oc, :, lanes]
            self.send(x, src, self.chip.at[:, x], at.sib)

    def second(self):
        at = self.at
        chip, full, lanes, w0 = self.chip, self.full, self.lanes, self.span.start
        for x in range(2):
            self.got(x, chip.at[:, x])

        def add(i, carry):
            w, r = lax.div(i, 8), lax.rem(i, 8)
            z, y = lax.div(r, 2), lax.rem(r, 2)
            for x in range(2):
                mine = full[w0 + w, z, y, at.c, :, x * lanes : (x + 1) * lanes]
                chip[w, x, z, y] = (
                    chip[w, x, z, y].astype(F32) + mine.astype(F32)
                ).astype(BF)
            return carry

        lax.fori_loop(0, 8 * self.count, add, 0)
        self.send(2, chip.at[:, at.ox, :, at.oy, :, self.cuts[0]], self.via_y, at.yn)
        self.send(3, chip.at[:, at.ox, :, at.oy, :, self.cuts[1]], self.via_x, at.xn)

    def third(self):
        at, chip = self.at, self.chip
        for part, (ref, x, y) in enumerate(
            ((self.via_y, at.ox, at.y), (self.via_x, at.x, at.oy))
        ):
            self.got(2 + part, ref)
            cut = self.cuts[part]

            def add(i, carry, ref=ref, x=x, y=y, cut=cut):
                w, z = lax.div(i, 4), lax.rem(i, 4)
                chip[w, x, z, y, :, cut] = (
                    chip[w, x, z, y, :, cut].astype(F32) + ref[w, z].astype(F32)
                ).astype(BF)
                return carry

            lax.fori_loop(0, 4 * self.count, add, 0)
        self.send(4, chip.at[:, at.ox, :, at.y], self.rx, at.xn)
        self.send(5, chip.at[:, at.x, :, at.oy], self.ry, at.yn)

    def fourth(self):
        at, chip = self.at, self.chip
        self.got(4, self.rx)
        self.got(5, self.ry)

        def add(i, carry):
            w, z = lax.div(i, 4), lax.rem(i, 4)
            chip[w, at.x, z, at.y] = (
                chip[w, at.x, z, at.y].astype(F32)
                + self.rx[w, z].astype(F32)
                + self.ry[w, z].astype(F32)
            ).astype(BF)
            return carry

        lax.fori_loop(0, 4 * self.count, add, 0)
        for k in (1, 2, 3):
            self.send(
                5 + k, chip.at[:, at.x, at.zup(k), at.y], self.rz.at[k - 1], at.zpeer(k)
            )

    def fifth(self):
        at = self.at
        for k in (1, 2, 3):
            self.got(5 + k, self.rz.at[k - 1])

        def add(w, carry):
            total = self.chip[w, at.x, at.z, at.y].astype(F32)
            for k in range(3):
                total = total + self.rz[k, w].astype(F32)
            self.fin[w, at.c] = total.astype(BF)
            return carry

        lax.fori_loop(0, self.count, add, 0)
        mine = self.fin.at[:, at.c]
        self.send(9, mine, mine, at.sib)

    def last(self):
        self.got(9, self.fin.at[:, self.at.oc])


REDUCE_SLOTS = 10


def reduce_bufs(count, rows, lanes, cut):
    return [
        pltpu.VMEM((count, 2, 4, 2, rows, lanes), BF),
        pltpu.VMEM((count, 4, rows, cut), BF),
        pltpu.VMEM((count, 4, rows, lanes - cut), BF),
        pltpu.VMEM((count, 4, rows, lanes), BF),
        pltpu.VMEM((count, 4, rows, lanes), BF),
        pltpu.VMEM((3, count, rows, lanes), BF),
        pltpu.VMEM((count, 2, rows, lanes), BF),
    ]


def pick(rows, cols, start):
    col = lax.broadcasted_iota(jnp.int32, (rows, cols), 1)
    row = lax.broadcasted_iota(jnp.int32, (rows, cols), 0)
    return jnp.where(col == row + start, 1.0, 0.0).astype(BF)


def dot_nt(a, b):
    return lax.dot_general(a, b, (((1,), (1,)), ((), ())), preferred_element_type=F32)


def dot_nn(a, b):
    return lax.dot_general(a, b, (((1,), (0,)), ((), ())), preferred_element_type=F32)


def dot_tn(a, b):
    return lax.dot_general(a, b, (((0,), (0,)), ((), ())), preferred_element_type=F32)


def norm_stats(values):
    center = values - jnp.mean(values, axis=-1, keepdims=True)
    scale = lax.rsqrt(jnp.mean(center * center, axis=-1, keepdims=True) + EPS)
    return center * scale, scale


def gelu_both(value):
    c0, c1 = 0.7978845608028654, 0.044715
    square = value * value
    tanh = jnp.tanh(c0 * value * (1.0 + c1 * square))
    half = 0.5 + 0.5 * tanh
    slope = half + 0.5 * value * (1.0 - tanh * tanh) * (c0 + 3.0 * c0 * c1 * square)
    return value * half, slope


def softmax(scores):
    powered = jnp.exp(scores - jnp.max(scores, axis=-1, keepdims=True))
    return powered / jnp.sum(powered, axis=-1, keepdims=True)


class Layer:
    def __init__(self, **refs):
        self.__dict__.update(refs)
        self.tokens, self.dmodel = self.nrm.shape
        self.images = self.own_images
        self.txt = self.tokens // self.images
        self.mem_len = self.mk.shape[0] // self.images
        lane = lax.broadcasted_iota(jnp.int32, (1, 4 * HEAD), 1)
        self.head_lanes = [
            jnp.where((lane >= HEAD * h) & (lane < HEAD * (h + 1)), 1.0, 0.0)
            for h in range(4)
        ]

    def weight(self, i):
        return self.full_s[i].reshape(self.dmodel, self.dmodel)

    def put_weight(self, i, value):
        self.full_s[i] = value.astype(BF).reshape(self.full_s.shape[1:])

    def blocks(self, size, fn, total=None):
        def step(i, carry):
            fn(pl.ds(pl.multiple_of(i * size, size), size))
            return carry

        lax.fori_loop(0, (total or self.tokens) // size, step, 0)

    def spread(self, value):
        return jnp.concatenate(
            [value * mask.astype(BF) for mask in self.head_lanes], axis=0
        )

    def gather_heads(self, value):
        n = value.shape[0] // 4
        out = value[:n] * self.head_lanes[0]
        for h in range(1, 4):
            out = out + value[h * n : (h + 1) * n] * self.head_lanes[h]
        return out

    def norm_into(self, source, index):
        gain, shift = self.norms[2 * index : 2 * index + 1], self.norms[2 * index + 1 : 2 * index + 2]

        def block(rows):
            hat, _ = norm_stats(source[rows, :].astype(F32))
            self.nrm[rows, :] = (hat * gain + shift).astype(BF)

        self.blocks(128, block)

    def norm_back(self, source, upstream, index, finish):
        gain = self.norms[2 * index : 2 * index + 1]

        def step(i, carry):
            rows = pl.ds(pl.multiple_of(i * 64, 64), 64)
            hat, scale = norm_stats(source[rows, :].astype(F32))
            up = upstream[rows, :]
            scaled = up * gain
            first = jnp.mean(scaled, axis=-1, keepdims=True)
            second = jnp.mean(scaled * hat, axis=-1, keepdims=True)
            finish(rows, scale * (scaled - first - hat * second))
            gains, shifts = carry
            return (
                gains + jnp.sum(up * hat, axis=0, keepdims=True),
                shifts + jnp.sum(up, axis=0, keepdims=True),
            )

        zero = jnp.zeros((1, self.dmodel), F32)
        gains, shifts = lax.fori_loop(0, self.tokens // 64, step, (zero, zero))
        self.norm_grads[2 * index : 2 * index + 1, :] = gains
        self.norm_grads[2 * index + 1 : 2 * index + 2, :] = shifts


    def project(self, out, source, i):
        value = self.memory() if source is self else source[...]
        out[...] = dot_nt(value, self.weight(i)).astype(BF)

    def allowed(self, p):
        n = 2 * self.txt
        row = lax.broadcasted_iota(jnp.int32, (n, n), 0)
        col = lax.broadcasted_iota(jnp.int32, (n, n), 1)
        late = col >= self.txt
        length = jnp.where(
            late, self.txt + self.lengths[2 * p + 1], self.lengths[2 * p]
        )
        return (col <= row) & (col < length) & (late == (row >= self.txt))

    def self_forward(self, start, stop):
        def pair(p, carry):
            rows = pl.ds(pl.multiple_of(p * 128, 128), 128)
            allow = self.allowed(p)
            for g in range(self.dmodel // 256):
                cols = slice(256 * g, 256 * g + 256)
                scores = dot_nt(self.spread(self.q[rows, cols]), self.k[rows, cols])
                scores = scores.reshape(4, 128, 128) * HEAD**-0.5
                scores = jnp.where(allow[None], scores, NEG)
                probs = softmax(scores).reshape(512, 128).astype(BF)
                self.ps[p, g] = probs
                mixed = dot_nn(probs, self.v[rows, cols])
                self.sm[rows, cols] = self.gather_heads(mixed).astype(BF)
            return carry

        lax.fori_loop(start, stop, pair, 0)

    def add_after_self(self):
        def block(rows):
            self.after_self[rows, :] = self.io[rows, :].astype(F32) + dot_nt(
                self.sm[rows, :], self.weight(3)
            )

        self.blocks(256, block)

    def memory_in(self):
        n, size = self.images, self.mem_len
        total = n * size

        def block(i, carry):
            row = lax.broadcasted_iota(jnp.int32, (size, total), 0)
            col = lax.broadcasted_iota(jnp.int32, (size, total), 1)
            hot = jnp.where(col == n * row + i, 1.0, 0.0).astype(BF)
            rows = pl.ds(pl.multiple_of(i * size, 32), size)
            self.mk[rows, :] = dot_nn(hot, self.memory()).astype(BF)
            return carry

        lax.fori_loop(0, n, block, 0)
        self.rows[...] = self.mk[...].reshape(self.rows.shape)

    def memory(self):
        return self.rows[...].reshape(self.mk.shape)

    def memory_out(self):
        n, size = self.images, self.mem_len
        short, total = size // n, n * size

        def block(b, carry):
            row = lax.broadcasted_iota(jnp.int32, (size, total), 0)
            col = lax.broadcasted_iota(jnp.int32, (size, total), 1)
            image = row & (n - 1)
            slot = lax.shift_right_logical(row, n.bit_length() - 1) + b * short
            hot = jnp.where(col == image * size + slot, 1.0, 0.0).astype(BF)
            back = dot_nn(hot, self.mk[...]).astype(BF)
            self.rows[b] = back.reshape(self.rows.shape[1:])
            return carry

        lax.fori_loop(0, n, block, 0)

    def probs_at(self, i, g):
        size = 4 * self.txt
        start = pl.multiple_of(lax.rem(i, 2) * size, size)
        return lax.div(i, 2), g, pl.ds(start, size), slice(0, self.mem_len)

    def cross_forward(self, start, stop):
        def image(i, carry):
            rows = pl.ds(pl.multiple_of(i * self.txt, 64), self.txt)
            mems = pl.ds(pl.multiple_of(i * self.mem_len, 32), self.mem_len)
            for g in range(self.dmodel // 256):
                cols = slice(256 * g, 256 * g + 256)
                scores = dot_nt(self.spread(self.cq[rows, cols]), self.mk[mems, cols])
                probs = softmax(scores * HEAD**-0.5).astype(BF)
                self.ps[self.probs_at(i, g)] = probs
                mixed = dot_nn(probs, self.mv[mems, cols])
                self.cm[rows, cols] = self.gather_heads(mixed).astype(BF)
            return carry

        lax.fori_loop(start, stop, image, 0)

    def add_after_cross(self):
        def block(rows):
            self.after_cross[rows, :] = self.after_self[rows, :] + dot_nt(
                self.cm[rows, :], self.weight(7)
            )

        self.blocks(256, block)


    def mask_top(self):
        def block(rows):
            self.io[rows, :] = self.io[rows, :] * self.valid[rows, :1]

        self.blocks(128, block)

    def feed_start(self):
        def block(rows):
            self.acc_out[rows, :] = self.after_cross[rows, :]
            self.acc_up[rows, :] = jnp.zeros((128, self.dmodel), F32)

        self.blocks(128, block)

    def feed_chunk(self, s):
        dmodel = self.dmodel
        units = self.t2.shape[1]

        def w_in(lo=0, n=units):
            return self.full_in[s].reshape(units, dmodel)[lo : lo + n]

        def w_out(lo=0, n=units):
            return self.full_out[s, :, :, :, :, lo : lo + n].reshape(dmodel, n)

        def block(rows):
            for lo in range(0, units, 512):
                before = dot_nt(self.nrm[rows, :], w_in(lo, 512))
                act, slope = gelu_both(before)
                self.t2[rows, lo : lo + 512] = act.astype(BF)
                up = dot_nn(self.io[rows, :], w_out(lo, 512))
                self.t3[rows, lo : lo + 512] = (slope * up).astype(BF)

        self.blocks(256, block)

        def block(rows):
            self.acc_out[rows, :] += dot_nt(self.t2[rows, :], w_out())
            self.acc_up[rows, :] += dot_nn(self.t3[rows, :], w_in())

        self.blocks(256, block)
        shape = self.full_out.shape[1:5]
        for lo in range(0, units, 512):
            grad = dot_tn(self.io[...], self.t2[:, lo : lo + 512]).astype(BF)
            self.full_out[s, :, :, :, :, lo : lo + 512] = grad.reshape(shape + (512,))
        grad = dot_tn(self.t3[...], self.nrm[...]).astype(BF)
        self.full_in[s] = grad.reshape(self.full_in.shape[1:])

    def layer_out(self, out):
        def block(rows):
            out[rows, : self.dmodel] = (self.acc_out[rows, :] * self.valid[rows, :1].astype(F32)).astype(BF)

        self.blocks(128, block)


    def third_back(self):
        def finish(rows, grad):
            total = self.io[rows, :].astype(F32) + grad
            self.acc_up[rows, :] = total
            self.io[rows, :] = total.astype(BF)

        self.norm_back(self.after_cross, self.acc_up, 2, finish)

    def output_back(self, i, mixed, out):
        out[:, : self.dmodel] = dot_nn(self.io[...], self.weight(i)).astype(BF)
        self.put_weight(i, dot_tn(self.io[...], mixed[...]))

    def attend_back(self, probs, up, q, k, v, rows, mems, cols):
        low_q = self.spread(q[rows, cols])
        low_up = self.spread(up[rows, cols])
        keys, values = k[mems, cols], v[mems, cols]
        full = probs.astype(F32)
        prob_grad = dot_nt(low_up, values)
        score = full * (prob_grad - jnp.sum(prob_grad * full, axis=-1, keepdims=True))
        score = (score * HEAD**-0.5).astype(BF)
        v[mems, cols] = dot_tn(probs, low_up).astype(BF)
        k[mems, cols] = dot_tn(score, low_q).astype(BF)
        q[rows, cols] = self.gather_heads(dot_nn(score, keys)).astype(BF)

    def cross_back(self, start, stop):
        def image(i, carry):
            rows = pl.ds(pl.multiple_of(i * self.txt, 64), self.txt)
            mems = pl.ds(pl.multiple_of(i * self.mem_len, 32), self.mem_len)
            for g in range(self.dmodel // 256):
                cols = slice(256 * g, 256 * g + 256)
                probs = self.ps[self.probs_at(i, g)]
                self.attend_back(
                    probs, self.t2, self.cq, self.mk, self.mv, rows, mems, cols
                )
            return carry

        lax.fori_loop(start, stop, image, 0)

    def self_back(self, start, stop):
        def pair(p, carry):
            rows = pl.ds(pl.multiple_of(p * 128, 128), 128)
            for g in range(self.dmodel // 256):
                cols = slice(256 * g, 256 * g + 256)
                self.attend_back(
                    self.ps[p, g], self.t2, self.q, self.k, self.v, rows, rows, cols
                )
            return carry

        lax.fori_loop(start, stop, pair, 0)

    def memory_back(self):
        key_grad = dot_tn(self.mk[...], self.memory())

        def block(rows):
            total = dot_nn(self.mk[rows, :], self.weight(5)) + dot_nn(
                self.mv[rows, :], self.weight(6)
            )
            self.mk[rows, :] = total.astype(BF)

        self.blocks(256, block, self.mk.shape[0])
        self.put_weight(5, key_grad)
        self.put_weight(6, dot_tn(self.mv[...], self.memory()))
        self.memory_out()

    def second_up(self):
        def block(rows):
            self.acc_out[rows, :] = dot_nn(self.cq[rows, :], self.weight(4))

        self.blocks(256, block)

    def query_grad(self):
        self.put_weight(4, dot_tn(self.cq[...], self.nrm[...]))

    def second_back(self):
        def finish(rows, grad):
            total = self.acc_up[rows, :] + grad
            self.acc_up[rows, :] = total
            self.io[rows, :] = total.astype(BF)

        self.norm_back(self.after_self, self.acc_out, 1, finish)

    def first_up(self):
        def block(rows):
            self.acc_out[rows, :] = (
                dot_nn(self.q[rows, :], self.weight(0))
                + dot_nn(self.k[rows, :], self.weight(1))
                + dot_nn(self.v[rows, :], self.weight(2))
            )

        self.blocks(256, block)

    def first_grads(self):
        for i, low in enumerate((self.q, self.k, self.v)):
            self.put_weight(i, dot_tn(low[...], self.nrm[...]))

    def first_back(self, text, out):
        def finish(rows, grad):
            out[rows, : self.dmodel] = (self.acc_up[rows, :] + grad).astype(BF)

        self.norm_back(text, self.acc_out, 0, finish)


class NormSum:
    def __init__(self, at, sums, recv, sends, recvs):
        self.at, self.sums, self.recv, self.sends, self.recvs = at, sums, recv, sends, recvs
        flip = (at.d, (at.z + 1 - 2 * lax.rem(at.z, 2)) * 2 + at.y)
        self.peers = [at.sib, at.xn, at.yn, flip, at.zpeer(2)]
        self.out = []

    def start(self, i):
        copy = remote(
            self.sums.at[i], self.recv.at[i], self.sends, self.recvs, i, self.peers[i]
        )
        copy.start()
        self.out.append(copy)

    def finish(self, i):
        self.out[i].wait_recv()
        self.sums[i + 1] = self.sums[i] + self.recv[i]


SMALL = ((0, 3), (3, 5), (5, 7), (7, 8))
SMALL_BACK = ((7, 8), (4, 7), (3, 4), (0, 3))
THIRDS = 3
NAMES = ("nrm", "io", "q", "k", "v", "sm", "cq", "cm")
WIDE = ("after_self", "after_cross", "acc_out", "acc_up")


def whole_kernel(own_images, *refs):
    refs = list(refs)

    def take(n):
        out = refs[:n]
        del refs[:n]
        return out

    shards, (rows_in, text_in, top_in, lengths), vectors = take(10), take(4), take(6)
    fins, (layer_out, text_out, rows_out, norm_out, spill) = take(3), take(5)
    full_s, full_in, full_out, pair_s, pair_in, pair_out = take(6)
    bufs = [take(7) for _ in range(2 * THIRDS + len(SMALL_BACK))]
    narrow, wide = take(len(NAMES)), take(len(WIDE))
    t2, t3, rows, mk, mv, ps, valid, norms, norm_sums, norm_recv = take(10)
    (psend, precv, gsend, grecv, hsend, hrecv, rsend, rrecv, bsend, brecv, nsend, nrecv, local) = refs
    at = Place()
    greet(at)
    layer = Layer(
        own_images=own_images,
        full_s=full_s,
        full_in=full_in,
        full_out=full_out,
        rows=rows,
        mk=mk,
        mv=mv,
        ps=ps,
        t2=t2,
        t3=t3,
        lengths=lengths,
        valid=valid,
        norms=norms,
        norm_grads=norm_sums.at[0],
        **dict(zip(NAMES, narrow)),
        **dict(zip(WIDE, wide)),
    )
    half, dmodel = full_s.shape[4:]
    lanes, half_in, lanes_out = dmodel // 2, full_in.shape[4], full_out.shape[5] // 2

    pairs = [pair_s.at[i] for i in range(8)] + [pair_in]
    own, other = [], []
    for i in range(9):
        depth = shards[i].shape[0]
        mine = pairs[i].at[pl.ds(pl.multiple_of(at.c * depth, 8), depth), :]
        other.append(remote(shards[i], mine, psend, precv, i, at.sib))
        own.append(pltpu.make_async_copy(shards[i], mine, local.at[i]))
    for core, peer in ((at.c, None), (at.oc, at.sib)):
        src = shards[9].at[pl.ds(pl.multiple_of(core * half, 16), half), :]
        if peer is None:
            own.append(pltpu.make_async_copy(src, pair_out.at[at.c], local.at[9]))
        else:
            other.append(remote(src, pair_out.at[at.c], psend, precv, 9, peer))
    for a, b in zip(other, own):
        a.start()
        b.start()
    load = pltpu.make_async_copy(text_in, layer.io, local.at[10])
    load.start()

    def ready(i):
        own[i].wait()
        if i < 9:
            depth = shards[i].shape[0]
            theirs = pairs[i].at[pl.ds(pl.multiple_of(at.oc * depth, 8), depth), :]
        else:
            theirs = pair_out.at[at.oc]
        remote(theirs, theirs, psend, precv, i, at.sib).wait_recv()

    x_lanes = pl.ds(pl.multiple_of(at.x * lanes, 128), lanes)

    def lay_small(w):
        ready(w)
        block = dot_nt(pick(half, 2 * half, at.c * half), pair_s[w])
        full_s[w, at.z, at.y, at.c, :, x_lanes] = block.astype(BF)

    def lay_third(s):
        start = 2 * half_in * s + at.c * half_in
        block = dot_nt(pick(half_in, pair_in.shape[1], start), pair_in[...])
        full_in[s, at.z, at.y, at.c, :, x_lanes] = block.astype(BF)
        for b in range(4):
            lo = pl.multiple_of(at.x * lanes_out + 128 * b, 128)
            cut = (b % 2) * (128 * THIRDS) + 128 * s
            full_out[s, at.z, at.y, at.c, :, pl.ds(lo, 128)] = pair_out[
                b // 2, :, cut : cut + 128
            ]

    g_small = [
        Gather(at, full_s, slice(*span), 128, gsend, grecv, GATHER_SLOTS * g)
        for g, span in enumerate(SMALL)
    ]
    g_feed = []
    for s in range(THIRDS):
        base = GATHER_SLOTS * (len(SMALL) + 2 * s)
        span = slice(s, s + 1)
        g_feed.append(
            (
                Gather(at, full_in, span, 128, gsend, grecv, base),
                Gather(at, full_out, span, 256, gsend, grecv, base + GATHER_SLOTS),
            )
        )
    for group in g_small:
        for w in range(group.span.start, group.span.stop):
            lay_small(w)
        group.begin()
    ready(8)
    ready(9)
    for s in range(THIRDS):
        lay_third(s)
        for group in g_feed[s]:
            group.begin()

    mems = []
    for k in range(1, 8):
        to = lax.rem(at.m + k, 8)
        src = rows_in.at[:, pl.ds(pl.multiple_of(to * own_images, 8), own_images), :]
        copy = remote(src, rows.at[at.m], rsend, rrecv, k - 1, at.mpeer(k))
        copy.start()
        mems.append(copy)
    here = pl.ds(pl.multiple_of(at.m * own_images, 8), own_images)
    keep = pltpu.make_async_copy(rows_in.at[:, here, :], rows.at[at.m], local.at[11])
    keep.start()

    for i, vector in enumerate(vectors):
        norms[i : i + 1, :] = vector[...].reshape(1, dmodel)
    row = lax.broadcasted_iota(jnp.int32, valid.shape, 0)
    limit = jnp.zeros(valid.shape, jnp.int32)
    for i in range(own_images):
        first = i * layer.txt
        limit = jnp.where(row >= first, first + lengths[i], limit)
    valid[...] = jnp.where(row < limit, 1.0, 0.0).astype(BF)

    def each(groups, name):
        for group in groups:
            getattr(group, name)()

    g0, g1, g2, g3 = g_small
    f0, f1, f2 = g_feed
    load.wait()
    layer.norm_into(layer.io, 0)
    g0.second()
    g0.third()
    g1.second()
    g0.fourth()
    g2.second()
    g0.last()
    layer.project(layer.q, layer.nrm, 0)
    g1.third()
    layer.project(layer.k, layer.nrm, 1)
    layer.project(layer.v, layer.nrm, 2)
    g3.second()
    layer.self_forward(0, 1)
    g1.fourth()
    layer.self_forward(1, 2)
    g2.third()
    each(f0, "second")
    layer.self_forward(2, 3)
    g1.last()
    layer.self_forward(3, 4)
    away = pltpu.make_async_copy(ps, spill, local.at[13])
    away.start()
    g2.fourth()
    layer.add_after_self()
    g3.third()
    each(f1, "second")
    top = pltpu.make_async_copy(top_in, layer.io, local.at[10])
    top.start()
    layer.norm_into(layer.after_self, 1)
    layer.project(layer.cq, layer.nrm, 4)
    keep.wait()
    for k in range(1, 8):
        ref = rows.at[lax.rem(at.m + 8 - k, 8)]
        remote(ref, ref, rsend, rrecv, k - 1, at.sib).wait_recv()
    layer.memory_in()
    g3.fourth()
    g2.last()
    each(f0, "third")
    layer.project(layer.mk, layer, 5)
    layer.project(layer.mv, layer, 6)
    each(f2, "second")
    away.wait()
    layer.cross_forward(0, 2)
    each(f0, "fourth")
    layer.cross_forward(2, 4)
    each(f1, "third")
    layer.cross_forward(4, 6)
    g3.last()
    layer.cross_forward(6, 8)
    layer.add_after_cross()
    layer.norm_into(layer.after_cross, 2)
    top.wait()
    layer.mask_top()
    layer.feed_start()
    for copy in other + mems:
        copy.wait_send()
    each(g_small, "drain")

    r_feed, r_small = [], []
    for s in range(THIRDS):
        span = slice(s, s + 1)
        r_feed.append(
            [
                Reduce(at, full, span, bufs[2 * s + i], hsend, hrecv, REDUCE_SLOTS * (2 * s + i))
                for i, full in enumerate((full_in, full_out))
            ]
        )
    for g, span in enumerate(SMALL_BACK):
        n = 2 * THIRDS + g
        r_small.append(
            Reduce(at, full_s, slice(*span), bufs[n], hsend, hrecv, REDUCE_SLOTS * n)
        )
    r0, r1, r2 = r_feed
    r_co, r_cross, r_so, r_self = r_small

    each(f0, "last")
    each(f0, "drain")
    each(f1, "fourth")
    layer.feed_chunk(0)
    each(r0, "begin")
    each(f2, "third")
    each(f1, "last")
    each(f1, "drain")
    each(r0, "second")
    layer.feed_chunk(1)
    each(r1, "begin")
    each(f2, "fourth")
    each(r0, "third")
    each(f2, "last")
    each(f2, "drain")
    each(r1, "second")
    layer.feed_chunk(2)
    each(r2, "begin")
    layer.layer_out(t3)
    save = pltpu.make_async_copy(t3.at[:, 0:dmodel], layer_out, local.at[12])
    save.start()
    each(r1, "third")
    each(r2, "second")
    layer.third_back()
    layer.output_back(7, layer.cm, t2)
    r_co.begin()
    each(r0, "fourth")
    layer.cross_back(0, 3)
    each(r2, "third")
    r_co.second()
    layer.cross_back(3, 6)
    each(r1, "fourth")
    layer.cross_back(6, 8)
    again = pltpu.make_async_copy(spill, ps, local.at[13])
    again.start()
    r_co.third()
    layer.second_up()
    layer.norm_into(layer.after_self, 1)
    layer.query_grad()
    layer.memory_back()
    r_cross.begin()
    backs = []
    for k in range(1, 8):
        to = lax.rem(at.m + k, 8)
        copy = remote(rows.at[to], rows_out.at[:, here, :], bsend, brecv, k - 1, at.mpeer(k))
        copy.start()
        backs.append(copy)
    keep = pltpu.make_async_copy(rows.at[at.m], rows_out.at[:, here, :], local.at[11])
    keep.start()
    layer.second_back()
    each(r2, "fourth")
    r_cross.second()
    layer.output_back(3, layer.sm, t2)
    r_so.begin()
    text = pltpu.make_async_copy(text_in, layer.sm, local.at[10])
    text.start()
    again.wait()
    layer.self_back(0, 2)
    r_co.fourth()
    r_so.second()
    layer.self_back(2, 4)
    r_cross.third()
    text.wait()
    layer.norm_into(layer.sm, 0)
    layer.first_up()
    layer.first_grads()
    r_self.begin()
    r_so.third()
    save.wait()
    layer.first_back(layer.sm, t3)
    save = pltpu.make_async_copy(t3.at[:, 0:dmodel], text_out, local.at[12])
    save.start()
    norm = NormSum(at, norm_sums, norm_recv, nsend, nrecv)
    norm.start(0)
    r_self.second()
    norm.finish(0)
    norm.start(1)
    each(r0, "fifth")
    each(r1, "fifth")
    norm.finish(1)
    norm.start(2)
    r_cross.fourth()
    r_so.fourth()
    r_self.third()
    norm.finish(2)
    norm.start(3)
    each(r2, "fifth")
    r_co.fifth()
    norm.finish(3)
    norm.start(4)
    stores = []

    def store(group, out):
        group.last()
        copy = pltpu.make_async_copy(
            group.fin, out.at[group.span], local.at[14 + len(stores)]
        )
        copy.start()
        stores.append(copy)

    fin_s, fin_in, fin_out = fins
    for s in range(THIRDS):
        store(r_feed[s][0], fin_in)
        store(r_feed[s][1], fin_out)
    r_self.fourth()
    r_cross.fifth()
    r_so.fifth()
    norm.finish(4)
    norm_out[...] = norm_sums[5]
    store(r_co, fin_s)
    r_self.fifth()
    store(r_cross, fin_s)
    store(r_so, fin_s)
    store(r_self, fin_s)
    save.wait()
    keep.wait()
    for k in range(1, 8):
        m = lax.rem(at.m + 8 - k, 8)
        there = pl.ds(pl.multiple_of(m * own_images, 8), own_images)
        ref = rows_out.at[:, there, :]
        remote(ref, ref, bsend, brecv, k - 1, at.sib).wait_recv()
    for copy in backs + norm.out:
        copy.wait_send()
    each(r_small, "drain")
    for groups in r_feed:
        each(groups, "drain")
    for copy in stores:
        copy.wait()


def whole(shards, rows, text, top, lengths, vectors):
    depth, width = shards[0].shape
    dmodel = depth * 4
    half = width // 2
    lanes = dmodel // 2
    ff = shards[8].shape[1] * 8
    units = ff // THIRDS
    half_in = units // 16
    shapes = [
        (8, 4, 2, 2, half, dmodel),
        (THIRDS, 4, 2, 2, half_in, dmodel),
        (THIRDS, 4, 2, 2, half, units),
    ]
    tokens = text.shape[0]
    images = lengths.shape[0]
    mem_rows = rows.shape[0] * rows.shape[1]
    groups = dmodel // 256
    any_ = pl.BlockSpec(memory_space=pl.ANY)
    vmem = pl.BlockSpec(memory_space=pltpu.VMEM)
    smem = pl.BlockSpec(memory_space=pltpu.SMEM)
    sems = pltpu.SemaphoreType.DMA
    scratch = [pltpu.VMEM(s, BF) for s in shapes]
    scratch += [
        pltpu.VMEM((8, 2 * depth, width), BF),
        pltpu.VMEM((2 * depth, 4 * width), BF),
        pltpu.VMEM((2, half, 4 * depth), BF),
    ]
    for _ in range(THIRDS):
        scratch += reduce_bufs(1, half_in, lanes, 128)
        scratch += reduce_bufs(1, half, units // 2, 256)
    for a, b in SMALL_BACK:
        scratch += reduce_bufs(b - a, half, lanes, 128)
    scratch += [pltpu.VMEM((tokens, dmodel), BF) for _ in NAMES]
    scratch += [pltpu.VMEM((tokens, dmodel), F32) for _ in WIDE]
    scratch += [
        pltpu.VMEM((tokens, units), BF),
        pltpu.VMEM((tokens, units), BF),
        pltpu.VMEM((8, rows.shape[0], images, dmodel), BF),
        pltpu.VMEM((mem_rows, dmodel), BF),
        pltpu.VMEM((mem_rows, dmodel), BF),
        pltpu.VMEM((images // 2, groups, 512, 128), BF),
        pltpu.VMEM((tokens, 128), BF),
        pltpu.VMEM((8, dmodel), F32),
        pltpu.VMEM((6, 8, dmodel), F32),
        pltpu.VMEM((5, 8, dmodel), F32),
    ]
    gathers = len(SMALL) + 2 * THIRDS
    reduces = len(SMALL_BACK) + 2 * THIRDS
    for n in (10, gathers * GATHER_SLOTS, reduces * REDUCE_SLOTS, 7, 7, 5):
        scratch += [sems((n,)), sems((n,))]
    scratch += [sems((14 + reduces,))]
    return pl.pallas_call(
        functools.partial(whole_kernel, images),
        out_shape=[
            jax.ShapeDtypeStruct((8, 2, half, lanes), BF),
            jax.ShapeDtypeStruct((THIRDS, 2, half_in, lanes), BF),
            jax.ShapeDtypeStruct((THIRDS, 2, half, units // 2), BF),
            jax.ShapeDtypeStruct(text.shape, BF),
            jax.ShapeDtypeStruct(text.shape, BF),
            jax.ShapeDtypeStruct(rows.shape, BF),
            jax.ShapeDtypeStruct((8, dmodel), F32),
            jax.ShapeDtypeStruct((images // 2, groups, 512, 128), BF),
        ],
        in_specs=[any_] * 13 + [smem] + [vmem] * 6,
        out_specs=[any_] * 6 + [vmem, any_],
        scratch_shapes=scratch,
        compiler_params=pltpu.CompilerParams(
            collective_id=0, has_side_effects=True, vmem_limit_bytes=63 << 20
        ),
    )(*shards, rows, text, top, lengths, *vectors)


def finish_kernel(*refs):
    fin_s, fin_in, fin_out, norm, *moved = refs[:7]
    outs, norm_outs, targets, sem = refs[7:17], refs[17:23], refs[23:26], refs[26]
    copies = []
    for i, (a, b) in enumerate(zip(moved, targets)):
        copy = pltpu.make_async_copy(a, b, sem.at[i])
        copy.start()
        copies.append(copy)
    c = lax.rem(lax.axis_index("dp"), 2)
    depth = outs[0].shape[0]
    sel = pick(depth, 2 * depth, c * depth)
    for w in range(8):
        both = fin_s[w].reshape(outs[w].shape[1], 2 * depth)
        outs[w][...] = dot_nt(sel, both)
    outs[8][...] = dot_nt(sel, fin_in[...].reshape(outs[8].shape[1], 2 * depth))
    half = fin_out.shape[2]
    for s in range(THIRDS):
        for h in range(2):
            for b in range(2):
                lo = pl.multiple_of(c * 256 + 128 * b, 128)
                cut = b * (128 * THIRDS) + 128 * s
                outs[9][half * h : half * (h + 1), cut : cut + 128] = fin_out[
                    s, h, :, pl.ds(lo, 128)
                ].astype(F32)
    for i, out in enumerate(norm_outs):
        out[...] = norm[i : i + 1, :].reshape(out.shape)
    for copy in copies:
        copy.wait()


def finish(fin_s, fin_in, fin_out, norm, moved, shapes):
    any_ = pl.BlockSpec(memory_space=pl.ANY)
    vmem = pl.BlockSpec(memory_space=pltpu.VMEM)
    return pl.pallas_call(
        finish_kernel,
        out_shape=[jax.ShapeDtypeStruct(s, F32) for s in shapes]
        + [jax.ShapeDtypeStruct(norm.shape[1:], F32)] * 6
        + [jax.ShapeDtypeStruct(a.shape, a.dtype) for a in moved],
        in_specs=[vmem] * 7,
        out_specs=[vmem] * 16 + [any_] * 3,
        scratch_shapes=[pltpu.SemaphoreType.DMA((3,))],
    )(fin_s, fin_in, fin_out, norm, *moved)


def fits(mesh_shape, text, memory, mats):
    images, txt, dmodel = text.shape
    depth, width = mats[0].shape
    return (
        mesh_shape["dp"] == 4
        and mesh_shape["mem"] == 8
        and images == 8
        and txt == HEAD == 64
        and memory.shape[0] == 8 * images
        and (memory.shape[1] * 8) % 32 == 0
        and memory.shape[1] * 8 <= 128
        and dmodel == HEADS * HEAD == 4 * depth == 8 * width
        and dmodel % 256 == 0
        and width % 32 == 0
        and mats[8].shape == (depth, 4 * width)
        and 4 * width == 128 * THIRDS
        and mats[9].shape == (4 * depth, width)
    )


def shards_lean(text, lengths, memory, out_grad, *params):
    mats, vectors = params[:10], params[10:]
    images, txt, dmodel = text.shape
    tokens = images * txt
    mats = mats[:9] + (mats[9].T,)
    fin_s, fin_in, fin_out, layer_out, text_grad, back, norm_sums, _ = whole(
        mats,
        memory.transpose(1, 0, 2),
        text.reshape(tokens, dmodel),
        out_grad.reshape(tokens, dmodel),
        lengths,
        vectors,
    )
    *grads, layer_out, text_grad, back = finish(
        fin_s,
        fin_in,
        fin_out,
        norm_sums,
        (layer_out, text_grad, back),
        [mat.shape for mat in mats],
    )
    return (
        layer_out.reshape(text.shape),
        text_grad.reshape(text.shape),
        back.transpose(1, 0, 2),
        *grads[:9],
        grads[9].T,
        *grads[10:],
    )


def solution(mesh):
    def pick_form(text, lengths, memory, out_grad, *params):
        lean = fits(mesh.shape, text, memory, params[:10])
        form = shards_lean if lean else shards
        return form(text, lengths, memory, out_grad, *params)

    return jax.shard_map(
        pick_form,
        mesh=mesh,
        in_specs=(
            P(("dp", "mem"), None, None),
            P(("dp", "mem")),
            P("dp", "mem", None),
            P(("dp", "mem"), None, None),
            P("dp", "mem"),
            P("dp", "mem"),
            P("dp", "mem"),
            P("dp", "mem"),
            P("dp", "mem"),
            P("dp", "mem"),
            P("dp", "mem"),
            P("dp", "mem"),
            P("dp", "mem"),
            P("dp", "mem"),
            P(),
            P(),
            P(),
            P(),
            P(),
            P(),
        ),
        out_specs=(
            P(("dp", "mem"), None, None),
            P(("dp", "mem"), None, None),
            P("dp", "mem", None),
            P("dp", "mem"),
            P("dp", "mem"),
            P("dp", "mem"),
            P("dp", "mem"),
            P("dp", "mem"),
            P("dp", "mem"),
            P("dp", "mem"),
            P("dp", "mem"),
            P("dp", "mem"),
            P("dp", "mem"),
            P(),
            P(),
            P(),
            P(),
            P(),
            P(),
        ),
        check_vma=False,
    )
```

```python
import functools

import jax
import jax.numpy as jnp
from jax import lax
from jax.experimental import pallas as pl
from jax.experimental.pallas import tpu as pltpu
from jax.sharding import PartitionSpec as P

HEADS = 12
HEAD = 64
MESH = pl.DeviceIdType.MESH
BF = jnp.bfloat16
F32 = jnp.float32
EPS = 1e-06
NEG = -1e30


def layer_norm(values, scaling, offsets):
    center = values - jnp.mean(values, axis=-1, keepdims=True)
    spread = jnp.mean(center * center, axis=-1, keepdims=True)
    return center * lax.rsqrt(spread + EPS) * scaling + offsets


def norm_back(values, scaling, offsets, upstream):
    _, pull_back = jax.vjp(layer_norm, values, scaling, offsets)
    return pull_back(upstream)


def split_heads(values):
    return values.reshape(values.shape[0], values.shape[1], HEADS, HEAD)


def join_heads(values):
    return values.reshape(values.shape[0], values.shape[1], HEADS * HEAD)


def apply_mat(acts, matrix):
    return jnp.einsum("bsd,de->bse", acts, matrix, preferred_element_type=jnp.float32)


def apply_back(grads, matrix):
    return jnp.einsum("bse,de->bsd", grads, matrix, preferred_element_type=jnp.float32)


def mat_grad(acts, grads):
    return jnp.einsum("bsd,bse->de", acts, grads, preferred_element_type=jnp.float32)


def score_rows(queries, keys, allowed):
    score_scale = HEAD ** (-0.5)
    scores = (
        jnp.einsum(
            "bshd,bthd->bhst",
            split_heads(queries),
            split_heads(keys),
            preferred_element_type=jnp.float32,
        )
        * score_scale
    )
    if allowed is not None:
        scores = jnp.where(allowed, scores, NEG)
    return scores


def attend_fwd(queries, keys, values, allowed):
    scores = score_rows(queries, keys, allowed)
    highest = jnp.max(scores, axis=-1, keepdims=True)
    powered = jnp.exp(scores - highest)
    expo_sum = jnp.sum(powered, axis=-1, keepdims=True)
    weights = (powered / expo_sum).astype(jnp.bfloat16)
    mixed_heads = jnp.einsum(
        "bhst,bthd->bshd", weights, split_heads(values), preferred_element_type=jnp.float32
    )
    return (join_heads(mixed_heads).astype(jnp.bfloat16), highest + jnp.log(expo_sum))


def attend_back(queries, keys, values, allowed, log_sum, upstream):
    score_scale = HEAD ** (-0.5)
    probs_full = jnp.exp(score_rows(queries, keys, allowed) - log_sum)
    heads_up = split_heads(upstream)
    prob_grad = jnp.einsum(
        "bshd,bthd->bhst", heads_up, split_heads(values), preferred_element_type=jnp.float32
    )
    score_low = (
        probs_full * (prob_grad - jnp.sum(prob_grad * probs_full, axis=-1, keepdims=True))
    ).astype(jnp.bfloat16)
    value_grad = jnp.einsum(
        "bhst,bshd->bthd",
        probs_full.astype(jnp.bfloat16),
        heads_up,
        preferred_element_type=jnp.float32,
    )
    query_grad = (
        jnp.einsum(
            "bhst,bthd->bshd", score_low, split_heads(keys), preferred_element_type=jnp.float32
        )
        * score_scale
    )
    key_grad = (
        jnp.einsum(
            "bhst,bshd->bthd", score_low, split_heads(queries), preferred_element_type=jnp.float32
        )
        * score_scale
    )
    return (
        join_heads(query_grad).astype(jnp.bfloat16),
        join_heads(key_grad).astype(jnp.bfloat16),
        join_heads(value_grad).astype(jnp.bfloat16),
    )


def fetch_weights(mats):
    columns = (
        lax.all_gather(mats[0], "mem", axis=1, tiled=True),
        lax.all_gather(mats[1], "mem", axis=1, tiled=True),
        lax.all_gather(mats[2], "mem", axis=1, tiled=True),
        lax.all_gather(mats[3], "mem", axis=1, tiled=True),
        lax.all_gather(mats[4], "mem", axis=1, tiled=True),
        lax.all_gather(mats[5], "mem", axis=1, tiled=True),
        lax.all_gather(mats[6], "mem", axis=1, tiled=True),
        lax.all_gather(mats[7], "mem", axis=1, tiled=True),
        lax.all_gather(mats[8], "mem", axis=1, tiled=True),
        lax.all_gather(mats[9], "mem", axis=1, tiled=True),
    )
    return (
        lax.all_gather(columns[0], "dp", axis=0, tiled=True),
        lax.all_gather(columns[1], "dp", axis=0, tiled=True),
        lax.all_gather(columns[2], "dp", axis=0, tiled=True),
        lax.all_gather(columns[3], "dp", axis=0, tiled=True),
        lax.all_gather(columns[4], "dp", axis=0, tiled=True),
        lax.all_gather(columns[5], "dp", axis=0, tiled=True),
        lax.all_gather(columns[6], "dp", axis=0, tiled=True),
        lax.all_gather(columns[7], "dp", axis=0, tiled=True),
        lax.all_gather(columns[8], "dp", axis=0, tiled=True),
        lax.all_gather(columns[9], "dp", axis=0, tiled=True),
    )


def reduce_all(grads):
    row_sums = (
        lax.psum_scatter(
            grads[0].astype(jnp.bfloat16), "dp", scatter_dimension=0, tiled=True
        ).astype(jnp.float32),
        lax.psum_scatter(
            grads[1].astype(jnp.bfloat16), "dp", scatter_dimension=0, tiled=True
        ).astype(jnp.float32),
        lax.psum_scatter(
            grads[2].astype(jnp.bfloat16), "dp", scatter_dimension=0, tiled=True
        ).astype(jnp.float32),
        lax.psum_scatter(
            grads[3].astype(jnp.bfloat16), "dp", scatter_dimension=0, tiled=True
        ).astype(jnp.float32),
        lax.psum_scatter(
            grads[4].astype(jnp.bfloat16), "dp", scatter_dimension=0, tiled=True
        ).astype(jnp.float32),
        lax.psum_scatter(
            grads[5].astype(jnp.bfloat16), "dp", scatter_dimension=0, tiled=True
        ).astype(jnp.float32),
        lax.psum_scatter(
            grads[6].astype(jnp.bfloat16), "dp", scatter_dimension=0, tiled=True
        ).astype(jnp.float32),
        lax.psum_scatter(
            grads[7].astype(jnp.bfloat16), "dp", scatter_dimension=0, tiled=True
        ).astype(jnp.float32),
        lax.psum_scatter(
            grads[8].astype(jnp.bfloat16), "dp", scatter_dimension=0, tiled=True
        ).astype(jnp.float32),
        lax.psum_scatter(
            grads[9].astype(jnp.bfloat16), "dp", scatter_dimension=0, tiled=True
        ).astype(jnp.float32),
    )
    return (
        lax.psum_scatter(
            row_sums[0].astype(jnp.bfloat16), "mem", scatter_dimension=1, tiled=True
        ).astype(jnp.float32),
        lax.psum_scatter(
            row_sums[1].astype(jnp.bfloat16), "mem", scatter_dimension=1, tiled=True
        ).astype(jnp.float32),
        lax.psum_scatter(
            row_sums[2].astype(jnp.bfloat16), "mem", scatter_dimension=1, tiled=True
        ).astype(jnp.float32),
        lax.psum_scatter(
            row_sums[3].astype(jnp.bfloat16), "mem", scatter_dimension=1, tiled=True
        ).astype(jnp.float32),
        lax.psum_scatter(
            row_sums[4].astype(jnp.bfloat16), "mem", scatter_dimension=1, tiled=True
        ).astype(jnp.float32),
        lax.psum_scatter(
            row_sums[5].astype(jnp.bfloat16), "mem", scatter_dimension=1, tiled=True
        ).astype(jnp.float32),
        lax.psum_scatter(
            row_sums[6].astype(jnp.bfloat16), "mem", scatter_dimension=1, tiled=True
        ).astype(jnp.float32),
        lax.psum_scatter(
            row_sums[7].astype(jnp.bfloat16), "mem", scatter_dimension=1, tiled=True
        ).astype(jnp.float32),
        lax.psum_scatter(
            row_sums[8].astype(jnp.bfloat16), "mem", scatter_dimension=1, tiled=True
        ).astype(jnp.float32),
        lax.psum_scatter(
            row_sums[9].astype(jnp.bfloat16), "mem", scatter_dimension=1, tiled=True
        ).astype(jnp.float32),
    )


def shards(
    text,
    lengths,
    memory,
    out_grad,
    self_query,
    self_key,
    self_value,
    self_output,
    cross_query,
    cross_key,
    cross_value,
    cross_output,
    hidden_in,
    hidden_out,
    first_gain,
    first_shift,
    second_gain,
    second_shift,
    third_gain,
    third_shift,
):
    mats = (
        self_query,
        self_key,
        self_value,
        self_output,
        cross_query,
        cross_key,
        cross_value,
        cross_output,
        hidden_in,
        hidden_out,
    )
    full_mats = fetch_weights(mats)
    w_query, w_key, w_value, w_output, m_query, m_key, m_value, m_output, w_in, w_out = full_mats
    places = jnp.arange(text.shape[1])
    valid_row = places[None, :] < lengths[:, None]
    allowed = (places[None, :] <= places[:, None])[None, None] & valid_row[:, None, None, :]
    residual = text.astype(jnp.float32)
    first = layer_norm(residual, first_gain, first_shift).astype(jnp.bfloat16)
    queries = apply_mat(first, w_query).astype(jnp.bfloat16)
    keys = apply_mat(first, w_key).astype(jnp.bfloat16)
    values = apply_mat(first, w_value).astype(jnp.bfloat16)
    self_mixed, self_lse = attend_fwd(queries, keys, values, allowed)
    after_self = residual + apply_mat(self_mixed, w_output)
    memory_rows = lax.all_to_all(memory, "mem", split_axis=0, concat_axis=1, tiled=True)
    second = layer_norm(after_self, second_gain, second_shift).astype(jnp.bfloat16)
    cross_queries = apply_mat(second, m_query).astype(jnp.bfloat16)
    mem_keys = apply_mat(memory_rows, m_key).astype(jnp.bfloat16)
    mem_values = apply_mat(memory_rows, m_value).astype(jnp.bfloat16)
    cross_mixed, cross_lse = attend_fwd(cross_queries, mem_keys, mem_values, None)
    after_cross = after_self + apply_mat(cross_mixed, m_output)
    third = layer_norm(after_cross, third_gain, third_shift).astype(jnp.bfloat16)
    before_act = apply_mat(third, w_in)
    activated = jax.nn.gelu(before_act).astype(jnp.bfloat16)
    final = after_cross + apply_mat(activated, w_out)
    layer_out = jnp.where(valid_row[:, :, None], final, 0.0).astype(jnp.bfloat16)
    b_query, b_key, b_value, b_output, n_query, n_key, n_value, n_output, b_in, b_out = full_mats
    grad_top = jnp.where(valid_row[:, :, None], out_grad.astype(jnp.float32), 0.0)
    top_low = grad_top.astype(jnp.bfloat16)
    hidden_out_grad = mat_grad(activated, top_low)
    _, gelu_pull = jax.vjp(jax.nn.gelu, before_act)
    act_low = gelu_pull(apply_back(top_low, b_out))[0].astype(jnp.bfloat16)
    hidden_in_grad = mat_grad(third, act_low)
    cross_input, third_gain_grad, third_shift_grad = norm_back(
        after_cross, third_gain, third_shift, apply_back(act_low, b_in)
    )
    grad_cross = grad_top + cross_input
    cross_low = grad_cross.astype(jnp.bfloat16)
    cross_output_grad = mat_grad(cross_mixed, cross_low)
    mixed_up = apply_back(cross_low, n_output).astype(jnp.bfloat16)
    cross_query_low, mem_key_low, mem_value_low = attend_back(
        cross_queries, mem_keys, mem_values, None, cross_lse, mixed_up
    )
    cross_query_grad = mat_grad(second, cross_query_low)
    cross_key_grad = mat_grad(memory_rows, mem_key_low)
    cross_value_grad = mat_grad(memory_rows, mem_value_low)
    mem_back = (apply_back(mem_key_low, n_key) + apply_back(mem_value_low, n_value)).astype(
        jnp.bfloat16
    )
    memory_grad = lax.all_to_all(mem_back, "mem", split_axis=1, concat_axis=0, tiled=True)
    self_input, second_gain_grad, second_shift_grad = norm_back(
        after_self, second_gain, second_shift, apply_back(cross_query_low, n_query)
    )
    grad_self = grad_cross + self_input
    self_low = grad_self.astype(jnp.bfloat16)
    self_output_grad = mat_grad(self_mixed, self_low)
    self_up = apply_back(self_low, b_output).astype(jnp.bfloat16)
    query_low, key_low, value_low = attend_back(queries, keys, values, allowed, self_lse, self_up)
    self_query_grad = mat_grad(first, query_low)
    self_key_grad = mat_grad(first, key_low)
    self_value_grad = mat_grad(first, value_low)
    first_up = (
        apply_back(query_low, b_query) + apply_back(key_low, b_key) + apply_back(value_low, b_value)
    )
    text_input, first_gain_grad, first_shift_grad = norm_back(
        residual, first_gain, first_shift, first_up
    )
    text_grad = (grad_self + text_input).astype(jnp.bfloat16)
    weight_sums = reduce_all(
        (
            self_query_grad,
            self_key_grad,
            self_value_grad,
            self_output_grad,
            cross_query_grad,
            cross_key_grad,
            cross_value_grad,
            cross_output_grad,
            hidden_in_grad,
            hidden_out_grad,
        )
    )
    norm_sums = lax.psum(
        (
            first_gain_grad,
            first_shift_grad,
            second_gain_grad,
            second_shift_grad,
            third_gain_grad,
            third_shift_grad,
        ),
        ("dp", "mem"),
    )
    return (
        layer_out,
        text_grad,
        memory_grad,
        weight_sums[0],
        weight_sums[1],
        weight_sums[2],
        weight_sums[3],
        weight_sums[4],
        weight_sums[5],
        weight_sums[6],
        weight_sums[7],
        weight_sums[8],
        weight_sums[9],
        norm_sums[0],
        norm_sums[1],
        norm_sums[2],
        norm_sums[3],
        norm_sums[4],
        norm_sums[5],
    )


class Place:
    def __init__(self):
        self.d = lax.axis_index("dp")
        self.m = lax.axis_index("mem")
        self.c = lax.rem(self.d, 2)
        self.x = lax.div(self.d, 2)
        self.y = lax.rem(self.m, 2)
        self.z = lax.div(self.m, 2)
        self.oc, self.ox, self.oy = 1 - self.c, 1 - self.x, 1 - self.y
        self.sib = (self.x * 2 + self.oc, self.m)
        self.xn = (self.ox * 2 + self.c, self.m)
        self.yn = (self.d, self.z * 2 + self.oy)
        self.xyn = (self.ox * 2 + self.c, self.z * 2 + self.oy)

    def zup(self, k):
        return lax.rem(self.z + k, 4)

    def zpeer(self, k):
        return (self.d, self.zup(k) * 2 + self.y)

    def mpeer(self, k):
        return (self.d, lax.rem(self.m + k, 8))


def greet(at):
    barrier = pltpu.get_barrier_semaphore()
    peers = [at.sib, at.xn, at.xyn] + [at.mpeer(k) for k in range(1, 8)]
    for peer in peers:
        pl.semaphore_signal(barrier, inc=1, device_id=peer, device_id_type=MESH)
    pl.semaphore_wait(barrier, len(peers))


def remote(src, dst, send, recv, peer):
    return pltpu.make_async_remote_copy(
        src_ref=src,
        dst_ref=dst,
        send_sem=send,
        recv_sem=recv,
        device_id=peer,
        device_id_type=MESH,
    )


class Gather:
    SENDS, RECVS = 3, 8

    def __init__(self, at, full, span, via_y, sends, recvs, index):
        self.at, self.full, self.span = at, full, span
        self.sends = [sends.at[self.SENDS * index + i] for i in range(self.SENDS)]
        self.recvs = [recvs.at[self.RECVS * index + i] for i in range(self.RECVS)]
        self.lanes = full.shape[-1] // 2
        self.cuts = ((0, via_y), (via_y, self.lanes - via_y))

    def piece(self, z, y, h, x, cut=None):
        start, size = cut or (0, self.lanes)
        lo = pl.multiple_of(x * self.lanes + start, 128)
        return self.full.at[self.span, z, y, h, :, pl.ds(lo, size)]

    def send(self, kind, slot, ref, peer):
        remote(ref, ref, self.sends[kind], self.recvs[slot], peer).start()

    def got(self, slot, ref):
        remote(ref, ref, self.sends[0], self.recvs[slot], self.at.sib).wait_recv()

    def begin(self):
        at = self.at
        own = self.piece(at.z, at.y, at.c, at.x)
        for k in (1, 2, 3):
            self.send(2, k - 1, own, at.zpeer(k))
        self.send(1, 3, own, at.xn)
        self.send(1, 4, own, at.yn)
        self.send(0, 7, own, at.sib)

    def second(self, k):
        at = self.at
        ref = self.piece(at.zup(4 - k), at.y, at.c, at.x)
        self.got(k - 1, ref)
        self.send(1, 3, ref, at.xn)
        self.send(1, 4, ref, at.yn)
        self.send(0, 7, ref, at.sib)

    def third(self, part):
        at, every = self.at, slice(None)
        x, y, peer = ((at.ox, at.y, at.yn), (at.x, at.oy, at.xn))[part]
        ref = self.piece(every, y, at.c, x)
        self.got(3 + part, ref)
        self.send(1, 5 + part, self.piece(every, y, at.c, x, self.cuts[part]), peer)
        self.send(0, 7, ref, at.sib)

    def fourth(self):
        at = self.at
        for part, cut in enumerate(self.cuts):
            ref = self.piece(slice(None), at.oy, at.c, at.ox, cut)
            self.got(5 + part, ref)
            self.send(0, 7, ref, at.sib)

    def last(self):
        self.got(7, self.full.at[self.span, :, :, self.at.oc])

    def drain(self):
        at = self.at
        for kind, ref in enumerate(
            (
                self.full.at[self.span, :, :, at.c],
                self.full.at[self.span, pl.ds(0, 3), :, at.c],
                self.piece(pl.ds(0, 3), at.y, at.c, at.x),
            )
        ):
            remote(ref, ref, self.sends[kind], self.recvs[0], at.sib).wait_send()


class Reduce:
    RECVS = 7

    def __init__(self, at, full, span, bufs, sends, recvs, index):
        self.at, self.full, self.span = at, full, span
        self.chip, self.via_y, self.via_x, self.rx, self.ry, self.rz, self.fin = bufs
        self.sent = sends.at[index]
        self.recvs = [recvs.at[self.RECVS * index + i] for i in range(self.RECVS)]
        self.count, self.lanes = self.chip.shape[0], full.shape[-1] // 2
        cut = self.via_y.shape[-1]
        self.cuts = (slice(0, cut), slice(cut, self.lanes))

    def send(self, slot, src, dst, peer):
        remote(src, dst, self.sent, self.recvs[slot], peer).start()

    def got(self, slot, ref):
        remote(ref, ref, self.sent, self.recvs[slot], self.at.sib).wait_recv()

    def begin(self):
        at = self.at
        for x in range(2):
            lanes = slice(x * self.lanes, (x + 1) * self.lanes)
            src = self.full.at[self.span, :, :, at.oc, :, lanes]
            self.send(0, src, self.chip.at[:, x], at.sib)

    def second(self):
        at = self.at
        chip, full, lanes, w0 = self.chip, self.full, self.lanes, self.span.start
        self.got(0, chip)

        def add(i, carry):
            w, r = lax.div(i, 8), lax.rem(i, 8)
            z, y = lax.div(r, 2), lax.rem(r, 2)
            for x in range(2):
                mine = full[w0 + w, z, y, at.c, :, x * lanes : (x + 1) * lanes]
                chip[w, x, z, y] = (
                    chip[w, x, z, y].astype(F32) + mine.astype(F32)
                ).astype(BF)
            return carry

        lax.fori_loop(0, 8 * self.count, add, 0)
        self.send(1, chip.at[:, at.ox, :, at.oy, :, self.cuts[0]], self.via_y, at.yn)
        self.send(2, chip.at[:, at.ox, :, at.oy, :, self.cuts[1]], self.via_x, at.xn)

    def third(self, part):
        at, chip = self.at, self.chip
        ref = (self.via_y, self.via_x)[part]
        x, y = ((at.ox, at.y), (at.x, at.oy))[part]
        cut = self.cuts[part]
        self.got(1 + part, ref)

        def add(i, carry):
            w, z = lax.div(i, 4), lax.rem(i, 4)
            chip[w, x, z, y, :, cut] = (
                chip[w, x, z, y, :, cut].astype(F32) + ref[w, z].astype(F32)
            ).astype(BF)
            return carry

        lax.fori_loop(0, 4 * self.count, add, 0)
        box, peer = ((self.rx, at.xn), (self.ry, at.yn))[part]
        self.send(3 + part, chip.at[:, x, :, y], box, peer)

    def fourth(self):
        at, chip = self.at, self.chip
        self.got(3, self.rx)
        self.got(4, self.ry)

        def add(i, carry):
            w, z = lax.div(i, 4), lax.rem(i, 4)
            chip[w, at.x, z, at.y] = (
                chip[w, at.x, z, at.y].astype(F32)
                + self.rx[w, z].astype(F32)
                + self.ry[w, z].astype(F32)
            ).astype(BF)
            return carry

        lax.fori_loop(0, 4 * self.count, add, 0)
        for k in (1, 2, 3):
            src = chip.at[:, at.x, at.zup(k), at.y]
            self.send(5, src, self.rz.at[k - 1], at.zpeer(k))

    def fifth(self):
        at = self.at
        self.got(5, self.rz)

        def add(w, carry):
            total = self.chip[w, at.x, at.z, at.y].astype(F32)
            for k in range(3):
                total = total + self.rz[k, w].astype(F32)
            self.fin[w, at.c] = total.astype(BF)
            return carry

        lax.fori_loop(0, self.count, add, 0)
        mine = self.fin.at[:, at.c]
        self.send(6, mine, mine, at.sib)

    def last(self):
        self.got(6, self.fin.at[:, self.at.oc])

    def drain(self):
        ref = self.full.at[self.span]
        remote(ref, ref, self.sent, self.recvs[0], self.at.sib).wait_send()


def reduce_bufs(count, rows, lanes, cut):
    return [
        pltpu.VMEM((count, 2, 4, 2, rows, lanes), BF),
        pltpu.VMEM((count, 4, rows, cut), BF),
        pltpu.VMEM((count, 4, rows, lanes - cut), BF),
        pltpu.VMEM((count, 4, rows, lanes), BF),
        pltpu.VMEM((count, 4, rows, lanes), BF),
        pltpu.VMEM((3, count, rows, lanes), BF),
        pltpu.VMEM((count, 2, rows, lanes), BF),
    ]


def pick(rows, cols, start):
    col = lax.broadcasted_iota(jnp.int32, (rows, cols), 1)
    row = lax.broadcasted_iota(jnp.int32, (rows, cols), 0)
    return jnp.where(col == row + start, 1.0, 0.0).astype(BF)


def dot_nt(a, b):
    return lax.dot_general(a, b, (((1,), (1,)), ((), ())), preferred_element_type=F32)


def dot_nn(a, b):
    return lax.dot_general(a, b, (((1,), (0,)), ((), ())), preferred_element_type=F32)


def dot_tn(a, b):
    return lax.dot_general(a, b, (((0,), (0,)), ((), ())), preferred_element_type=F32)


def norm_stats(values):
    center = values - jnp.mean(values, axis=-1, keepdims=True)
    scale = lax.rsqrt(jnp.mean(center * center, axis=-1, keepdims=True) + EPS)
    return center * scale, scale


def gelu_both(value):
    c0, c1 = 0.7978845608028654, 0.044715
    square = value * value
    tanh = jnp.tanh(c0 * value * (1.0 + c1 * square))
    half = 0.5 + 0.5 * tanh
    slope = half + 0.5 * value * (1.0 - tanh * tanh) * (c0 + 3.0 * c0 * c1 * square)
    return value * half, slope


def softmax(scores):
    powered = jnp.exp(scores - jnp.max(scores, axis=-1, keepdims=True))
    return powered / jnp.sum(powered, axis=-1, keepdims=True)


class Layer:
    def __init__(self, **refs):
        self.__dict__.update(refs)
        self.tokens, self.dmodel = self.nrm.shape
        self.images = self.own_images
        self.txt = self.tokens // self.images
        self.mem_len = self.mkv.shape[1] // self.images
        lane = lax.broadcasted_iota(jnp.int32, (1, 4 * HEAD), 1)
        self.head_lanes = [
            jnp.where((lane >= HEAD * h) & (lane < HEAD * (h + 1)), 1.0, 0.0)
            for h in range(4)
        ]

    def weight(self, i):
        return self.full_s[i].reshape(self.dmodel, self.dmodel)

    def put_weight(self, i, value):
        self.full_s[i] = value.astype(BF).reshape(self.full_s.shape[1:])

    def blocks(self, size, fn, total=None):
        def step(i, carry):
            fn(pl.ds(pl.multiple_of(i * size, size), size))
            return carry

        lax.fori_loop(0, (total or self.tokens) // size, step, 0)

    def spread(self, value):
        return jnp.concatenate(
            [value * mask.astype(BF) for mask in self.head_lanes], axis=0
        )

    def gather_heads(self, value):
        n = value.shape[0] // 4
        out = value[:n] * self.head_lanes[0]
        for h in range(1, 4):
            out = out + value[h * n : (h + 1) * n] * self.head_lanes[h]
        return out

    def norm_into(self, source, index):
        gain, shift = self.norms[2 * index : 2 * index + 1], self.norms[2 * index + 1 : 2 * index + 2]

        def block(rows):
            hat, _ = norm_stats(source[rows, :].astype(F32))
            self.nrm[rows, :] = (hat * gain + shift).astype(BF)

        self.blocks(128, block)

    def norm_back(self, source, upstream, index, finish):
        gain = self.norms[2 * index : 2 * index + 1]

        def step(i, carry):
            rows = pl.ds(pl.multiple_of(i * 64, 64), 64)
            hat, scale = norm_stats(source[rows, :].astype(F32))
            up = upstream[rows, :]
            scaled = up * gain
            first = jnp.mean(scaled, axis=-1, keepdims=True)
            second = jnp.mean(scaled * hat, axis=-1, keepdims=True)
            finish(rows, scale * (scaled - first - hat * second))
            gains, shifts = carry
            return (
                gains + jnp.sum(up * hat, axis=0, keepdims=True),
                shifts + jnp.sum(up, axis=0, keepdims=True),
            )

        zero = jnp.zeros((1, self.dmodel), F32)
        gains, shifts = lax.fori_loop(0, self.tokens // 64, step, (zero, zero))
        self.norm_grads[2 * index : 2 * index + 1, :] = gains
        self.norm_grads[2 * index + 1 : 2 * index + 2, :] = shifts


    def project(self, outs, value, first):
        def step(i, carry):
            outs[i] = dot_nt(value(), self.weight(first + i)).astype(BF)
            return carry

        lax.fori_loop(0, outs.shape[0], step, 0)

    def allowed(self, p):
        n = 2 * self.txt
        row = lax.broadcasted_iota(jnp.int32, (n, n), 0)
        col = lax.broadcasted_iota(jnp.int32, (n, n), 1)
        late = col >= self.txt
        length = jnp.where(
            late, self.txt + self.lengths[2 * p + 1], self.lengths[2 * p]
        )
        return (col <= row) & (col < length) & (late == (row >= self.txt))

    def self_forward(self, start, stop):
        def pair(p, carry):
            rows = pl.ds(pl.multiple_of(p * 128, 128), 128)
            allow = self.allowed(p)
            for g in range(self.dmodel // 256):
                cols = slice(256 * g, 256 * g + 256)
                scores = dot_nt(self.spread(self.qkv[0, rows, cols]), self.qkv[1, rows, cols])
                scores = scores.reshape(4, 128, 128) * HEAD**-0.5
                scores = jnp.where(allow[None], scores, NEG)
                probs = softmax(scores).reshape(512, 128).astype(BF)
                self.ps[p, g] = probs
                mixed = dot_nn(probs, self.qkv[2, rows, cols])
                self.sm[rows, cols] = self.gather_heads(mixed).astype(BF)
            return carry

        lax.fori_loop(start, stop, pair, 0)

    def add_after_self(self):
        def block(rows):
            self.after_self[rows, :] = self.io[rows, :].astype(F32) + dot_nt(
                self.sm[rows, :], self.weight(3)
            )

        self.blocks(256, block)

    def memory_in(self):
        n, size = self.images, self.mem_len
        total = n * size

        def block(i, carry):
            row = lax.broadcasted_iota(jnp.int32, (size, total), 0)
            col = lax.broadcasted_iota(jnp.int32, (size, total), 1)
            hot = jnp.where(col == n * row + i, 1.0, 0.0).astype(BF)
            rows = pl.ds(pl.multiple_of(i * size, 32), size)
            self.mkv[0, rows, :] = dot_nn(hot, self.memory()).astype(BF)
            return carry

        lax.fori_loop(0, n, block, 0)
        self.rows[...] = self.mkv[0].reshape(self.rows.shape)

    def memory(self):
        return self.rows[...].reshape(self.mkv.shape[1:])

    def memory_out(self):
        n, size = self.images, self.mem_len
        short, total = size // n, n * size

        def block(b, carry):
            row = lax.broadcasted_iota(jnp.int32, (size, total), 0)
            col = lax.broadcasted_iota(jnp.int32, (size, total), 1)
            image = row & (n - 1)
            slot = lax.shift_right_logical(row, n.bit_length() - 1) + b * short
            hot = jnp.where(col == image * size + slot, 1.0, 0.0).astype(BF)
            low, high = self.cm[...], self.t2[: total - self.tokens, : self.dmodel]
            back = dot_nn(hot[:, : self.tokens], low) + dot_nn(hot[:, self.tokens :], high)
            self.rows[b] = back.astype(BF).reshape(self.rows.shape[1:])
            return carry

        lax.fori_loop(0, n, block, 0)

    def probs_at(self, i, g):
        size = 4 * self.txt
        start = pl.multiple_of(lax.rem(i, 2) * size, size)
        return lax.div(i, 2), g, pl.ds(start, size), slice(0, self.mem_len)

    def cross_forward(self, start, stop):
        def image(i, carry):
            rows = pl.ds(pl.multiple_of(i * self.txt, 64), self.txt)
            mems = pl.ds(pl.multiple_of(i * self.mem_len, 32), self.mem_len)
            for g in range(self.dmodel // 256):
                cols = slice(256 * g, 256 * g + 256)
                scores = dot_nt(self.spread(self.cq[0, rows, cols]), self.mkv[0, mems, cols])
                probs = softmax(scores * HEAD**-0.5).astype(BF)
                self.ps[self.probs_at(i, g)] = probs
                mixed = dot_nn(probs, self.mkv[1, mems, cols])
                self.cm[rows, cols] = self.gather_heads(mixed).astype(BF)
            return carry

        lax.fori_loop(start, stop, image, 0)

    def add_after_cross(self):
        def block(rows):
            self.after_cross[rows, :] = self.after_self[rows, :] + dot_nt(
                self.cm[rows, :], self.weight(7)
            )

        self.blocks(256, block)


    def mask_top(self):
        def block(rows):
            self.io[rows, :] = self.io[rows, :] * self.valid[rows, :1]

        self.blocks(128, block)

    def feed_start(self):
        def block(rows):
            self.acc_out[rows, :] = self.after_cross[rows, :]
            self.acc_up[rows, :] = jnp.zeros((128, self.dmodel), F32)

        self.blocks(128, block)

    def feed_chunk(self, s):
        dmodel = self.dmodel
        units = self.t2.shape[1]

        def w_in(lo=0, n=units):
            return self.full_in[s].reshape(units, dmodel)[lo : lo + n]

        def w_out(lo=0, n=units):
            return self.full_out[s, :, :, :, :, lo : lo + n].reshape(dmodel, n)

        def block(rows):
            for lo in range(0, units, 512):
                before = dot_nt(self.nrm[rows, :], w_in(lo, 512))
                act, slope = gelu_both(before)
                self.t2[rows, lo : lo + 512] = act.astype(BF)
                up = dot_nn(self.io[rows, :], w_out(lo, 512))
                self.t3[rows, lo : lo + 512] = (slope * up).astype(BF)

        self.blocks(256, block)

        def block(rows):
            self.acc_out[rows, :] += dot_nt(self.t2[rows, :], w_out())
            self.acc_up[rows, :] += dot_nn(self.t3[rows, :], w_in())

        self.blocks(256, block)
        shape = self.full_out.shape[1:5]
        for lo in range(0, units, 512):
            grad = dot_tn(self.io[...], self.t2[:, lo : lo + 512]).astype(BF)
            self.full_out[s, :, :, :, :, lo : lo + 512] = grad.reshape(shape + (512,))
        grad = dot_tn(self.t3[...], self.nrm[...]).astype(BF)
        self.full_in[s] = grad.reshape(self.full_in.shape[1:])

    def layer_out(self, out):
        def block(rows):
            out[rows, : self.dmodel] = (self.acc_out[rows, :] * self.valid[rows, :1].astype(F32)).astype(BF)

        self.blocks(128, block)


    def third_back(self):
        def finish(rows, grad):
            total = self.io[rows, :].astype(F32) + grad
            self.acc_up[rows, :] = total
            self.io[rows, :] = total.astype(BF)

        self.norm_back(self.after_cross, self.acc_up, 2, finish)

    def output_back(self, i, mixed, out):
        out[:, : self.dmodel] = dot_nn(self.io[...], self.weight(i)).astype(BF)
        self.put_weight(i, dot_tn(self.io[...], mixed[...]))

    def attend_back(self, probs, up, q, k, v, rows, mems, cols):
        low_q = self.spread(q[rows, cols])
        low_up = self.spread(up[rows, cols])
        keys, values = k[mems, cols], v[mems, cols]
        full = probs.astype(F32)
        prob_grad = dot_nt(low_up, values)
        score = full * (prob_grad - jnp.sum(prob_grad * full, axis=-1, keepdims=True))
        score = (score * HEAD**-0.5).astype(BF)
        v[mems, cols] = dot_tn(probs, low_up).astype(BF)
        k[mems, cols] = dot_tn(score, low_q).astype(BF)
        q[rows, cols] = self.gather_heads(dot_nn(score, keys)).astype(BF)

    def cross_back(self, start, stop):
        def image(i, carry):
            rows = pl.ds(pl.multiple_of(i * self.txt, 64), self.txt)
            mems = pl.ds(pl.multiple_of(i * self.mem_len, 32), self.mem_len)
            for g in range(self.dmodel // 256):
                cols = slice(256 * g, 256 * g + 256)
                probs = self.ps[self.probs_at(i, g)]
                self.attend_back(
                    probs,
                    self.t2,
                    self.cq.at[0],
                    self.mkv.at[0],
                    self.mkv.at[1],
                    rows,
                    mems,
                    cols,
                )
            return carry

        lax.fori_loop(start, stop, image, 0)

    def self_back(self, start, stop):
        def pair(p, carry):
            rows = pl.ds(pl.multiple_of(p * 128, 128), 128)
            for g in range(self.dmodel // 256):
                cols = slice(256 * g, 256 * g + 256)
                self.attend_back(
                    self.ps[p, g],
                    self.t2,
                    self.qkv.at[0],
                    self.qkv.at[1],
                    self.qkv.at[2],
                    rows,
                    rows,
                    cols,
                )
            return carry

        lax.fori_loop(start, stop, pair, 0)

    def memory_back(self):
        size = 256
        keys, values = self.mkv.at[0], self.mkv.at[1]

        def back(rows):
            total = dot_nn(keys[rows, :], self.weight(5)) + dot_nn(
                values[rows, :], self.weight(6)
            )
            return total.astype(BF)

        def block(rows):
            self.cm[rows, :] = back(rows)

        self.blocks(size, block)
        for start in range(self.tokens, self.mkv.shape[1], size):
            there = slice(start - self.tokens, start - self.tokens + size)
            self.t2[there, : self.dmodel] = back(slice(start, start + size))

    def weight_grads(self, lows, value, first):
        def step(i, carry):
            self.put_weight(first + i, dot_tn(lows[i], value()))
            return carry

        lax.fori_loop(0, lows.shape[0], step, 0)

    def second_up(self):
        def block(rows):
            self.acc_out[rows, :] = dot_nn(self.cq[0, rows, :], self.weight(4))

        self.blocks(256, block)

    def second_back(self):
        def finish(rows, grad):
            total = self.acc_up[rows, :] + grad
            self.acc_up[rows, :] = total
            self.io[rows, :] = total.astype(BF)

        self.norm_back(self.after_self, self.acc_out, 1, finish)

    def first_up(self):
        def block(rows):
            self.acc_out[rows, :] = (
                dot_nn(self.qkv[0, rows, :], self.weight(0))
                + dot_nn(self.qkv[1, rows, :], self.weight(1))
                + dot_nn(self.qkv[2, rows, :], self.weight(2))
            )

        self.blocks(256, block)

    def first_back(self, text, out):
        def finish(rows, grad):
            out[rows, : self.dmodel] = (self.acc_up[rows, :] + grad).astype(BF)

        self.norm_back(text, self.acc_out, 0, finish)


class NormSum:
    def __init__(self, at, sums, pair, plane, line, out, sends, recvs):
        self.at, self.sums, self.pair = at, sums, pair
        self.boxes = (plane, line)
        self.sends, self.recvs = sends, recvs
        self.me = (at.x * 2 + at.y, at.z)
        self.target = (line.at[at.z], out)
        self.peers = ((at.xn, at.yn, at.xyn), tuple(at.zpeer(k) for k in (1, 2, 3)))
        self.out = []

    def start(self, stage):
        if stage == 0:
            copy = remote(
                self.sums, self.pair, self.sends.at[0], self.recvs.at[0], self.at.sib
            )
            copy.start()
            self.out.append(copy)
            return
        box = self.boxes[stage - 1].at[self.me[stage - 1]]
        for k, peer in enumerate(self.peers[stage - 1]):
            i = 3 * stage - 2 + k
            copy = remote(box, box, self.sends.at[i], self.recvs.at[i], peer)
            copy.start()
            self.out.append(copy)

    def finish(self, stage):
        if stage == 0:
            self.out[0].wait_recv()
            self.boxes[0][self.me[0]] = self.sums[...] + self.pair[...]
            return
        for copy in self.out[3 * stage - 2 : 3 * stage + 1]:
            copy.wait_recv()
        box = self.boxes[stage - 1]
        total = box[0] + box[1] + box[2] + box[3]
        self.target[stage - 1][...] = total


SMALL = ((0, 2), (2, 3), (3, 5), (5, 7), (7, 8))
SMALL_BACK = ((7, 8), (4, 5), (3, 4), (0, 3), (5, 7))
THIRDS = 3
NAMES = ("nrm", "io", "sm", "cm")
WIDE = ("after_self", "after_cross", "acc_out", "acc_up")


def whole_kernel(own_images, *refs):
    refs = list(refs)

    def take(n):
        out = refs[:n]
        del refs[:n]
        return out

    shards, (rows_in, text_in, top_in, lengths), vectors = take(10), take(4), take(6)
    fins, (layer_out, text_out, rows_out, norm_out, spill) = take(3), take(5)
    full_s, full_in, full_out, pair_s, pair_in, pair_out = take(6)
    bufs = [take(7) for _ in range(2 * THIRDS + len(SMALL_BACK))]
    narrow, wide = take(len(NAMES)), take(len(WIDE))
    qkv, cq, mkv, t2, t3, rows, ps, valid, norms = take(9)
    norm_sums, norm_pair, norm_plane, norm_line = take(4)
    (psend, precv, gsend, grecv, hsend, hrecv, rsend, rrecv, bsend, brecv, nsend, nrecv, local) = refs
    at = Place()
    greet(at)
    layer = Layer(
        own_images=own_images,
        full_s=full_s,
        full_in=full_in,
        full_out=full_out,
        rows=rows,
        qkv=qkv,
        cq=cq,
        mkv=mkv,
        ps=ps,
        t2=t2,
        t3=t3,
        lengths=lengths,
        valid=valid,
        norms=norms,
        norm_grads=norm_sums,
        **dict(zip(NAMES, narrow)),
        **dict(zip(WIDE, wide)),
    )
    half, dmodel = full_s.shape[4:]
    lanes, half_in, lanes_out = dmodel // 2, full_in.shape[4], full_out.shape[5] // 2

    pairs = [pair_s.at[i] for i in range(8)] + [pair_in]
    own, other = [], []
    for i in range(9):
        depth = shards[i].shape[0]
        mine = pairs[i].at[pl.ds(pl.multiple_of(at.c * depth, 8), depth), :]
        other.append(remote(shards[i], mine, psend.at[i], precv.at[i], at.sib))
        own.append(pltpu.make_async_copy(shards[i], mine, local.at[i]))
    for core, peer in ((at.c, None), (at.oc, at.sib)):
        src = shards[9].at[pl.ds(pl.multiple_of(core * half, 16), half), :]
        if peer is None:
            own.append(pltpu.make_async_copy(src, pair_out.at[at.c], local.at[9]))
        else:
            other.append(remote(src, pair_out.at[at.c], psend.at[9], precv.at[9], peer))
    for a, b in zip(other, own):
        a.start()
        b.start()
    load = pltpu.make_async_copy(text_in, layer.io, local.at[10])
    load.start()

    def ready(i):
        own[i].wait()
        if i < 9:
            depth = shards[i].shape[0]
            theirs = pairs[i].at[pl.ds(pl.multiple_of(at.oc * depth, 8), depth), :]
        else:
            theirs = pair_out.at[at.oc]
        remote(theirs, theirs, psend.at[i], precv.at[i], at.sib).wait_recv()

    x_lanes = pl.ds(pl.multiple_of(at.x * lanes, 128), lanes)

    def lay_small(w):
        ready(w)
        block = dot_nt(pick(half, 2 * half, at.c * half), pair_s[w])
        full_s[w, at.z, at.y, at.c, :, x_lanes] = block.astype(BF)

    def lay_third(s, part):
        if part == 0:
            start = 2 * half_in * s + at.c * half_in
            block = dot_nt(pick(half_in, pair_in.shape[1], start), pair_in[...])
            full_in[s, at.z, at.y, at.c, :, x_lanes] = block.astype(BF)
            return
        for b in range(4):
            lo = pl.multiple_of(at.x * lanes_out + 128 * b, 128)
            cut = (b % 2) * (128 * THIRDS) + 128 * s
            full_out[s, at.z, at.y, at.c, :, pl.ds(lo, 128)] = pair_out[
                b // 2, :, cut : cut + 128
            ]

    g_small = [
        Gather(at, full_s, slice(*span), 128, gsend, grecv, g)
        for g, span in enumerate(SMALL)
    ]
    g_feed = []
    for s in range(THIRDS):
        index = len(SMALL) + 2 * s
        span = slice(s, s + 1)
        g_feed.append(
            (
                Gather(at, full_in, span, 128, gsend, grecv, index),
                Gather(at, full_out, span, 256, gsend, grecv, index + 1),
            )
        )

    def begin(group):
        for w in range(group.span.start, group.span.stop):
            lay_small(w)
        group.begin()

    arrived = []

    def begin_third(s, part):
        if part not in arrived:
            arrived.append(part)
            ready(8 + part)
        lay_third(s, part)
        g_feed[s][part].begin()

    here = pl.ds(pl.multiple_of(at.m * own_images, 8), own_images)
    keep = pltpu.make_async_copy(rows_in.at[:, here, :], rows.at[at.m], local.at[11])

    def begin_memory():
        for k in range(1, 8):
            to = lax.rem(at.m + k, 8) * own_images
            src = rows_in.at[:, pl.ds(pl.multiple_of(to, 8), own_images), :]
            remote(src, rows.at[at.m], rsend.at[0], rrecv.at[k - 1], at.mpeer(k)).start()
        keep.start()

    for i, vector in enumerate(vectors):
        norms[i : i + 1, :] = vector[...].reshape(1, dmodel)
    row = lax.broadcasted_iota(jnp.int32, valid.shape, 0)
    limit = jnp.zeros(valid.shape, jnp.int32)
    for i in range(own_images):
        first = i * layer.txt
        limit = jnp.where(row >= first, first + lengths[i], limit)
    valid[...] = jnp.where(row < limit, 1.0, 0.0).astype(BF)

    def each(groups, name):
        for group in groups:
            getattr(group, name)()

    seven = rows.at[pl.ds(0, 7)]

    def end_memory():
        keep.wait()
        for k in range(1, 8):
            ref = rows.at[lax.rem(at.m + 8 - k, 8)]
            remote(ref, ref, rsend.at[0], rrecv.at[k - 1], at.sib).wait_recv()

    def drain_small():
        for copy in other:
            copy.wait_send()
        remote(seven, seven, rsend.at[0], rrecv.at[0], at.sib).wait_send()
        each(g_small, "drain")

    def send_memory():
        for k in range(1, 8):
            src, dst = rows.at[lax.rem(at.m + k, 8)], rows_out.at[:, here, :]
            remote(src, dst, bsend.at[0], brecv.at[k - 1], at.mpeer(k)).start()
        keep_back.start()

    def move(src, dst, i):
        return pltpu.make_async_copy(src, dst, local.at[i])

    top, text = move(top_in, layer.io, 10), move(text_in, layer.sm, 10)
    away, again = move(ps, spill, 13), move(spill, ps, 13)
    packed = t3.at[:, 0:dmodel]
    save_out, save_text = move(packed, layer_out, 12), move(packed, text_out, 12)
    keep_back = move(rows.at[at.m], rows_out.at[:, here, :], 11)
    norm = NormSum(at, norm_sums, norm_pair, norm_plane, norm_line, norm_out, nsend, nrecv)
    fin_s, fin_in, fin_out = fins
    stores = []

    def store(group, out):
        group.last()
        copy = move(group.fin, out.at[group.span], 14 + len(stores))
        copy.start()
        stores.append(copy)

    r_feed, r_small = [], []
    for s in range(THIRDS):
        span = slice(s, s + 1)
        r_feed.append(
            [
                Reduce(at, full, span, bufs[2 * s + i], hsend, hrecv, 2 * s + i)
                for i, full in enumerate((full_in, full_out))
            ]
        )
    for g, span in enumerate(SMALL_BACK):
        n = 2 * THIRDS + g
        r_small.append(Reduce(at, full_s, slice(*span), bufs[n], hsend, hrecv, n))

    begin(g_small[1])
    begin(g_small[0])
    begin_third(1, 0)
    begin(g_small[2])
    g_small[0].second(1)
    begin(g_small[3])
    g_small[1].second(1)
    g_small[0].second(2)
    g_small[0].second(3)
    g_feed[1][0].second(1)
    begin(g_small[4])
    begin_third(0, 0)
    g_small[1].second(2)
    g_small[2].second(1)
    g_small[0].third(1)
    g_small[1].second(3)
    begin_third(1, 1)
    g_small[2].second(2)
    g_small[3].second(1)
    g_small[1].third(0)
    g_small[2].second(3)
    load.wait()
    layer.norm_into(layer.io, 0)
    g_small[1].third(1)
    g_small[3].second(2)
    g_small[0].third(0)
    g_small[2].third(0)
    g_small[3].second(3)
    begin_memory()
    g_feed[1][0].second(2)
    g_small[0].fourth()
    g_small[1].fourth()
    g_small[4].second(1)
    g_small[0].last()
    g_small[3].third(0)
    g_feed[1][0].second(3)
    g_small[3].third(1)
    begin_third(0, 1)
    g_small[1].last()
    g_feed[0][0].second(1)
    g_small[4].second(2)
    g_small[4].second(3)
    g_feed[0][0].second(2)
    g_feed[1][1].second(1)
    g_feed[0][0].second(3)
    g_feed[1][1].second(2)
    g_small[2].third(1)
    g_feed[1][1].second(3)
    layer.project(layer.qkv, lambda: layer.nrm[...], 0)
    layer.self_forward(0, 2)
    layer.self_forward(2, 4)
    away.start()
    g_feed[0][0].third(1)
    g_small[4].third(0)
    g_feed[1][0].third(1)
    begin_third(2, 0)
    g_small[3].fourth()
    g_small[2].fourth()
    g_feed[0][0].third(0)
    g_small[2].last()
    g_feed[1][1].third(1)
    g_feed[1][0].third(0)
    layer.add_after_self()
    top.start()
    g_small[4].third(1)
    g_feed[1][1].third(0)
    layer.norm_into(layer.after_self, 1)
    layer.project(layer.cq, lambda: layer.nrm[...], 4)
    begin_third(2, 1)
    g_small[3].last()
    g_feed[0][0].fourth()
    g_feed[0][0].last()
    g_feed[1][0].fourth()
    end_memory()
    layer.memory_in()
    g_feed[0][1].second(1)
    layer.project(layer.mkv, layer.memory, 5)
    g_feed[0][1].second(2)
    g_feed[0][1].second(3)
    g_feed[1][1].fourth()
    g_small[4].fourth()
    away.wait()
    layer.cross_forward(0, 4)
    g_feed[0][1].third(0)
    g_feed[0][1].third(1)
    g_feed[2][0].second(1)
    layer.cross_forward(4, 8)
    g_feed[2][0].second(2)
    g_feed[1][1].last()
    g_small[4].last()
    g_feed[2][1].second(1)
    g_feed[2][1].second(2)
    layer.add_after_cross()
    g_feed[0][1].fourth()
    layer.norm_into(layer.after_cross, 2)
    top.wait()
    layer.mask_top()
    layer.feed_start()
    drain_small()
    g_feed[2][1].second(3)
    g_feed[0][1].last()
    g_feed[2][0].second(3)
    each(g_feed[0], "drain")
    layer.feed_chunk(0)
    g_feed[2][1].third(1)
    r_feed[0][0].begin()
    g_feed[2][1].third(0)
    g_feed[2][0].third(0)
    g_feed[1][0].last()
    r_feed[0][1].begin()
    g_feed[2][0].third(1)
    each(g_feed[1], "drain")
    layer.feed_chunk(1)
    r_feed[0][0].second()
    g_feed[2][1].fourth()
    g_feed[2][0].fourth()
    r_feed[0][1].second()
    g_feed[2][0].last()
    r_feed[1][0].begin()
    g_feed[2][1].last()
    r_feed[0][0].third(0)
    each(g_feed[2], "drain")
    layer.feed_chunk(2)
    r_feed[0][1].third(1)
    r_feed[2][0].begin()
    r_feed[0][1].third(0)
    layer.third_back()
    r_feed[1][0].second()
    r_feed[0][0].third(1)
    layer.output_back(7, layer.cm, t2)
    r_feed[2][0].second()
    layer.cross_back(0, 4)
    r_feed[1][0].third(0)
    r_feed[1][1].begin()
    r_feed[1][0].third(1)
    r_feed[0][1].fourth()
    layer.cross_back(4, 8)
    again.start()
    r_feed[0][0].fourth()
    r_feed[2][0].third(1)
    r_feed[2][1].begin()
    r_small[0].begin()
    r_feed[2][0].third(0)
    layer.layer_out(t3)
    save_out.start()
    layer.memory_back()
    r_feed[1][0].fourth()
    r_feed[1][1].second()
    layer.second_up()
    r_small[0].second()
    layer.weight_grads(layer.mkv, layer.memory, 5)
    r_feed[2][0].fourth()
    r_feed[2][1].second()
    r_small[4].begin()
    layer.memory_out()
    r_small[0].third(0)
    r_small[0].third(1)
    send_memory()
    layer.norm_into(layer.after_self, 1)
    layer.weight_grads(layer.cq, lambda: layer.nrm[...], 4)
    r_feed[1][1].third(0)
    r_small[1].begin()
    layer.second_back()
    r_small[4].second()
    r_feed[1][1].third(1)
    r_feed[0][1].fifth()
    layer.output_back(3, layer.sm, t2)
    text.start()
    text.wait()
    layer.norm_into(layer.sm, 0)
    again.wait()
    layer.self_back(0, 2)
    r_small[1].second()
    layer.self_back(2, 4)
    r_small[4].third(0)
    layer.first_up()
    layer.weight_grads(layer.qkv, lambda: layer.nrm[...], 0)
    r_small[4].third(1)
    r_feed[2][1].third(0)
    r_small[1].third(1)
    r_feed[1][0].fifth()
    r_small[3].begin()
    r_small[0].fourth()
    r_feed[0][0].fifth()
    r_small[1].third(0)
    r_small[2].begin()
    store(r_feed[1][0], fin_in)
    r_feed[2][1].third(1)
    r_small[2].second()
    store(r_feed[0][1], fin_out)
    save_out.wait()
    layer.first_back(layer.sm, t3)
    save_text.start()
    r_feed[2][0].fifth()
    r_small[4].fourth()
    r_feed[1][1].fourth()
    r_small[3].second()
    r_small[2].third(0)
    r_small[2].third(1)
    r_small[3].third(0)
    r_small[1].fourth()
    norm.start(0)
    r_feed[2][1].fourth()
    r_small[3].third(1)
    r_small[2].fourth()
    r_feed[1][1].fifth()
    r_small[0].fifth()
    store(r_feed[2][0], fin_in)
    r_small[4].fifth()
    store(r_small[0], fin_s)
    r_small[3].fourth()
    r_small[1].fifth()
    norm.finish(0)
    norm.start(1)
    r_small[2].fifth()
    norm.finish(1)
    norm.start(2)
    store(r_feed[1][1], fin_out)
    r_feed[2][1].fifth()
    r_small[3].fifth()
    store(r_feed[0][0], fin_in)
    store(r_small[4], fin_s)
    store(r_small[2], fin_s)
    store(r_small[1], fin_s)
    store(r_small[3], fin_s)
    store(r_feed[2][1], fin_out)
    norm.finish(2)

    save_text.wait()
    keep_back.wait()
    for k in range(1, 8):
        m = lax.rem(at.m + 8 - k, 8)
        there = pl.ds(pl.multiple_of(m * own_images, 8), own_images)
        ref = rows_out.at[:, there, :]
        remote(ref, ref, bsend.at[0], brecv.at[k - 1], at.sib).wait_recv()
    remote(seven, seven, bsend.at[0], brecv.at[0], at.sib).wait_send()
    for copy in norm.out:
        copy.wait_send()
    each(r_small, "drain")
    for groups in r_feed:
        each(groups, "drain")
    for copy in stores:
        copy.wait()


def whole(shards, rows, text, top, lengths, vectors):
    depth, width = shards[0].shape
    dmodel = depth * 4
    half = width // 2
    lanes = dmodel // 2
    ff = shards[8].shape[1] * 8
    units = ff // THIRDS
    half_in = units // 16
    shapes = [
        (8, 4, 2, 2, half, dmodel),
        (THIRDS, 4, 2, 2, half_in, dmodel),
        (THIRDS, 4, 2, 2, half, units),
    ]
    tokens = text.shape[0]
    images = lengths.shape[0]
    mem_rows = rows.shape[0] * rows.shape[1]
    groups = dmodel // 256
    any_ = pl.BlockSpec(memory_space=pl.ANY)
    vmem = pl.BlockSpec(memory_space=pltpu.VMEM)
    smem = pl.BlockSpec(memory_space=pltpu.SMEM)
    sems = pltpu.SemaphoreType.DMA
    scratch = [pltpu.VMEM(s, BF) for s in shapes]
    scratch += [
        pltpu.VMEM((8, 2 * depth, width), BF),
        pltpu.VMEM((2 * depth, 4 * width), BF),
        pltpu.VMEM((2, half, 4 * depth), BF),
    ]
    for _ in range(THIRDS):
        scratch += reduce_bufs(1, half_in, lanes, 128)
        scratch += reduce_bufs(1, half, units // 2, 256)
    for a, b in SMALL_BACK:
        scratch += reduce_bufs(b - a, half, lanes, 128)
    scratch += [pltpu.VMEM((tokens, dmodel), BF) for _ in NAMES]
    scratch += [pltpu.VMEM((tokens, dmodel), F32) for _ in WIDE]
    stacks = [(3, tokens, dmodel), (1, tokens, dmodel), (2, mem_rows, dmodel)]
    scratch += [pltpu.VMEM(s, BF) for s in stacks]
    scratch += [
        pltpu.VMEM((tokens, units), BF),
        pltpu.VMEM((tokens, units), BF),
        pltpu.VMEM((8, rows.shape[0], images, dmodel), BF),
        pltpu.VMEM((images // 2, groups, 512, 128), BF),
        pltpu.VMEM((tokens, 128), BF),
        pltpu.VMEM((8, dmodel), F32),
        pltpu.VMEM((8, dmodel), F32),
        pltpu.VMEM((8, dmodel), F32),
        pltpu.VMEM((4, 8, dmodel), F32),
        pltpu.VMEM((4, 8, dmodel), F32),
    ]
    gathers = len(SMALL) + 2 * THIRDS
    reduces = len(SMALL_BACK) + 2 * THIRDS
    counts = (10, 10, Gather.SENDS * gathers, Gather.RECVS * gathers)
    counts += (reduces, Reduce.RECVS * reduces, 1, 7, 1, 7, 7, 7, 14 + reduces)
    scratch += [sems((n,)) for n in counts]
    return pl.pallas_call(
        functools.partial(whole_kernel, images),
        out_shape=[
            jax.ShapeDtypeStruct((8, 2, half, lanes), BF),
            jax.ShapeDtypeStruct((THIRDS, 2, half_in, lanes), BF),
            jax.ShapeDtypeStruct((THIRDS, 2, half, units // 2), BF),
            jax.ShapeDtypeStruct(text.shape, BF),
            jax.ShapeDtypeStruct(text.shape, BF),
            jax.ShapeDtypeStruct(rows.shape, BF),
            jax.ShapeDtypeStruct((8, dmodel), F32),
            jax.ShapeDtypeStruct((images // 2, groups, 512, 128), BF),
        ],
        in_specs=[any_] * 13 + [smem] + [vmem] * 6,
        out_specs=[any_] * 6 + [vmem, any_],
        scratch_shapes=scratch,
        compiler_params=pltpu.CompilerParams(
            collective_id=0, has_side_effects=True, vmem_limit_bytes=63 << 20
        ),
    )(*shards, rows, text, top, lengths, *vectors)


def finish_kernel(*refs):
    fin_s, fin_in, fin_out, norm, *moved = refs[:7]
    outs, norm_outs, targets, sem = refs[7:17], refs[17:23], refs[23:26], refs[26]
    copies = []
    for i, (a, b) in enumerate(zip(moved, targets)):
        copy = pltpu.make_async_copy(a, b, sem.at[i])
        copy.start()
        copies.append(copy)
    c = lax.rem(lax.axis_index("dp"), 2)
    depth = outs[0].shape[0]
    sel = pick(depth, 2 * depth, c * depth)
    for w in range(8):
        both = fin_s[w].reshape(outs[w].shape[1], 2 * depth)
        outs[w][...] = dot_nt(sel, both)
    outs[8][...] = dot_nt(sel, fin_in[...].reshape(outs[8].shape[1], 2 * depth))
    half = fin_out.shape[2]
    for s in range(THIRDS):
        for h in range(2):
            for b in range(2):
                lo = pl.multiple_of(c * 256 + 128 * b, 128)
                cut = b * (128 * THIRDS) + 128 * s
                outs[9][half * h : half * (h + 1), cut : cut + 128] = fin_out[
                    s, h, :, pl.ds(lo, 128)
                ].astype(F32)
    for i, out in enumerate(norm_outs):
        out[...] = norm[i : i + 1, :].reshape(out.shape)
    for copy in copies:
        copy.wait()


def finish(fin_s, fin_in, fin_out, norm, moved, shapes):
    any_ = pl.BlockSpec(memory_space=pl.ANY)
    vmem = pl.BlockSpec(memory_space=pltpu.VMEM)
    return pl.pallas_call(
        finish_kernel,
        out_shape=[jax.ShapeDtypeStruct(s, F32) for s in shapes]
        + [jax.ShapeDtypeStruct(norm.shape[1:], F32)] * 6
        + [jax.ShapeDtypeStruct(a.shape, a.dtype) for a in moved],
        in_specs=[vmem] * 7,
        out_specs=[vmem] * 16 + [any_] * 3,
        scratch_shapes=[pltpu.SemaphoreType.DMA((3,))],
    )(fin_s, fin_in, fin_out, norm, *moved)


def fits(mesh_shape, text, memory, mats):
    images, txt, dmodel = text.shape
    depth, width = mats[0].shape
    return (
        mesh_shape["dp"] == 4
        and mesh_shape["mem"] == 8
        and images == 8
        and txt == HEAD == 64
        and memory.shape[0] == 8 * images
        and (memory.shape[1] * 8) % 32 == 0
        and memory.shape[1] * 8 <= 128
        and dmodel == HEADS * HEAD == 4 * depth == 8 * width
        and dmodel % 256 == 0
        and width % 32 == 0
        and mats[8].shape == (depth, 4 * width)
        and 4 * width == 128 * THIRDS
        and mats[9].shape == (4 * depth, width)
    )


def shards_lean(text, lengths, memory, out_grad, *params):
    mats, vectors = params[:10], params[10:]
    images, txt, dmodel = text.shape
    tokens = images * txt
    mats = mats[:9] + (mats[9].T,)
    fin_s, fin_in, fin_out, layer_out, text_grad, back, norm_sums, _ = whole(
        mats,
        memory.transpose(1, 0, 2),
        text.reshape(tokens, dmodel),
        out_grad.reshape(tokens, dmodel),
        lengths,
        vectors,
    )
    *grads, layer_out, text_grad, back = finish(
        fin_s,
        fin_in,
        fin_out,
        norm_sums,
        (layer_out, text_grad, back),
        [mat.shape for mat in mats],
    )
    return (
        layer_out.reshape(text.shape),
        text_grad.reshape(text.shape),
        back.transpose(1, 0, 2),
        *grads[:9],
        grads[9].T,
        *grads[10:],
    )


def solution(mesh):
    def pick_form(text, lengths, memory, out_grad, *params):
        lean = fits(mesh.shape, text, memory, params[:10])
        form = shards_lean if lean else shards
        return form(text, lengths, memory, out_grad, *params)

    return jax.shard_map(
        pick_form,
        mesh=mesh,
        in_specs=(
            P(("dp", "mem"), None, None),
            P(("dp", "mem")),
            P("dp", "mem", None),
            P(("dp", "mem"), None, None),
            P("dp", "mem"),
            P("dp", "mem"),
            P("dp", "mem"),
            P("dp", "mem"),
            P("dp", "mem"),
            P("dp", "mem"),
            P("dp", "mem"),
            P("dp", "mem"),
            P("dp", "mem"),
            P("dp", "mem"),
            P(),
            P(),
            P(),
            P(),
            P(),
            P(),
        ),
        out_specs=(
            P(("dp", "mem"), None, None),
            P(("dp", "mem"), None, None),
            P("dp", "mem", None),
            P("dp", "mem"),
            P("dp", "mem"),
            P("dp", "mem"),
            P("dp", "mem"),
            P("dp", "mem"),
            P("dp", "mem"),
            P("dp", "mem"),
            P("dp", "mem"),
            P("dp", "mem"),
            P("dp", "mem"),
            P(),
            P(),
            P(),
            P(),
            P(),
            P(),
        ),
        check_vma=False,
    )
```

```python
import functools

import jax
import jax.numpy as jnp
from jax import lax
from jax.experimental import pallas as pl
from jax.experimental.pallas import tpu as pltpu
from jax.sharding import PartitionSpec as P

HEADS = 12
HEAD = 64
MESH = pl.DeviceIdType.MESH
BF = jnp.bfloat16
F32 = jnp.float32
EPS = 1e-06
NEG = -1e30


def layer_norm(values, scaling, offsets):
    center = values - jnp.mean(values, axis=-1, keepdims=True)
    spread = jnp.mean(center * center, axis=-1, keepdims=True)
    return center * lax.rsqrt(spread + EPS) * scaling + offsets


def norm_back(values, scaling, offsets, upstream):
    _, pull_back = jax.vjp(layer_norm, values, scaling, offsets)
    return pull_back(upstream)


def split_heads(values):
    return values.reshape(values.shape[0], values.shape[1], HEADS, HEAD)


def join_heads(values):
    return values.reshape(values.shape[0], values.shape[1], HEADS * HEAD)


def apply_mat(acts, matrix):
    return jnp.einsum("bsd,de->bse", acts, matrix, preferred_element_type=jnp.float32)


def apply_back(grads, matrix):
    return jnp.einsum("bse,de->bsd", grads, matrix, preferred_element_type=jnp.float32)


def mat_grad(acts, grads):
    return jnp.einsum("bsd,bse->de", acts, grads, preferred_element_type=jnp.float32)


def score_rows(queries, keys, allowed):
    score_scale = HEAD ** (-0.5)
    scores = (
        jnp.einsum(
            "bshd,bthd->bhst",
            split_heads(queries),
            split_heads(keys),
            preferred_element_type=jnp.float32,
        )
        * score_scale
    )
    if allowed is not None:
        scores = jnp.where(allowed, scores, NEG)
    return scores


def attend_fwd(queries, keys, values, allowed):
    scores = score_rows(queries, keys, allowed)
    highest = jnp.max(scores, axis=-1, keepdims=True)
    powered = jnp.exp(scores - highest)
    expo_sum = jnp.sum(powered, axis=-1, keepdims=True)
    weights = (powered / expo_sum).astype(jnp.bfloat16)
    mixed_heads = jnp.einsum(
        "bhst,bthd->bshd", weights, split_heads(values), preferred_element_type=jnp.float32
    )
    return (join_heads(mixed_heads).astype(jnp.bfloat16), highest + jnp.log(expo_sum))


def attend_back(queries, keys, values, allowed, log_sum, upstream):
    score_scale = HEAD ** (-0.5)
    probs_full = jnp.exp(score_rows(queries, keys, allowed) - log_sum)
    heads_up = split_heads(upstream)
    prob_grad = jnp.einsum(
        "bshd,bthd->bhst", heads_up, split_heads(values), preferred_element_type=jnp.float32
    )
    score_low = (
        probs_full * (prob_grad - jnp.sum(prob_grad * probs_full, axis=-1, keepdims=True))
    ).astype(jnp.bfloat16)
    value_grad = jnp.einsum(
        "bhst,bshd->bthd",
        probs_full.astype(jnp.bfloat16),
        heads_up,
        preferred_element_type=jnp.float32,
    )
    query_grad = (
        jnp.einsum(
            "bhst,bthd->bshd", score_low, split_heads(keys), preferred_element_type=jnp.float32
        )
        * score_scale
    )
    key_grad = (
        jnp.einsum(
            "bhst,bshd->bthd", score_low, split_heads(queries), preferred_element_type=jnp.float32
        )
        * score_scale
    )
    return (
        join_heads(query_grad).astype(jnp.bfloat16),
        join_heads(key_grad).astype(jnp.bfloat16),
        join_heads(value_grad).astype(jnp.bfloat16),
    )


def fetch_weights(mats):
    columns = (
        lax.all_gather(mats[0], "mem", axis=1, tiled=True),
        lax.all_gather(mats[1], "mem", axis=1, tiled=True),
        lax.all_gather(mats[2], "mem", axis=1, tiled=True),
        lax.all_gather(mats[3], "mem", axis=1, tiled=True),
        lax.all_gather(mats[4], "mem", axis=1, tiled=True),
        lax.all_gather(mats[5], "mem", axis=1, tiled=True),
        lax.all_gather(mats[6], "mem", axis=1, tiled=True),
        lax.all_gather(mats[7], "mem", axis=1, tiled=True),
        lax.all_gather(mats[8], "mem", axis=1, tiled=True),
        lax.all_gather(mats[9], "mem", axis=1, tiled=True),
    )
    return (
        lax.all_gather(columns[0], "dp", axis=0, tiled=True),
        lax.all_gather(columns[1], "dp", axis=0, tiled=True),
        lax.all_gather(columns[2], "dp", axis=0, tiled=True),
        lax.all_gather(columns[3], "dp", axis=0, tiled=True),
        lax.all_gather(columns[4], "dp", axis=0, tiled=True),
        lax.all_gather(columns[5], "dp", axis=0, tiled=True),
        lax.all_gather(columns[6], "dp", axis=0, tiled=True),
        lax.all_gather(columns[7], "dp", axis=0, tiled=True),
        lax.all_gather(columns[8], "dp", axis=0, tiled=True),
        lax.all_gather(columns[9], "dp", axis=0, tiled=True),
    )


def reduce_all(grads):
    row_sums = (
        lax.psum_scatter(
            grads[0].astype(jnp.bfloat16), "dp", scatter_dimension=0, tiled=True
        ).astype(jnp.float32),
        lax.psum_scatter(
            grads[1].astype(jnp.bfloat16), "dp", scatter_dimension=0, tiled=True
        ).astype(jnp.float32),
        lax.psum_scatter(
            grads[2].astype(jnp.bfloat16), "dp", scatter_dimension=0, tiled=True
        ).astype(jnp.float32),
        lax.psum_scatter(
            grads[3].astype(jnp.bfloat16), "dp", scatter_dimension=0, tiled=True
        ).astype(jnp.float32),
        lax.psum_scatter(
            grads[4].astype(jnp.bfloat16), "dp", scatter_dimension=0, tiled=True
        ).astype(jnp.float32),
        lax.psum_scatter(
            grads[5].astype(jnp.bfloat16), "dp", scatter_dimension=0, tiled=True
        ).astype(jnp.float32),
        lax.psum_scatter(
            grads[6].astype(jnp.bfloat16), "dp", scatter_dimension=0, tiled=True
        ).astype(jnp.float32),
        lax.psum_scatter(
            grads[7].astype(jnp.bfloat16), "dp", scatter_dimension=0, tiled=True
        ).astype(jnp.float32),
        lax.psum_scatter(
            grads[8].astype(jnp.bfloat16), "dp", scatter_dimension=0, tiled=True
        ).astype(jnp.float32),
        lax.psum_scatter(
            grads[9].astype(jnp.bfloat16), "dp", scatter_dimension=0, tiled=True
        ).astype(jnp.float32),
    )
    return (
        lax.psum_scatter(
            row_sums[0].astype(jnp.bfloat16), "mem", scatter_dimension=1, tiled=True
        ).astype(jnp.float32),
        lax.psum_scatter(
            row_sums[1].astype(jnp.bfloat16), "mem", scatter_dimension=1, tiled=True
        ).astype(jnp.float32),
        lax.psum_scatter(
            row_sums[2].astype(jnp.bfloat16), "mem", scatter_dimension=1, tiled=True
        ).astype(jnp.float32),
        lax.psum_scatter(
            row_sums[3].astype(jnp.bfloat16), "mem", scatter_dimension=1, tiled=True
        ).astype(jnp.float32),
        lax.psum_scatter(
            row_sums[4].astype(jnp.bfloat16), "mem", scatter_dimension=1, tiled=True
        ).astype(jnp.float32),
        lax.psum_scatter(
            row_sums[5].astype(jnp.bfloat16), "mem", scatter_dimension=1, tiled=True
        ).astype(jnp.float32),
        lax.psum_scatter(
            row_sums[6].astype(jnp.bfloat16), "mem", scatter_dimension=1, tiled=True
        ).astype(jnp.float32),
        lax.psum_scatter(
            row_sums[7].astype(jnp.bfloat16), "mem", scatter_dimension=1, tiled=True
        ).astype(jnp.float32),
        lax.psum_scatter(
            row_sums[8].astype(jnp.bfloat16), "mem", scatter_dimension=1, tiled=True
        ).astype(jnp.float32),
        lax.psum_scatter(
            row_sums[9].astype(jnp.bfloat16), "mem", scatter_dimension=1, tiled=True
        ).astype(jnp.float32),
    )


def shards(
    text,
    lengths,
    memory,
    out_grad,
    self_query,
    self_key,
    self_value,
    self_output,
    cross_query,
    cross_key,
    cross_value,
    cross_output,
    hidden_in,
    hidden_out,
    first_gain,
    first_shift,
    second_gain,
    second_shift,
    third_gain,
    third_shift,
):
    mats = (
        self_query,
        self_key,
        self_value,
        self_output,
        cross_query,
        cross_key,
        cross_value,
        cross_output,
        hidden_in,
        hidden_out,
    )
    full_mats = fetch_weights(mats)
    w_query, w_key, w_value, w_output, m_query, m_key, m_value, m_output, w_in, w_out = full_mats
    places = jnp.arange(text.shape[1])
    valid_row = places[None, :] < lengths[:, None]
    allowed = (places[None, :] <= places[:, None])[None, None] & valid_row[:, None, None, :]
    residual = text.astype(jnp.float32)
    first = layer_norm(residual, first_gain, first_shift).astype(jnp.bfloat16)
    queries = apply_mat(first, w_query).astype(jnp.bfloat16)
    keys = apply_mat(first, w_key).astype(jnp.bfloat16)
    values = apply_mat(first, w_value).astype(jnp.bfloat16)
    self_mixed, self_lse = attend_fwd(queries, keys, values, allowed)
    after_self = residual + apply_mat(self_mixed, w_output)
    memory_rows = lax.all_to_all(memory, "mem", split_axis=0, concat_axis=1, tiled=True)
    second = layer_norm(after_self, second_gain, second_shift).astype(jnp.bfloat16)
    cross_queries = apply_mat(second, m_query).astype(jnp.bfloat16)
    mem_keys = apply_mat(memory_rows, m_key).astype(jnp.bfloat16)
    mem_values = apply_mat(memory_rows, m_value).astype(jnp.bfloat16)
    cross_mixed, cross_lse = attend_fwd(cross_queries, mem_keys, mem_values, None)
    after_cross = after_self + apply_mat(cross_mixed, m_output)
    third = layer_norm(after_cross, third_gain, third_shift).astype(jnp.bfloat16)
    before_act = apply_mat(third, w_in)
    activated = jax.nn.gelu(before_act).astype(jnp.bfloat16)
    final = after_cross + apply_mat(activated, w_out)
    layer_out = jnp.where(valid_row[:, :, None], final, 0.0).astype(jnp.bfloat16)
    b_query, b_key, b_value, b_output, n_query, n_key, n_value, n_output, b_in, b_out = full_mats
    grad_top = jnp.where(valid_row[:, :, None], out_grad.astype(jnp.float32), 0.0)
    top_low = grad_top.astype(jnp.bfloat16)
    hidden_out_grad = mat_grad(activated, top_low)
    _, gelu_pull = jax.vjp(jax.nn.gelu, before_act)
    act_low = gelu_pull(apply_back(top_low, b_out))[0].astype(jnp.bfloat16)
    hidden_in_grad = mat_grad(third, act_low)
    cross_input, third_gain_grad, third_shift_grad = norm_back(
        after_cross, third_gain, third_shift, apply_back(act_low, b_in)
    )
    grad_cross = grad_top + cross_input
    cross_low = grad_cross.astype(jnp.bfloat16)
    cross_output_grad = mat_grad(cross_mixed, cross_low)
    mixed_up = apply_back(cross_low, n_output).astype(jnp.bfloat16)
    cross_query_low, mem_key_low, mem_value_low = attend_back(
        cross_queries, mem_keys, mem_values, None, cross_lse, mixed_up
    )
    cross_query_grad = mat_grad(second, cross_query_low)
    cross_key_grad = mat_grad(memory_rows, mem_key_low)
    cross_value_grad = mat_grad(memory_rows, mem_value_low)
    mem_back = (apply_back(mem_key_low, n_key) + apply_back(mem_value_low, n_value)).astype(
        jnp.bfloat16
    )
    memory_grad = lax.all_to_all(mem_back, "mem", split_axis=1, concat_axis=0, tiled=True)
    self_input, second_gain_grad, second_shift_grad = norm_back(
        after_self, second_gain, second_shift, apply_back(cross_query_low, n_query)
    )
    grad_self = grad_cross + self_input
    self_low = grad_self.astype(jnp.bfloat16)
    self_output_grad = mat_grad(self_mixed, self_low)
    self_up = apply_back(self_low, b_output).astype(jnp.bfloat16)
    query_low, key_low, value_low = attend_back(queries, keys, values, allowed, self_lse, self_up)
    self_query_grad = mat_grad(first, query_low)
    self_key_grad = mat_grad(first, key_low)
    self_value_grad = mat_grad(first, value_low)
    first_up = (
        apply_back(query_low, b_query) + apply_back(key_low, b_key) + apply_back(value_low, b_value)
    )
    text_input, first_gain_grad, first_shift_grad = norm_back(
        residual, first_gain, first_shift, first_up
    )
    text_grad = (grad_self + text_input).astype(jnp.bfloat16)
    weight_sums = reduce_all(
        (
            self_query_grad,
            self_key_grad,
            self_value_grad,
            self_output_grad,
            cross_query_grad,
            cross_key_grad,
            cross_value_grad,
            cross_output_grad,
            hidden_in_grad,
            hidden_out_grad,
        )
    )
    norm_sums = lax.psum(
        (
            first_gain_grad,
            first_shift_grad,
            second_gain_grad,
            second_shift_grad,
            third_gain_grad,
            third_shift_grad,
        ),
        ("dp", "mem"),
    )
    return (
        layer_out,
        text_grad,
        memory_grad,
        weight_sums[0],
        weight_sums[1],
        weight_sums[2],
        weight_sums[3],
        weight_sums[4],
        weight_sums[5],
        weight_sums[6],
        weight_sums[7],
        weight_sums[8],
        weight_sums[9],
        norm_sums[0],
        norm_sums[1],
        norm_sums[2],
        norm_sums[3],
        norm_sums[4],
        norm_sums[5],
    )


class Place:
    def __init__(self):
        self.d = lax.axis_index("dp")
        self.m = lax.axis_index("mem")
        self.c = lax.rem(self.d, 2)
        self.x = lax.div(self.d, 2)
        self.y = lax.rem(self.m, 2)
        self.z = lax.div(self.m, 2)
        self.oc, self.ox, self.oy = 1 - self.c, 1 - self.x, 1 - self.y
        self.sib = (self.x * 2 + self.oc, self.m)
        self.xn = (self.ox * 2 + self.c, self.m)
        self.yn = (self.d, self.z * 2 + self.oy)
        self.xyn = (self.ox * 2 + self.c, self.z * 2 + self.oy)

        self.side = lax.div(self.z, 2)
        self.inner = lax.rem(lax.div(self.z + 1, 2), 2) == 1
        self.flip = self.z + 1 - 2 * lax.rem(self.z, 2)
        self.ours, self.theirs = pl.ds(2 * self.side, 2), pl.ds(2 - 2 * self.side, 2)
        self.flip_peer = (self.d, self.flip * 2 + self.y)
        self.across = (self.d, (3 - self.z) * 2 + self.y)

    def zpeer(self, k):
        return (self.d, lax.rem(self.z + k, 4) * 2 + self.y)

    def mpeer(self, k):
        return (self.d, lax.rem(self.m + k, 8))


def greet(at):
    barrier = pltpu.get_barrier_semaphore()
    peers = [at.sib, at.xn, at.xyn] + [at.mpeer(k) for k in range(1, 8)]
    for peer in peers:
        pl.semaphore_signal(barrier, inc=1, device_id=peer, device_id_type=MESH)
    pl.semaphore_wait(barrier, len(peers))


def remote(src, dst, send, recv, peer):
    return pltpu.make_async_remote_copy(
        src_ref=src,
        dst_ref=dst,
        send_sem=send,
        recv_sem=recv,
        device_id=peer,
        device_id_type=MESH,
    )


class Gather:
    SENDS, RECVS = 4, 7

    def __init__(self, at, full, span, via_y, sends, recvs, index):
        self.at, self.full, self.span = at, full, span
        self.sends = [sends.at[self.SENDS * index + i] for i in range(self.SENDS)]
        self.recvs = [recvs.at[self.RECVS * index + i] for i in range(self.RECVS)]
        self.lanes = full.shape[-1] // 2
        self.cuts = ((0, via_y), (via_y, self.lanes - via_y))

    def piece(self, z, y, h, x, cut=None):
        start, size = cut or (0, self.lanes)
        lo = pl.multiple_of(x * self.lanes + start, 128)
        return self.full.at[self.span, z, y, h, :, pl.ds(lo, size)]

    def send(self, kind, slot, ref, peer):
        remote(ref, ref, self.sends[kind], self.recvs[slot], peer).start()

    def got(self, slot, ref):
        remote(ref, ref, self.sends[0], self.recvs[slot], self.at.sib).wait_recv()

    def sent(self, kind, ref):
        remote(ref, ref, self.sends[kind], self.recvs[0], self.at.sib).wait_send()

    def line(self, z):
        return self.piece(z, self.at.y, self.at.c, self.at.x)

    def begin(self):
        at = self.at
        own = self.line(at.z)
        self.send(2, 0, own, at.flip_peer)
        self.send(1, 2, own, at.xn)
        self.send(1, 3, own, at.yn)
        self.send(0, 6, own, at.sib)

    def spread(self, ref):
        at = self.at
        self.send(1, 2, ref, at.xn)
        self.send(1, 3, ref, at.yn)
        self.send(0, 6, ref, at.sib)

    def second(self, k):
        at = self.at
        if k == 1:
            self.got(0, self.line(at.flip))
            pl.when(at.inner)(lambda: self.send(3, 1, self.line(at.ours), at.across))
            self.spread(self.line(at.flip))
        elif k == 2:

            @pl.when(at.inner)
            def _():
                self.got(1, self.line(at.theirs))
                self.send(3, 1, self.line(at.theirs), at.flip_peer)
        else:
            pl.when(~at.inner)(lambda: self.got(1, self.line(at.theirs)))
            self.spread(self.line(at.theirs))

    def third(self, part):
        at, every = self.at, slice(None)
        x, y, peer = ((at.ox, at.y, at.yn), (at.x, at.oy, at.xn))[part]
        ref = self.piece(every, y, at.c, x)
        self.got(2 + part, ref)
        self.send(1, 4 + part, self.piece(every, y, at.c, x, self.cuts[part]), peer)
        self.send(0, 6, ref, at.sib)

    def fourth(self):
        at = self.at
        for part, cut in enumerate(self.cuts):
            ref = self.piece(slice(None), at.oy, at.c, at.ox, cut)
            self.got(4 + part, ref)
            self.send(0, 6, ref, at.sib)

    def last(self):
        self.got(6, self.full.at[self.span, :, :, self.at.oc])

    def drain(self):
        at = self.at
        self.sent(0, self.full.at[self.span, :, :, at.c])
        self.sent(1, self.full.at[self.span, pl.ds(0, 3), :, at.c])
        self.sent(2, self.line(at.z))
        pl.when(at.inner)(lambda: self.sent(3, self.line(slice(None))))


class GatherLast(Gather):
    def block(self, z):
        return self.full.at[self.span, z, :, self.at.c]

    def begin(self):
        self.spread(self.line(self.at.z))

    def third(self, part):
        at = self.at
        x, y, peer = ((at.ox, at.y, at.yn), (at.x, at.oy, at.xn))[part]
        ref = self.piece(at.z, y, at.c, x)
        self.got(2 + part, ref)
        self.send(1, 4 + part, self.piece(at.z, y, at.c, x, self.cuts[part]), peer)
        self.send(0, 6, ref, at.sib)

    def fourth(self):
        at = self.at
        for part, cut in enumerate(self.cuts):
            ref = self.piece(at.z, at.oy, at.c, at.ox, cut)
            self.got(4 + part, ref)
            self.send(0, 6, ref, at.sib)
        self.send(2, 0, self.block(at.z), at.flip_peer)

    def second(self, k):
        at = self.at
        if k == 1:
            ref = self.block(at.flip)
            self.got(0, ref)
            pl.when(at.inner)(lambda: self.send(3, 1, self.block(at.ours), at.across))
            self.send(0, 6, ref, at.sib)
        elif k == 2:

            @pl.when(at.inner)
            def _():
                self.got(1, self.block(at.theirs))
                self.send(3, 1, self.block(at.theirs), at.flip_peer)
        else:
            pl.when(~at.inner)(lambda: self.got(1, self.block(at.theirs)))
            self.send(0, 6, self.block(at.theirs), at.sib)

    def drain(self):
        at = self.at
        self.sent(0, self.full.at[self.span, :, :, at.c])
        self.sent(1, self.line(pl.ds(0, 3)))
        self.sent(2, self.block(at.z))
        pl.when(at.inner)(lambda: self.sent(3, self.full.at[self.span, :, :, at.c]))


class Reduce:
    RECVS = 9

    def __init__(self, at, full, span, bufs, sends, recvs, index):
        self.at, self.full, self.span = at, full, span
        (self.chip, self.via_y, self.via_x, self.rx, self.ry) = bufs[:5]
        (self.outer, self.middle, self.pair, self.fin) = bufs[5:]
        self.sends = sends.at[index]
        self.recvs = [recvs.at[self.RECVS * index + i] for i in range(self.RECVS)]
        self.count, self.lanes = self.chip.shape[0], full.shape[-1] // 2
        cut = self.via_y.shape[-1]
        self.cuts = (slice(0, cut), slice(cut, self.lanes))

    def send(self, slot, src, dst, peer):
        remote(src, dst, self.sends, self.recvs[slot], peer).start()

    def got(self, slot, ref):
        remote(ref, ref, self.sends, self.recvs[slot], self.at.sib).wait_recv()

    def begin(self):
        at = self.at
        for x in range(2):
            lanes = slice(x * self.lanes, (x + 1) * self.lanes)
            src = self.full.at[self.span, :, :, at.oc, :, lanes]
            self.send(0, src, self.chip.at[:, x], at.sib)

    def add_cores(self):
        at = self.at
        chip, full, lanes, w0 = self.chip, self.full, self.lanes, self.span.start
        self.got(0, chip)

        def add(i, carry):
            w, r = lax.div(i, 8), lax.rem(i, 8)
            z, y = lax.div(r, 2), lax.rem(r, 2)
            for x in range(2):
                mine = full[w0 + w, z, y, at.c, :, x * lanes : (x + 1) * lanes]
                chip[w, x, z, y] = (
                    chip[w, x, z, y].astype(F32) + mine.astype(F32)
                ).astype(BF)
            return carry

        lax.fori_loop(0, 8 * self.count, add, 0)

    def second(self):
        at, chip = self.at, self.chip
        self.add_cores()
        self.send(1, chip.at[:, at.ox, :, at.oy, :, self.cuts[0]], self.via_y, at.yn)
        self.send(2, chip.at[:, at.ox, :, at.oy, :, self.cuts[1]], self.via_x, at.xn)

    def third(self, part):
        at, chip = self.at, self.chip
        ref = (self.via_y, self.via_x)[part]
        x, y = ((at.ox, at.y), (at.x, at.oy))[part]
        cut = self.cuts[part]
        self.got(1 + part, ref)

        def add(i, carry):
            w, z = lax.div(i, 4), lax.rem(i, 4)
            chip[w, x, z, y, :, cut] = (
                chip[w, x, z, y, :, cut].astype(F32) + ref[w, z].astype(F32)
            ).astype(BF)
            return carry

        lax.fori_loop(0, 4 * self.count, add, 0)
        box, peer = ((self.rx, at.xn), (self.ry, at.yn))[part]
        self.send(3 + part, chip.at[:, x, :, y], box, peer)

    def fourth(self):
        at, chip = self.at, self.chip
        self.got(3, self.rx)
        self.got(4, self.ry)

        def add(i, carry):
            w, z = lax.div(i, 4), lax.rem(i, 4)
            chip[w, at.x, z, at.y] = (
                chip[w, at.x, z, at.y].astype(F32)
                + self.rx[w, z].astype(F32)
                + self.ry[w, z].astype(F32)
            ).astype(BF)
            return carry

        lax.fori_loop(0, 4 * self.count, add, 0)
        self.inward()

    def line(self, z):
        return self.chip.at[:, self.at.x, z, self.at.y]

    def inward(self):
        at = self.at
        pl.when(~at.inner)(
            lambda: self.send(5, self.line(at.theirs), self.outer, at.flip_peer)
        )

    def add_line(self, start, ref):
        at, chip = self.at, self.chip

        def add(i, carry):
            w, z = lax.div(i, 2), lax.rem(i, 2)
            chip[w, at.x, start + z, at.y] = (
                chip[w, at.x, start + z, at.y].astype(F32) + ref[w, z].astype(F32)
            ).astype(BF)
            return carry

        lax.fori_loop(0, 2 * self.count, add, 0)

    def relay(self, stage):
        at = self.at
        if stage == 0:

            @pl.when(at.inner)
            def _():
                self.got(5, self.outer)
                self.add_line(2 - 2 * at.side, self.outer)
                self.send(6, self.line(at.theirs), self.middle, at.across)

            return

        @pl.when(at.inner)
        def _():
            self.got(6, self.middle)
            self.add_line(2 * at.side, self.middle)

        self.send(7, self.line(at.flip), self.pair, at.flip_peer)

    def finish(self, terms):
        at = self.at

        def add(w, carry):
            total = self.chip[w, at.x, at.z, at.y].astype(F32)
            for term in terms:
                total = total + term[w].astype(F32)
            self.fin[w, at.c] = total.astype(BF)
            return carry

        lax.fori_loop(0, self.count, add, 0)
        mine = self.fin.at[:, at.c]
        self.send(8, mine, mine, at.sib)

    def fifth(self):
        self.got(7, self.pair)
        self.finish([self.pair])

    def last(self):
        self.got(8, self.fin.at[:, self.at.oc])

    def drain(self):
        ref = self.full.at[self.span]
        remote(ref, ref, self.sends, self.recvs[0], self.at.sib).wait_send()


class ReduceFirst(Reduce):
    def line(self, z):
        return self.chip.at[:, :, z]

    def second(self):
        self.add_cores()
        self.inward()

    def add_line(self, start, ref, n=2):
        chip = self.chip

        def add(i, carry):
            w, r = lax.div(i, 4 * n), lax.rem(i, 4 * n)
            z, r = lax.div(r, 4), lax.rem(r, 4)
            x, y = lax.div(r, 2), lax.rem(r, 2)
            chip[w, x, start + z, y] = (
                chip[w, x, start + z, y].astype(F32) + ref[w, x, z, y].astype(F32)
            ).astype(BF)
            return carry

        lax.fori_loop(0, 4 * n * self.count, add, 0)

    def fourth(self):
        at, chip = self.at, self.chip
        self.got(7, self.pair)

        def add(i, carry):
            w, r = lax.div(i, 4), lax.rem(i, 4)
            x, y = lax.div(r, 2), lax.rem(r, 2)
            chip[w, x, at.z, y] = (
                chip[w, x, at.z, y].astype(F32) + self.pair[w, x, y].astype(F32)
            ).astype(BF)
            return carry

        lax.fori_loop(0, 4 * self.count, add, 0)
        self.send(1, chip.at[:, at.ox, at.z, at.oy, :, self.cuts[0]], self.via_y, at.yn)
        self.send(2, chip.at[:, at.ox, at.z, at.oy, :, self.cuts[1]], self.via_x, at.xn)

    def third(self, part):
        at, chip = self.at, self.chip
        ref = (self.via_y, self.via_x)[part]
        x, y = ((at.ox, at.y), (at.x, at.oy))[part]
        cut = self.cuts[part]
        self.got(1 + part, ref)

        def add(w, carry):
            chip[w, x, at.z, y, :, cut] = (
                chip[w, x, at.z, y, :, cut].astype(F32) + ref[w].astype(F32)
            ).astype(BF)
            return carry

        lax.fori_loop(0, self.count, add, 0)
        box, peer = ((self.rx, at.xn), (self.ry, at.yn))[part]
        self.send(3 + part, chip.at[:, x, at.z, y], box, peer)

    def fifth(self):
        self.got(3, self.rx)
        self.got(4, self.ry)
        self.finish([self.rx, self.ry])


def reduce_bufs(count, rows, lanes, cut, z_first):
    one, line, block = (rows, lanes), (4, rows, lanes), (2, 2, 2, rows, lanes)
    if z_first:
        shapes = [(rows, cut), (rows, lanes - cut), one, one, block, block, block[1:]]
    else:
        pair = (2, rows, lanes)
        shapes = [(4, rows, cut), (4, rows, lanes - cut), line, line, pair, pair, one]
    shapes = [(2, 4, 2, rows, lanes)] + shapes + [(2, rows, lanes)]
    return [pltpu.VMEM((count,) + shape, BF) for shape in shapes]


def pick(rows, cols, start):
    col = lax.broadcasted_iota(jnp.int32, (rows, cols), 1)
    row = lax.broadcasted_iota(jnp.int32, (rows, cols), 0)
    return jnp.where(col == row + start, 1.0, 0.0).astype(BF)


def dot_nt(a, b):
    return lax.dot_general(a, b, (((1,), (1,)), ((), ())), preferred_element_type=F32)


def dot_nn(a, b):
    return lax.dot_general(a, b, (((1,), (0,)), ((), ())), preferred_element_type=F32)


def dot_tn(a, b):
    return lax.dot_general(a, b, (((0,), (0,)), ((), ())), preferred_element_type=F32)


def norm_stats(values):
    center = values - jnp.mean(values, axis=-1, keepdims=True)
    scale = lax.rsqrt(jnp.mean(center * center, axis=-1, keepdims=True) + EPS)
    return center * scale, scale


def gelu_both(value):
    c0, c1 = 0.7978845608028654, 0.044715
    square = value * value
    tanh = jnp.tanh(c0 * value * (1.0 + c1 * square))
    half = 0.5 + 0.5 * tanh
    slope = half + 0.5 * value * (1.0 - tanh * tanh) * (c0 + 3.0 * c0 * c1 * square)
    return value * half, slope


def softmax(scores):
    powered = jnp.exp(scores - jnp.max(scores, axis=-1, keepdims=True))
    return powered / jnp.sum(powered, axis=-1, keepdims=True)


class Layer:
    def __init__(self, **refs):
        self.__dict__.update(refs)
        self.tokens, self.dmodel = self.nrm.shape
        self.images = self.own_images
        self.txt = self.tokens // self.images
        self.mem_len = self.mkv.shape[1] // self.images
        lane = lax.broadcasted_iota(jnp.int32, (1, 4 * HEAD), 1)
        self.head_lanes = [
            jnp.where((lane >= HEAD * h) & (lane < HEAD * (h + 1)), 1.0, 0.0)
            for h in range(4)
        ]

    def weight(self, i):
        return self.full_s[i].reshape(self.dmodel, self.dmodel)

    def put_weight(self, i, value):
        self.full_s[i] = value.astype(BF).reshape(self.full_s.shape[1:])

    def blocks(self, size, fn, total=None):
        def step(i, carry):
            fn(pl.ds(pl.multiple_of(i * size, size), size))
            return carry

        lax.fori_loop(0, (total or self.tokens) // size, step, 0)

    def spread(self, value):
        return jnp.concatenate(
            [value * mask.astype(BF) for mask in self.head_lanes], axis=0
        )

    def gather_heads(self, value):
        n = value.shape[0] // 4
        out = value[:n] * self.head_lanes[0]
        for h in range(1, 4):
            out = out + value[h * n : (h + 1) * n] * self.head_lanes[h]
        return out

    def norm_into(self, source, index):
        gain, shift = self.norms[2 * index : 2 * index + 1], self.norms[2 * index + 1 : 2 * index + 2]

        def block(rows):
            hat, _ = norm_stats(source[rows, :].astype(F32))
            self.nrm[rows, :] = (hat * gain + shift).astype(BF)

        self.blocks(128, block)

    def norm_back(self, source, upstream, index, finish):
        gain = self.norms[2 * index : 2 * index + 1]

        def step(i, carry):
            rows = pl.ds(pl.multiple_of(i * 64, 64), 64)
            hat, scale = norm_stats(source[rows, :].astype(F32))
            up = upstream[rows, :]
            scaled = up * gain
            first = jnp.mean(scaled, axis=-1, keepdims=True)
            second = jnp.mean(scaled * hat, axis=-1, keepdims=True)
            finish(rows, scale * (scaled - first - hat * second))
            gains, shifts = carry
            return (
                gains + jnp.sum(up * hat, axis=0, keepdims=True),
                shifts + jnp.sum(up, axis=0, keepdims=True),
            )

        zero = jnp.zeros((1, self.dmodel), F32)
        gains, shifts = lax.fori_loop(0, self.tokens // 64, step, (zero, zero))
        self.norm_grads[2 * index : 2 * index + 1, :] = gains
        self.norm_grads[2 * index + 1 : 2 * index + 2, :] = shifts


    def project(self, outs, value, first):
        def step(i, carry):
            outs[i] = dot_nt(value(), self.weight(first + i)).astype(BF)
            return carry

        lax.fori_loop(0, outs.shape[0], step, 0)

    def allowed(self, p):
        n = 2 * self.txt
        row = lax.broadcasted_iota(jnp.int32, (n, n), 0)
        col = lax.broadcasted_iota(jnp.int32, (n, n), 1)
        late = col >= self.txt
        length = jnp.where(
            late, self.txt + self.lengths[2 * p + 1], self.lengths[2 * p]
        )
        return (col <= row) & (col < length) & (late == (row >= self.txt))

    def self_forward(self, start, stop):
        def pair(p, carry):
            rows = pl.ds(pl.multiple_of(p * 128, 128), 128)
            allow = self.allowed(p)
            for g in range(self.dmodel // 256):
                cols = slice(256 * g, 256 * g + 256)
                scores = dot_nt(self.spread(self.qkv[0, rows, cols]), self.qkv[1, rows, cols])
                scores = scores.reshape(4, 128, 128) * HEAD**-0.5
                scores = jnp.where(allow[None], scores, NEG)
                probs = softmax(scores).reshape(512, 128).astype(BF)
                self.ps[p, g] = probs
                mixed = dot_nn(probs, self.qkv[2, rows, cols])
                self.sm[rows, cols] = self.gather_heads(mixed).astype(BF)
            return carry

        lax.fori_loop(start, stop, pair, 0)

    def add_after_self(self):
        def block(rows):
            self.after_self[rows, :] = self.io[rows, :].astype(F32) + dot_nt(
                self.sm[rows, :], self.weight(3)
            )

        self.blocks(256, block)

    def memory_in(self):
        n, size = self.images, self.mem_len
        total = n * size

        def block(i, carry):
            row = lax.broadcasted_iota(jnp.int32, (size, total), 0)
            col = lax.broadcasted_iota(jnp.int32, (size, total), 1)
            hot = jnp.where(col == n * row + i, 1.0, 0.0).astype(BF)
            rows = pl.ds(pl.multiple_of(i * size, 32), size)
            self.mkv[0, rows, :] = dot_nn(hot, self.memory()).astype(BF)
            return carry

        lax.fori_loop(0, n, block, 0)
        self.rows[...] = self.mkv[0].reshape(self.rows.shape)

    def memory(self):
        return self.rows[...].reshape(self.mkv.shape[1:])

    def memory_out(self):
        n, size = self.images, self.mem_len
        short, total = size // n, n * size

        def block(b, carry):
            row = lax.broadcasted_iota(jnp.int32, (size, total), 0)
            col = lax.broadcasted_iota(jnp.int32, (size, total), 1)
            image = row & (n - 1)
            slot = lax.shift_right_logical(row, n.bit_length() - 1) + b * short
            hot = jnp.where(col == image * size + slot, 1.0, 0.0).astype(BF)
            low, high = self.cm[...], self.t2[: total - self.tokens, : self.dmodel]
            back = dot_nn(hot[:, : self.tokens], low) + dot_nn(hot[:, self.tokens :], high)
            self.rows[b] = back.astype(BF).reshape(self.rows.shape[1:])
            return carry

        lax.fori_loop(0, n, block, 0)

    def probs_at(self, i, g):
        size = 4 * self.txt
        start = pl.multiple_of(lax.rem(i, 2) * size, size)
        return lax.div(i, 2), g, pl.ds(start, size), slice(0, self.mem_len)

    def cross_forward(self, start, stop):
        def image(i, carry):
            rows = pl.ds(pl.multiple_of(i * self.txt, 64), self.txt)
            mems = pl.ds(pl.multiple_of(i * self.mem_len, 32), self.mem_len)
            for g in range(self.dmodel // 256):
                cols = slice(256 * g, 256 * g + 256)
                scores = dot_nt(self.spread(self.cq[0, rows, cols]), self.mkv[0, mems, cols])
                probs = softmax(scores * HEAD**-0.5).astype(BF)
                self.ps[self.probs_at(i, g)] = probs
                mixed = dot_nn(probs, self.mkv[1, mems, cols])
                self.cm[rows, cols] = self.gather_heads(mixed).astype(BF)
            return carry

        lax.fori_loop(start, stop, image, 0)

    def add_after_cross(self):
        def block(rows):
            self.after_cross[rows, :] = self.after_self[rows, :] + dot_nt(
                self.cm[rows, :], self.weight(7)
            )

        self.blocks(256, block)


    def mask_top(self):
        def block(rows):
            self.io[rows, :] = self.io[rows, :] * self.valid[rows, :1]

        self.blocks(128, block)

    def feed_start(self):
        def block(rows):
            self.acc_out[rows, :] = self.after_cross[rows, :]
            self.acc_up[rows, :] = jnp.zeros((128, self.dmodel), F32)

        self.blocks(128, block)

    def feed_chunk(self, s):
        dmodel = self.dmodel
        units = self.t2.shape[1]

        def w_in(lo=0, n=units):
            return self.full_in[s].reshape(units, dmodel)[lo : lo + n]

        def w_out(lo=0, n=units):
            return self.full_out[s, :, :, :, :, lo : lo + n].reshape(dmodel, n)

        def block(rows):
            for lo in range(0, units, 512):
                before = dot_nt(self.nrm[rows, :], w_in(lo, 512))
                act, slope = gelu_both(before)
                self.t2[rows, lo : lo + 512] = act.astype(BF)
                up = dot_nn(self.io[rows, :], w_out(lo, 512))
                self.t3[rows, lo : lo + 512] = (slope * up).astype(BF)

        self.blocks(256, block)

        def block(rows):
            self.acc_out[rows, :] += dot_nt(self.t2[rows, :], w_out())
            self.acc_up[rows, :] += dot_nn(self.t3[rows, :], w_in())

        self.blocks(256, block)
        shape = self.full_out.shape[1:5]
        for lo in range(0, units, 512):
            grad = dot_tn(self.io[...], self.t2[:, lo : lo + 512]).astype(BF)
            self.full_out[s, :, :, :, :, lo : lo + 512] = grad.reshape(shape + (512,))
        grad = dot_tn(self.t3[...], self.nrm[...]).astype(BF)
        self.full_in[s] = grad.reshape(self.full_in.shape[1:])

    def layer_out(self, out):
        def block(rows):
            out[rows, : self.dmodel] = (self.acc_out[rows, :] * self.valid[rows, :1].astype(F32)).astype(BF)

        self.blocks(128, block)


    def third_back(self):
        def finish(rows, grad):
            total = self.io[rows, :].astype(F32) + grad
            self.acc_up[rows, :] = total
            self.io[rows, :] = total.astype(BF)

        self.norm_back(self.after_cross, self.acc_up, 2, finish)

    def output_back(self, i, mixed, out):
        out[:, : self.dmodel] = dot_nn(self.io[...], self.weight(i)).astype(BF)
        self.put_weight(i, dot_tn(self.io[...], mixed[...]))

    def attend_back(self, probs, up, q, k, v, rows, mems, cols):
        low_q = self.spread(q[rows, cols])
        low_up = self.spread(up[rows, cols])
        keys, values = k[mems, cols], v[mems, cols]
        full = probs.astype(F32)
        prob_grad = dot_nt(low_up, values)
        score = full * (prob_grad - jnp.sum(prob_grad * full, axis=-1, keepdims=True))
        score = (score * HEAD**-0.5).astype(BF)
        v[mems, cols] = dot_tn(probs, low_up).astype(BF)
        k[mems, cols] = dot_tn(score, low_q).astype(BF)
        q[rows, cols] = self.gather_heads(dot_nn(score, keys)).astype(BF)

    def cross_back(self, start, stop):
        def image(i, carry):
            rows = pl.ds(pl.multiple_of(i * self.txt, 64), self.txt)
            mems = pl.ds(pl.multiple_of(i * self.mem_len, 32), self.mem_len)
            for g in range(self.dmodel // 256):
                cols = slice(256 * g, 256 * g + 256)
                probs = self.ps[self.probs_at(i, g)]
                self.attend_back(
                    probs,
                    self.t2,
                    self.cq.at[0],
                    self.mkv.at[0],
                    self.mkv.at[1],
                    rows,
                    mems,
                    cols,
                )
            return carry

        lax.fori_loop(start, stop, image, 0)

    def self_back(self, start, stop):
        def pair(p, carry):
            rows = pl.ds(pl.multiple_of(p * 128, 128), 128)
            for g in range(self.dmodel // 256):
                cols = slice(256 * g, 256 * g + 256)
                self.attend_back(
                    self.ps[p, g],
                    self.t2,
                    self.qkv.at[0],
                    self.qkv.at[1],
                    self.qkv.at[2],
                    rows,
                    rows,
                    cols,
                )
            return carry

        lax.fori_loop(start, stop, pair, 0)

    def memory_back(self):
        size = 256
        keys, values = self.mkv.at[0], self.mkv.at[1]

        def back(rows):
            total = dot_nn(keys[rows, :], self.weight(5)) + dot_nn(
                values[rows, :], self.weight(6)
            )
            return total.astype(BF)

        def block(rows):
            self.cm[rows, :] = back(rows)

        self.blocks(size, block)
        for start in range(self.tokens, self.mkv.shape[1], size):
            there = slice(start - self.tokens, start - self.tokens + size)
            self.t2[there, : self.dmodel] = back(slice(start, start + size))

    def weight_grads(self, lows, value, first):
        def step(i, carry):
            self.put_weight(first + i, dot_tn(lows[i], value()))
            return carry

        lax.fori_loop(0, lows.shape[0], step, 0)

    def second_up(self):
        def block(rows):
            self.acc_out[rows, :] = dot_nn(self.cq[0, rows, :], self.weight(4))

        self.blocks(256, block)

    def second_back(self):
        def finish(rows, grad):
            total = self.acc_up[rows, :] + grad
            self.acc_up[rows, :] = total
            self.io[rows, :] = total.astype(BF)

        self.norm_back(self.after_self, self.acc_out, 1, finish)

    def first_up(self):
        def block(rows):
            self.acc_out[rows, :] = (
                dot_nn(self.qkv[0, rows, :], self.weight(0))
                + dot_nn(self.qkv[1, rows, :], self.weight(1))
                + dot_nn(self.qkv[2, rows, :], self.weight(2))
            )

        self.blocks(256, block)

    def first_back(self, text, out):
        def finish(rows, grad):
            out[rows, : self.dmodel] = (self.acc_up[rows, :] + grad).astype(BF)

        self.norm_back(text, self.acc_out, 0, finish)


class NormSum:
    def __init__(self, at, sums, pair, plane, line, out, sends, recvs):
        self.at, self.sums, self.pair = at, sums, pair
        self.boxes = (plane, line)
        self.sends, self.recvs = sends, recvs
        self.me = (at.x * 2 + at.y, at.z)
        self.target = (line.at[at.z], out)
        self.peers = ((at.xn, at.yn, at.xyn), tuple(at.zpeer(k) for k in (1, 2, 3)))
        self.out = []

    def start(self, stage):
        if stage == 0:
            copy = remote(
                self.sums, self.pair, self.sends.at[0], self.recvs.at[0], self.at.sib
            )
            copy.start()
            self.out.append(copy)
            return
        box = self.boxes[stage - 1].at[self.me[stage - 1]]
        for k, peer in enumerate(self.peers[stage - 1]):
            i = 3 * stage - 2 + k
            copy = remote(box, box, self.sends.at[i], self.recvs.at[i], peer)
            copy.start()
            self.out.append(copy)

    def finish(self, stage):
        if stage == 0:
            self.out[0].wait_recv()
            self.boxes[0][self.me[0]] = self.sums[...] + self.pair[...]
            return
        for copy in self.out[3 * stage - 2 : 3 * stage + 1]:
            copy.wait_recv()
        box = self.boxes[stage - 1]
        total = box[0] + box[1] + box[2] + box[3]
        self.target[stage - 1][...] = total


SMALL = ((0, 2), (2, 3), (3, 5), (5, 7), (7, 8))
SMALL_BACK = ((7, 8), (4, 5), (3, 4), (0, 3), (5, 7))
THIRDS = 3
Z_LAST = (4, 9)
Z_FIRST_BACK = (0, 6)
NAMES = ("nrm", "io", "sm", "cm")
WIDE = ("after_self", "after_cross", "acc_out", "acc_up")


def whole_kernel(own_images, *refs):
    refs = list(refs)

    def take(n):
        out = refs[:n]
        del refs[:n]
        return out

    shards, (rows_in, text_in, top_in, lengths), vectors = take(10), take(4), take(6)
    fins, (layer_out, text_out, rows_out, norm_out, spill) = take(3), take(5)
    full_s, full_in, full_out, pair_s, pair_in, pair_out = take(6)
    bufs = [take(9) for _ in range(2 * THIRDS + len(SMALL_BACK))]
    narrow, wide = take(len(NAMES)), take(len(WIDE))
    qkv, cq, mkv, t2, t3, rows, ps, valid, norms = take(9)
    norm_sums, norm_pair, norm_plane, norm_line = take(4)
    (psend, precv, gsend, grecv, hsend, hrecv, rsend, rrecv, bsend, brecv, nsend, nrecv, local) = refs
    at = Place()
    greet(at)
    layer = Layer(
        own_images=own_images,
        full_s=full_s,
        full_in=full_in,
        full_out=full_out,
        rows=rows,
        qkv=qkv,
        cq=cq,
        mkv=mkv,
        ps=ps,
        t2=t2,
        t3=t3,
        lengths=lengths,
        valid=valid,
        norms=norms,
        norm_grads=norm_sums,
        **dict(zip(NAMES, narrow)),
        **dict(zip(WIDE, wide)),
    )
    half, dmodel = full_s.shape[4:]
    lanes, half_in, lanes_out = dmodel // 2, full_in.shape[4], full_out.shape[5] // 2

    pairs = [pair_s.at[i] for i in range(8)] + [pair_in]
    own, other = [], []
    for i in range(9):
        depth = shards[i].shape[0]
        mine = pairs[i].at[pl.ds(pl.multiple_of(at.c * depth, 8), depth), :]
        other.append(remote(shards[i], mine, psend.at[i], precv.at[i], at.sib))
        own.append(pltpu.make_async_copy(shards[i], mine, local.at[i]))
    for core, peer in ((at.c, None), (at.oc, at.sib)):
        src = shards[9].at[pl.ds(pl.multiple_of(core * half, 16), half), :]
        if peer is None:
            own.append(pltpu.make_async_copy(src, pair_out.at[at.c], local.at[9]))
        else:
            other.append(remote(src, pair_out.at[at.c], psend.at[9], precv.at[9], peer))
    for a, b in zip(other, own):
        a.start()
        b.start()
    load = pltpu.make_async_copy(text_in, layer.io, local.at[10])
    load.start()

    def ready(i):
        own[i].wait()
        if i < 9:
            depth = shards[i].shape[0]
            theirs = pairs[i].at[pl.ds(pl.multiple_of(at.oc * depth, 8), depth), :]
        else:
            theirs = pair_out.at[at.oc]
        remote(theirs, theirs, psend.at[i], precv.at[i], at.sib).wait_recv()

    x_lanes = pl.ds(pl.multiple_of(at.x * lanes, 128), lanes)

    def lay_small(w):
        ready(w)
        block = dot_nt(pick(half, 2 * half, at.c * half), pair_s[w])
        full_s[w, at.z, at.y, at.c, :, x_lanes] = block.astype(BF)

    def lay_third(s, part):
        if part == 0:
            start = 2 * half_in * s + at.c * half_in
            block = dot_nt(pick(half_in, pair_in.shape[1], start), pair_in[...])
            full_in[s, at.z, at.y, at.c, :, x_lanes] = block.astype(BF)
            return
        for b in range(4):
            lo = pl.multiple_of(at.x * lanes_out + 128 * b, 128)
            cut = (b % 2) * (128 * THIRDS) + 128 * s
            full_out[s, at.z, at.y, at.c, :, pl.ds(lo, 128)] = pair_out[
                b // 2, :, cut : cut + 128
            ]

    def gather(full, span, via_y, n):
        form = GatherLast if n in Z_LAST else Gather
        return form(at, full, span, via_y, gsend, grecv, n)

    g_small = [
        gather(full_s, slice(*span), 128, g)
        for g, span in enumerate(SMALL)
    ]
    g_feed = []
    for s in range(THIRDS):
        index = len(SMALL) + 2 * s
        span = slice(s, s + 1)
        g_feed.append(
            (
                gather(full_in, span, 128, index),
                gather(full_out, span, 256, index + 1),
            )
        )

    def begin(group):
        for w in range(group.span.start, group.span.stop):
            lay_small(w)
        group.begin()

    arrived = []

    def begin_third(s, part):
        if part not in arrived:
            arrived.append(part)
            ready(8 + part)
        lay_third(s, part)
        g_feed[s][part].begin()

    here = pl.ds(pl.multiple_of(at.m * own_images, 8), own_images)
    keep = pltpu.make_async_copy(rows_in.at[:, here, :], rows.at[at.m], local.at[11])

    def begin_memory():
        for k in range(1, 8):
            to = lax.rem(at.m + k, 8) * own_images
            src = rows_in.at[:, pl.ds(pl.multiple_of(to, 8), own_images), :]
            remote(src, rows.at[at.m], rsend.at[0], rrecv.at[k - 1], at.mpeer(k)).start()
        keep.start()

    for i, vector in enumerate(vectors):
        norms[i : i + 1, :] = vector[...].reshape(1, dmodel)
    row = lax.broadcasted_iota(jnp.int32, valid.shape, 0)
    limit = jnp.zeros(valid.shape, jnp.int32)
    for i in range(own_images):
        first = i * layer.txt
        limit = jnp.where(row >= first, first + lengths[i], limit)
    valid[...] = jnp.where(row < limit, 1.0, 0.0).astype(BF)

    def each(groups, name):
        for group in groups:
            getattr(group, name)()

    seven = rows.at[pl.ds(0, 7)]

    def end_memory():
        keep.wait()
        for k in range(1, 8):
            ref = rows.at[lax.rem(at.m + 8 - k, 8)]
            remote(ref, ref, rsend.at[0], rrecv.at[k - 1], at.sib).wait_recv()

    def drain_small():
        for copy in other:
            copy.wait_send()
        remote(seven, seven, rsend.at[0], rrecv.at[0], at.sib).wait_send()
        each(g_small, "drain")

    def send_memory():
        for k in range(1, 8):
            src, dst = rows.at[lax.rem(at.m + k, 8)], rows_out.at[:, here, :]
            remote(src, dst, bsend.at[0], brecv.at[k - 1], at.mpeer(k)).start()
        keep_back.start()

    def move(src, dst, i):
        return pltpu.make_async_copy(src, dst, local.at[i])

    top, text = move(top_in, layer.io, 10), move(text_in, layer.sm, 10)
    away, again = move(ps, spill, 13), move(spill, ps, 13)
    packed = t3.at[:, 0:dmodel]
    save_out, save_text = move(packed, layer_out, 12), move(packed, text_out, 12)
    keep_back = move(rows.at[at.m], rows_out.at[:, here, :], 11)
    norm = NormSum(at, norm_sums, norm_pair, norm_plane, norm_line, norm_out, nsend, nrecv)
    fin_s, fin_in, fin_out = fins
    stores = []

    def store(group, out):
        group.last()
        copy = move(group.fin, out.at[group.span], 14 + len(stores))
        copy.start()
        stores.append(copy)

    def reduce(full, span, n):
        form = ReduceFirst if n in Z_FIRST_BACK else Reduce
        return form(at, full, span, bufs[n], hsend, hrecv, n)

    r_feed, r_small = [], []
    for s in range(THIRDS):
        span = slice(s, s + 1)
        r_feed.append(
            [
                reduce(full, span, 2 * s + i)
                for i, full in enumerate((full_in, full_out))
            ]
        )
    for g, span in enumerate(SMALL_BACK):
        n = 2 * THIRDS + g
        r_small.append(reduce(full_s, slice(*span), n))

    begin(g_small[1])
    begin(g_small[2])
    begin_third(0, 1)
    begin(g_small[0])
    g_small[1].second(1)
    begin_third(2, 1)
    begin_third(2, 0)
    begin(g_small[4])
    begin_third(0, 0)
    g_small[2].second(1)
    begin(g_small[3])
    g_small[0].second(1)
    g_small[1].second(2)
    g_small[2].second(2)
    g_small[3].second(1)
    g_small[4].third(0)
    load.wait()
    layer.norm_into(layer.io, 0)
    g_small[4].third(1)
    g_small[0].second(2)
    g_feed[2][1].second(1)
    g_small[1].second(3)
    g_feed[0][0].second(1)
    g_feed[0][1].second(1)
    begin_third(1, 0)
    begin_third(1, 1)
    g_small[3].second(2)
    g_small[0].second(3)
    g_feed[0][0].second(2)
    g_feed[1][1].second(1)
    begin_memory()
    g_small[1].third(1)
    g_small[2].second(3)
    g_small[1].third(0)
    g_small[3].second(3)
    g_small[0].third(1)
    g_small[0].third(0)
    g_feed[2][0].third(0)
    g_small[4].fourth()
    g_small[2].third(1)
    g_small[2].third(0)
    g_feed[0][1].second(2)
    g_feed[0][0].second(3)
    g_small[3].third(0)
    g_small[0].fourth()
    g_feed[2][0].third(1)
    g_small[1].fourth()
    g_small[3].third(1)
    g_small[0].last()
    g_small[1].last()
    g_feed[1][0].second(1)
    g_feed[1][1].second(2)
    layer.project(layer.qkv, lambda: layer.nrm[...], 0)
    g_feed[0][1].second(3)
    g_feed[2][0].fourth()
    g_small[4].second(1)
    layer.self_forward(0, 2)
    g_small[2].fourth()
    g_feed[1][0].second(2)
    layer.self_forward(2, 4)
    away.start()
    g_feed[0][0].third(1)
    g_small[2].last()
    layer.add_after_self()
    top.start()
    g_feed[2][0].second(1)
    g_feed[2][1].second(2)
    layer.norm_into(layer.after_self, 1)
    layer.project(layer.cq, lambda: layer.nrm[...], 4)
    g_feed[1][0].second(3)
    g_feed[1][1].second(3)
    g_feed[0][1].third(0)
    g_small[3].fourth()
    g_small[4].second(2)
    end_memory()
    layer.memory_in()
    g_small[3].last()
    g_feed[2][1].second(3)
    g_feed[0][0].third(0)
    layer.project(layer.mkv, layer.memory, 5)
    g_feed[0][1].third(1)
    away.wait()
    layer.cross_forward(0, 4)
    g_feed[2][0].second(2)
    g_feed[1][0].third(0)
    g_feed[1][0].third(1)
    g_small[4].second(3)
    g_feed[1][1].third(1)
    g_feed[1][1].third(0)
    layer.cross_forward(4, 8)
    g_small[4].last()
    g_feed[0][1].fourth()
    layer.add_after_cross()
    g_feed[0][0].fourth()
    g_feed[2][1].third(1)
    layer.norm_into(layer.after_cross, 2)
    top.wait()
    layer.mask_top()
    layer.feed_start()
    drain_small()
    g_feed[0][1].last()
    g_feed[2][1].third(0)
    g_feed[0][0].last()
    g_feed[1][0].fourth()
    g_feed[1][1].fourth()
    each(g_feed[0], "drain")
    layer.feed_chunk(0)
    g_feed[2][0].second(3)
    g_feed[1][1].last()
    g_feed[2][1].fourth()
    r_feed[0][1].begin()
    g_feed[1][0].last()
    each(g_feed[1], "drain")
    layer.feed_chunk(1)
    g_feed[2][0].last()
    r_feed[0][1].second()
    r_feed[1][1].begin()
    r_feed[1][0].begin()
    g_feed[2][1].last()
    each(g_feed[2], "drain")
    layer.feed_chunk(2)
    r_feed[1][1].second()
    r_feed[2][1].begin()
    r_feed[0][1].third(1)
    r_feed[1][0].second()
    layer.third_back()
    layer.output_back(7, layer.cm, t2)
    r_feed[2][1].second()
    r_feed[2][0].begin()
    r_small[0].begin()
    layer.cross_back(0, 4)
    r_feed[2][0].second()
    r_feed[1][1].third(1)
    r_small[0].second()
    r_feed[1][0].third(1)
    r_feed[1][1].third(0)
    r_feed[0][1].third(0)
    r_feed[0][0].begin()
    layer.cross_back(4, 8)
    again.start()
    layer.memory_back()
    layer.weight_grads(layer.mkv, layer.memory, 5)
    r_feed[0][0].second()
    r_feed[2][1].third(1)
    r_small[4].begin()
    r_small[0].relay(0)
    r_feed[1][0].third(0)
    layer.memory_out()
    layer.layer_out(t3)
    save_out.start()
    layer.second_up()
    r_feed[2][1].third(0)
    r_small[4].second()
    r_feed[2][0].third(1)
    layer.second_back()
    send_memory()
    layer.output_back(3, layer.sm, t2)
    text.start()
    layer.norm_into(layer.after_self, 1)
    layer.weight_grads(layer.cq, lambda: layer.nrm[...], 4)
    r_feed[1][1].fourth()
    r_feed[0][1].fourth()
    r_small[2].begin()
    again.wait()
    layer.self_back(0, 2)
    r_small[4].third(0)
    r_small[1].begin()
    layer.self_back(2, 4)
    r_small[4].third(1)
    r_feed[2][1].fourth()
    text.wait()
    layer.norm_into(layer.sm, 0)
    layer.first_up()
    r_feed[2][0].third(0)
    layer.weight_grads(layer.qkv, lambda: layer.nrm[...], 0)
    r_small[1].second()
    r_small[3].begin()
    r_small[2].second()
    r_feed[0][0].relay(0)
    r_small[3].second()
    save_out.wait()
    layer.first_back(layer.sm, t3)
    save_text.start()
    r_feed[2][0].fourth()
    r_small[0].relay(1)
    r_feed[0][1].relay(0)
    r_small[1].third(0)
    r_small[4].fourth()
    r_small[1].third(1)
    r_small[3].third(0)
    r_feed[1][0].fourth()
    r_feed[2][0].relay(0)
    r_small[3].third(1)
    r_feed[2][1].relay(0)
    r_feed[1][1].relay(0)
    r_small[1].fourth()
    r_feed[0][0].relay(1)
    r_small[1].relay(0)
    r_small[3].fourth()
    r_feed[2][1].relay(1)
    r_small[0].fourth()
    r_small[2].third(1)
    r_feed[0][0].fourth()
    norm.start(0)
    r_feed[1][0].relay(0)
    r_small[4].relay(0)
    r_small[2].third(0)
    r_feed[2][0].relay(1)
    r_small[3].relay(0)
    r_feed[2][1].fifth()
    r_feed[0][0].third(1)
    r_small[0].third(1)
    r_feed[1][0].relay(1)
    r_small[2].fourth()
    norm.finish(0)
    norm.start(1)
    r_feed[0][1].relay(1)
    r_small[1].relay(1)
    r_feed[0][0].third(0)
    r_small[4].relay(1)
    r_feed[1][1].relay(1)
    r_feed[2][0].fifth()
    r_feed[0][1].fifth()
    store(r_feed[2][1], fin_out)
    r_small[2].relay(0)
    norm.finish(1)
    norm.start(2)
    store(r_feed[0][1], fin_out)
    r_small[0].third(0)
    r_small[3].relay(1)
    r_feed[0][0].fifth()
    r_small[1].fifth()
    r_feed[1][1].fifth()
    r_feed[1][0].fifth()
    r_small[4].fifth()
    r_small[2].relay(1)
    r_small[0].fifth()
    store(r_feed[0][0], fin_in)
    store(r_small[1], fin_s)
    store(r_feed[2][0], fin_in)
    store(r_feed[1][1], fin_out)
    store(r_small[0], fin_s)
    norm.finish(2)
    r_small[3].fifth()
    r_small[2].fifth()
    store(r_feed[1][0], fin_in)
    store(r_small[4], fin_s)
    store(r_small[3], fin_s)
    store(r_small[2], fin_s)
    save_text.wait()
    keep_back.wait()
    for k in range(1, 8):
        m = lax.rem(at.m + 8 - k, 8)
        there = pl.ds(pl.multiple_of(m * own_images, 8), own_images)
        ref = rows_out.at[:, there, :]
        remote(ref, ref, bsend.at[0], brecv.at[k - 1], at.sib).wait_recv()
    remote(seven, seven, bsend.at[0], brecv.at[0], at.sib).wait_send()
    for copy in norm.out:
        copy.wait_send()
    each(r_small, "drain")
    for groups in r_feed:
        each(groups, "drain")
    for copy in stores:
        copy.wait()


def whole(shards, rows, text, top, lengths, vectors):
    depth, width = shards[0].shape
    dmodel = depth * 4
    half = width // 2
    lanes = dmodel // 2
    ff = shards[8].shape[1] * 8
    units = ff // THIRDS
    half_in = units // 16
    shapes = [
        (8, 4, 2, 2, half, dmodel),
        (THIRDS, 4, 2, 2, half_in, dmodel),
        (THIRDS, 4, 2, 2, half, units),
    ]
    tokens = text.shape[0]
    images = lengths.shape[0]
    mem_rows = rows.shape[0] * rows.shape[1]
    groups = dmodel // 256
    any_ = pl.BlockSpec(memory_space=pl.ANY)
    vmem = pl.BlockSpec(memory_space=pltpu.VMEM)
    smem = pl.BlockSpec(memory_space=pltpu.SMEM)
    sems = pltpu.SemaphoreType.DMA
    scratch = [pltpu.VMEM(s, BF) for s in shapes]
    scratch += [
        pltpu.VMEM((8, 2 * depth, width), BF),
        pltpu.VMEM((2 * depth, 4 * width), BF),
        pltpu.VMEM((2, half, 4 * depth), BF),
    ]
    for s in range(THIRDS):
        n = 2 * s
        scratch += reduce_bufs(1, half_in, lanes, 128, n in Z_FIRST_BACK)
        scratch += reduce_bufs(1, half, units // 2, 256, n + 1 in Z_FIRST_BACK)
    for n, (a, b) in enumerate(SMALL_BACK, 2 * THIRDS):
        scratch += reduce_bufs(b - a, half, lanes, 128, n in Z_FIRST_BACK)
    scratch += [pltpu.VMEM((tokens, dmodel), BF) for _ in NAMES]
    scratch += [pltpu.VMEM((tokens, dmodel), F32) for _ in WIDE]
    stacks = [(3, tokens, dmodel), (1, tokens, dmodel), (2, mem_rows, dmodel)]
    scratch += [pltpu.VMEM(s, BF) for s in stacks]
    scratch += [
        pltpu.VMEM((tokens, units), BF),
        pltpu.VMEM((tokens, units), BF),
        pltpu.VMEM((8, rows.shape[0], images, dmodel), BF),
        pltpu.VMEM((images // 2, groups, 512, 128), BF),
        pltpu.VMEM((tokens, 128), BF),
        pltpu.VMEM((8, dmodel), F32),
        pltpu.VMEM((8, dmodel), F32),
        pltpu.VMEM((8, dmodel), F32),
        pltpu.VMEM((4, 8, dmodel), F32),
        pltpu.VMEM((4, 8, dmodel), F32),
    ]
    gathers = len(SMALL) + 2 * THIRDS
    reduces = len(SMALL_BACK) + 2 * THIRDS
    counts = (10, 10, Gather.SENDS * gathers, Gather.RECVS * gathers)
    counts += (reduces, Reduce.RECVS * reduces, 1, 7, 1, 7, 7, 7, 14 + reduces)
    scratch += [sems((n,)) for n in counts]
    return pl.pallas_call(
        functools.partial(whole_kernel, images),
        out_shape=[
            jax.ShapeDtypeStruct((8, 2, half, lanes), BF),
            jax.ShapeDtypeStruct((THIRDS, 2, half_in, lanes), BF),
            jax.ShapeDtypeStruct((THIRDS, 2, half, units // 2), BF),
            jax.ShapeDtypeStruct(text.shape, BF),
            jax.ShapeDtypeStruct(text.shape, BF),
            jax.ShapeDtypeStruct(rows.shape, BF),
            jax.ShapeDtypeStruct((8, dmodel), F32),
            jax.ShapeDtypeStruct((images // 2, groups, 512, 128), BF),
        ],
        in_specs=[any_] * 13 + [smem] + [vmem] * 6,
        out_specs=[any_] * 6 + [vmem, any_],
        scratch_shapes=scratch,
        compiler_params=pltpu.CompilerParams(
            collective_id=0, has_side_effects=True, vmem_limit_bytes=63 << 20
        ),
    )(*shards, rows, text, top, lengths, *vectors)


def finish_kernel(*refs):
    fin_s, fin_in, fin_out, norm, *moved = refs[:7]
    outs, norm_outs, targets, sem = refs[7:17], refs[17:23], refs[23:26], refs[26]
    copies = []
    for i, (a, b) in enumerate(zip(moved, targets)):
        copy = pltpu.make_async_copy(a, b, sem.at[i])
        copy.start()
        copies.append(copy)
    c = lax.rem(lax.axis_index("dp"), 2)
    depth = outs[0].shape[0]
    sel = pick(depth, 2 * depth, c * depth)
    for w in range(8):
        both = fin_s[w].reshape(outs[w].shape[1], 2 * depth)
        outs[w][...] = dot_nt(sel, both)
    outs[8][...] = dot_nt(sel, fin_in[...].reshape(outs[8].shape[1], 2 * depth))
    half = fin_out.shape[2]
    for s in range(THIRDS):
        for h in range(2):
            for b in range(2):
                lo = pl.multiple_of(c * 256 + 128 * b, 128)
                cut = b * (128 * THIRDS) + 128 * s
                outs[9][half * h : half * (h + 1), cut : cut + 128] = fin_out[
                    s, h, :, pl.ds(lo, 128)
                ].astype(F32)
    for i, out in enumerate(norm_outs):
        out[...] = norm[i : i + 1, :].reshape(out.shape)
    for copy in copies:
        copy.wait()


def finish(fin_s, fin_in, fin_out, norm, moved, shapes):
    any_ = pl.BlockSpec(memory_space=pl.ANY)
    vmem = pl.BlockSpec(memory_space=pltpu.VMEM)
    return pl.pallas_call(
        finish_kernel,
        out_shape=[jax.ShapeDtypeStruct(s, F32) for s in shapes]
        + [jax.ShapeDtypeStruct(norm.shape[1:], F32)] * 6
        + [jax.ShapeDtypeStruct(a.shape, a.dtype) for a in moved],
        in_specs=[vmem] * 7,
        out_specs=[vmem] * 16 + [any_] * 3,
        scratch_shapes=[pltpu.SemaphoreType.DMA((3,))],
    )(fin_s, fin_in, fin_out, norm, *moved)


def fits(mesh_shape, text, memory, mats):
    images, txt, dmodel = text.shape
    depth, width = mats[0].shape
    return (
        mesh_shape["dp"] == 4
        and mesh_shape["mem"] == 8
        and images == 8
        and txt == HEAD == 64
        and memory.shape[0] == 8 * images
        and (memory.shape[1] * 8) % 32 == 0
        and memory.shape[1] * 8 <= 128
        and dmodel == HEADS * HEAD == 4 * depth == 8 * width
        and dmodel % 256 == 0
        and width % 32 == 0
        and mats[8].shape == (depth, 4 * width)
        and 4 * width == 128 * THIRDS
        and mats[9].shape == (4 * depth, width)
    )


def shards_lean(text, lengths, memory, out_grad, *params):
    mats, vectors = params[:10], params[10:]
    images, txt, dmodel = text.shape
    tokens = images * txt
    mats = mats[:9] + (mats[9].T,)
    fin_s, fin_in, fin_out, layer_out, text_grad, back, norm_sums, _ = whole(
        mats,
        memory.transpose(1, 0, 2),
        text.reshape(tokens, dmodel),
        out_grad.reshape(tokens, dmodel),
        lengths,
        vectors,
    )
    *grads, layer_out, text_grad, back = finish(
        fin_s,
        fin_in,
        fin_out,
        norm_sums,
        (layer_out, text_grad, back),
        [mat.shape for mat in mats],
    )
    return (
        layer_out.reshape(text.shape),
        text_grad.reshape(text.shape),
        back.transpose(1, 0, 2),
        *grads[:9],
        grads[9].T,
        *grads[10:],
    )


def solution(mesh):
    def pick_form(text, lengths, memory, out_grad, *params):
        lean = fits(mesh.shape, text, memory, params[:10])
        form = shards_lean if lean else shards
        return form(text, lengths, memory, out_grad, *params)

    return jax.shard_map(
        pick_form,
        mesh=mesh,
        in_specs=(
            P(("dp", "mem"), None, None),
            P(("dp", "mem")),
            P("dp", "mem", None),
            P(("dp", "mem"), None, None),
            P("dp", "mem"),
            P("dp", "mem"),
            P("dp", "mem"),
            P("dp", "mem"),
            P("dp", "mem"),
            P("dp", "mem"),
            P("dp", "mem"),
            P("dp", "mem"),
            P("dp", "mem"),
            P("dp", "mem"),
            P(),
            P(),
            P(),
            P(),
            P(),
            P(),
        ),
        out_specs=(
            P(("dp", "mem"), None, None),
            P(("dp", "mem"), None, None),
            P("dp", "mem", None),
            P("dp", "mem"),
            P("dp", "mem"),
            P("dp", "mem"),
            P("dp", "mem"),
            P("dp", "mem"),
            P("dp", "mem"),
            P("dp", "mem"),
            P("dp", "mem"),
            P("dp", "mem"),
            P("dp", "mem"),
            P(),
            P(),
            P(),
            P(),
            P(),
            P(),
        ),
        check_vma=False,
    )
```

```python
import functools

import jax
import jax.numpy as jnp
from jax import lax
from jax.experimental import pallas as pl
from jax.experimental.pallas import tpu as pltpu
from jax.sharding import PartitionSpec as P

HEADS = 12
HEAD = 64
MESH = pl.DeviceIdType.MESH
BF = jnp.bfloat16
F32 = jnp.float32
EPS = 1e-06
NEG = -1e30


def layer_norm(values, scaling, offsets):
    center = values - jnp.mean(values, axis=-1, keepdims=True)
    spread = jnp.mean(center * center, axis=-1, keepdims=True)
    return center * lax.rsqrt(spread + EPS) * scaling + offsets


def norm_back(values, scaling, offsets, upstream):
    _, pull_back = jax.vjp(layer_norm, values, scaling, offsets)
    return pull_back(upstream)


def split_heads(values):
    return values.reshape(values.shape[0], values.shape[1], HEADS, HEAD)


def join_heads(values):
    return values.reshape(values.shape[0], values.shape[1], HEADS * HEAD)


def apply_mat(acts, matrix):
    return jnp.einsum("bsd,de->bse", acts, matrix, preferred_element_type=jnp.float32)


def apply_back(grads, matrix):
    return jnp.einsum("bse,de->bsd", grads, matrix, preferred_element_type=jnp.float32)


def mat_grad(acts, grads):
    return jnp.einsum("bsd,bse->de", acts, grads, preferred_element_type=jnp.float32)


def score_rows(queries, keys, allowed):
    score_scale = HEAD ** (-0.5)
    scores = (
        jnp.einsum(
            "bshd,bthd->bhst",
            split_heads(queries),
            split_heads(keys),
            preferred_element_type=jnp.float32,
        )
        * score_scale
    )
    if allowed is not None:
        scores = jnp.where(allowed, scores, NEG)
    return scores


def attend_fwd(queries, keys, values, allowed):
    scores = score_rows(queries, keys, allowed)
    highest = jnp.max(scores, axis=-1, keepdims=True)
    powered = jnp.exp(scores - highest)
    expo_sum = jnp.sum(powered, axis=-1, keepdims=True)
    weights = (powered / expo_sum).astype(jnp.bfloat16)
    mixed_heads = jnp.einsum(
        "bhst,bthd->bshd", weights, split_heads(values), preferred_element_type=jnp.float32
    )
    return (join_heads(mixed_heads).astype(jnp.bfloat16), highest + jnp.log(expo_sum))


def attend_back(queries, keys, values, allowed, log_sum, upstream):
    score_scale = HEAD ** (-0.5)
    probs_full = jnp.exp(score_rows(queries, keys, allowed) - log_sum)
    heads_up = split_heads(upstream)
    prob_grad = jnp.einsum(
        "bshd,bthd->bhst", heads_up, split_heads(values), preferred_element_type=jnp.float32
    )
    score_low = (
        probs_full * (prob_grad - jnp.sum(prob_grad * probs_full, axis=-1, keepdims=True))
    ).astype(jnp.bfloat16)
    value_grad = jnp.einsum(
        "bhst,bshd->bthd",
        probs_full.astype(jnp.bfloat16),
        heads_up,
        preferred_element_type=jnp.float32,
    )
    query_grad = (
        jnp.einsum(
            "bhst,bthd->bshd", score_low, split_heads(keys), preferred_element_type=jnp.float32
        )
        * score_scale
    )
    key_grad = (
        jnp.einsum(
            "bhst,bshd->bthd", score_low, split_heads(queries), preferred_element_type=jnp.float32
        )
        * score_scale
    )
    return (
        join_heads(query_grad).astype(jnp.bfloat16),
        join_heads(key_grad).astype(jnp.bfloat16),
        join_heads(value_grad).astype(jnp.bfloat16),
    )


def fetch_weights(mats):
    columns = (
        lax.all_gather(mats[0], "mem", axis=1, tiled=True),
        lax.all_gather(mats[1], "mem", axis=1, tiled=True),
        lax.all_gather(mats[2], "mem", axis=1, tiled=True),
        lax.all_gather(mats[3], "mem", axis=1, tiled=True),
        lax.all_gather(mats[4], "mem", axis=1, tiled=True),
        lax.all_gather(mats[5], "mem", axis=1, tiled=True),
        lax.all_gather(mats[6], "mem", axis=1, tiled=True),
        lax.all_gather(mats[7], "mem", axis=1, tiled=True),
        lax.all_gather(mats[8], "mem", axis=1, tiled=True),
        lax.all_gather(mats[9], "mem", axis=1, tiled=True),
    )
    return (
        lax.all_gather(columns[0], "dp", axis=0, tiled=True),
        lax.all_gather(columns[1], "dp", axis=0, tiled=True),
        lax.all_gather(columns[2], "dp", axis=0, tiled=True),
        lax.all_gather(columns[3], "dp", axis=0, tiled=True),
        lax.all_gather(columns[4], "dp", axis=0, tiled=True),
        lax.all_gather(columns[5], "dp", axis=0, tiled=True),
        lax.all_gather(columns[6], "dp", axis=0, tiled=True),
        lax.all_gather(columns[7], "dp", axis=0, tiled=True),
        lax.all_gather(columns[8], "dp", axis=0, tiled=True),
        lax.all_gather(columns[9], "dp", axis=0, tiled=True),
    )


def reduce_all(grads):
    row_sums = (
        lax.psum_scatter(
            grads[0].astype(jnp.bfloat16), "dp", scatter_dimension=0, tiled=True
        ).astype(jnp.float32),
        lax.psum_scatter(
            grads[1].astype(jnp.bfloat16), "dp", scatter_dimension=0, tiled=True
        ).astype(jnp.float32),
        lax.psum_scatter(
            grads[2].astype(jnp.bfloat16), "dp", scatter_dimension=0, tiled=True
        ).astype(jnp.float32),
        lax.psum_scatter(
            grads[3].astype(jnp.bfloat16), "dp", scatter_dimension=0, tiled=True
        ).astype(jnp.float32),
        lax.psum_scatter(
            grads[4].astype(jnp.bfloat16), "dp", scatter_dimension=0, tiled=True
        ).astype(jnp.float32),
        lax.psum_scatter(
            grads[5].astype(jnp.bfloat16), "dp", scatter_dimension=0, tiled=True
        ).astype(jnp.float32),
        lax.psum_scatter(
            grads[6].astype(jnp.bfloat16), "dp", scatter_dimension=0, tiled=True
        ).astype(jnp.float32),
        lax.psum_scatter(
            grads[7].astype(jnp.bfloat16), "dp", scatter_dimension=0, tiled=True
        ).astype(jnp.float32),
        lax.psum_scatter(
            grads[8].astype(jnp.bfloat16), "dp", scatter_dimension=0, tiled=True
        ).astype(jnp.float32),
        lax.psum_scatter(
            grads[9].astype(jnp.bfloat16), "dp", scatter_dimension=0, tiled=True
        ).astype(jnp.float32),
    )
    return (
        lax.psum_scatter(
            row_sums[0].astype(jnp.bfloat16), "mem", scatter_dimension=1, tiled=True
        ).astype(jnp.float32),
        lax.psum_scatter(
            row_sums[1].astype(jnp.bfloat16), "mem", scatter_dimension=1, tiled=True
        ).astype(jnp.float32),
        lax.psum_scatter(
            row_sums[2].astype(jnp.bfloat16), "mem", scatter_dimension=1, tiled=True
        ).astype(jnp.float32),
        lax.psum_scatter(
            row_sums[3].astype(jnp.bfloat16), "mem", scatter_dimension=1, tiled=True
        ).astype(jnp.float32),
        lax.psum_scatter(
            row_sums[4].astype(jnp.bfloat16), "mem", scatter_dimension=1, tiled=True
        ).astype(jnp.float32),
        lax.psum_scatter(
            row_sums[5].astype(jnp.bfloat16), "mem", scatter_dimension=1, tiled=True
        ).astype(jnp.float32),
        lax.psum_scatter(
            row_sums[6].astype(jnp.bfloat16), "mem", scatter_dimension=1, tiled=True
        ).astype(jnp.float32),
        lax.psum_scatter(
            row_sums[7].astype(jnp.bfloat16), "mem", scatter_dimension=1, tiled=True
        ).astype(jnp.float32),
        lax.psum_scatter(
            row_sums[8].astype(jnp.bfloat16), "mem", scatter_dimension=1, tiled=True
        ).astype(jnp.float32),
        lax.psum_scatter(
            row_sums[9].astype(jnp.bfloat16), "mem", scatter_dimension=1, tiled=True
        ).astype(jnp.float32),
    )


def shards(
    text,
    lengths,
    memory,
    out_grad,
    self_query,
    self_key,
    self_value,
    self_output,
    cross_query,
    cross_key,
    cross_value,
    cross_output,
    hidden_in,
    hidden_out,
    first_gain,
    first_shift,
    second_gain,
    second_shift,
    third_gain,
    third_shift,
):
    mats = (
        self_query,
        self_key,
        self_value,
        self_output,
        cross_query,
        cross_key,
        cross_value,
        cross_output,
        hidden_in,
        hidden_out,
    )
    full_mats = fetch_weights(mats)
    w_query, w_key, w_value, w_output, m_query, m_key, m_value, m_output, w_in, w_out = full_mats
    places = jnp.arange(text.shape[1])
    valid_row = places[None, :] < lengths[:, None]
    allowed = (places[None, :] <= places[:, None])[None, None] & valid_row[:, None, None, :]
    residual = text.astype(jnp.float32)
    first = layer_norm(residual, first_gain, first_shift).astype(jnp.bfloat16)
    queries = apply_mat(first, w_query).astype(jnp.bfloat16)
    keys = apply_mat(first, w_key).astype(jnp.bfloat16)
    values = apply_mat(first, w_value).astype(jnp.bfloat16)
    self_mixed, self_lse = attend_fwd(queries, keys, values, allowed)
    after_self = residual + apply_mat(self_mixed, w_output)
    memory_rows = lax.all_to_all(memory, "mem", split_axis=0, concat_axis=1, tiled=True)
    second = layer_norm(after_self, second_gain, second_shift).astype(jnp.bfloat16)
    cross_queries = apply_mat(second, m_query).astype(jnp.bfloat16)
    mem_keys = apply_mat(memory_rows, m_key).astype(jnp.bfloat16)
    mem_values = apply_mat(memory_rows, m_value).astype(jnp.bfloat16)
    cross_mixed, cross_lse = attend_fwd(cross_queries, mem_keys, mem_values, None)
    after_cross = after_self + apply_mat(cross_mixed, m_output)
    third = layer_norm(after_cross, third_gain, third_shift).astype(jnp.bfloat16)
    before_act = apply_mat(third, w_in)
    activated = jax.nn.gelu(before_act).astype(jnp.bfloat16)
    final = after_cross + apply_mat(activated, w_out)
    layer_out = jnp.where(valid_row[:, :, None], final, 0.0).astype(jnp.bfloat16)
    b_query, b_key, b_value, b_output, n_query, n_key, n_value, n_output, b_in, b_out = full_mats
    grad_top = jnp.where(valid_row[:, :, None], out_grad.astype(jnp.float32), 0.0)
    top_low = grad_top.astype(jnp.bfloat16)
    hidden_out_grad = mat_grad(activated, top_low)
    _, gelu_pull = jax.vjp(jax.nn.gelu, before_act)
    act_low = gelu_pull(apply_back(top_low, b_out))[0].astype(jnp.bfloat16)
    hidden_in_grad = mat_grad(third, act_low)
    cross_input, third_gain_grad, third_shift_grad = norm_back(
        after_cross, third_gain, third_shift, apply_back(act_low, b_in)
    )
    grad_cross = grad_top + cross_input
    cross_low = grad_cross.astype(jnp.bfloat16)
    cross_output_grad = mat_grad(cross_mixed, cross_low)
    mixed_up = apply_back(cross_low, n_output).astype(jnp.bfloat16)
    cross_query_low, mem_key_low, mem_value_low = attend_back(
        cross_queries, mem_keys, mem_values, None, cross_lse, mixed_up
    )
    cross_query_grad = mat_grad(second, cross_query_low)
    cross_key_grad = mat_grad(memory_rows, mem_key_low)
    cross_value_grad = mat_grad(memory_rows, mem_value_low)
    mem_back = (apply_back(mem_key_low, n_key) + apply_back(mem_value_low, n_value)).astype(
        jnp.bfloat16
    )
    memory_grad = lax.all_to_all(mem_back, "mem", split_axis=1, concat_axis=0, tiled=True)
    self_input, second_gain_grad, second_shift_grad = norm_back(
        after_self, second_gain, second_shift, apply_back(cross_query_low, n_query)
    )
    grad_self = grad_cross + self_input
    self_low = grad_self.astype(jnp.bfloat16)
    self_output_grad = mat_grad(self_mixed, self_low)
    self_up = apply_back(self_low, b_output).astype(jnp.bfloat16)
    query_low, key_low, value_low = attend_back(queries, keys, values, allowed, self_lse, self_up)
    self_query_grad = mat_grad(first, query_low)
    self_key_grad = mat_grad(first, key_low)
    self_value_grad = mat_grad(first, value_low)
    first_up = (
        apply_back(query_low, b_query) + apply_back(key_low, b_key) + apply_back(value_low, b_value)
    )
    text_input, first_gain_grad, first_shift_grad = norm_back(
        residual, first_gain, first_shift, first_up
    )
    text_grad = (grad_self + text_input).astype(jnp.bfloat16)
    weight_sums = reduce_all(
        (
            self_query_grad,
            self_key_grad,
            self_value_grad,
            self_output_grad,
            cross_query_grad,
            cross_key_grad,
            cross_value_grad,
            cross_output_grad,
            hidden_in_grad,
            hidden_out_grad,
        )
    )
    norm_sums = lax.psum(
        (
            first_gain_grad,
            first_shift_grad,
            second_gain_grad,
            second_shift_grad,
            third_gain_grad,
            third_shift_grad,
        ),
        ("dp", "mem"),
    )
    return (
        layer_out,
        text_grad,
        memory_grad,
        weight_sums[0],
        weight_sums[1],
        weight_sums[2],
        weight_sums[3],
        weight_sums[4],
        weight_sums[5],
        weight_sums[6],
        weight_sums[7],
        weight_sums[8],
        weight_sums[9],
        norm_sums[0],
        norm_sums[1],
        norm_sums[2],
        norm_sums[3],
        norm_sums[4],
        norm_sums[5],
    )


class Place:
    def __init__(self):
        self.d = lax.axis_index("dp")
        self.m = lax.axis_index("mem")
        self.c = lax.rem(self.d, 2)
        self.x = lax.div(self.d, 2)
        self.y = lax.rem(self.m, 2)
        self.z = lax.div(self.m, 2)
        self.oc, self.ox, self.oy = 1 - self.c, 1 - self.x, 1 - self.y
        self.sib = (self.x * 2 + self.oc, self.m)
        self.xn = (self.ox * 2 + self.c, self.m)
        self.yn = (self.d, self.z * 2 + self.oy)
        self.xyn = (self.ox * 2 + self.c, self.z * 2 + self.oy)

        self.side = lax.div(self.z, 2)
        self.inner = lax.rem(lax.div(self.z + 1, 2), 2) == 1
        self.flip = self.z + 1 - 2 * lax.rem(self.z, 2)
        self.ours, self.theirs = pl.ds(2 * self.side, 2), pl.ds(2 - 2 * self.side, 2)
        self.flip_peer = (self.d, self.flip * 2 + self.y)
        self.across = (self.d, (3 - self.z) * 2 + self.y)

    def zpeer(self, k):
        return (self.d, lax.rem(self.z + k, 4) * 2 + self.y)

    def mpeer(self, k):
        return (self.d, lax.rem(self.m + k, 8))


def greet(at):
    barrier = pltpu.get_barrier_semaphore()
    peers = [at.sib, at.xn, at.xyn] + [at.mpeer(k) for k in range(1, 8)]
    for peer in peers:
        pl.semaphore_signal(barrier, inc=1, device_id=peer, device_id_type=MESH)
    pl.semaphore_wait(barrier, len(peers))


def remote(src, dst, send, recv, peer):
    return pltpu.make_async_remote_copy(
        src_ref=src,
        dst_ref=dst,
        send_sem=send,
        recv_sem=recv,
        device_id=peer,
        device_id_type=MESH,
    )


class Gather:
    SENDS, RECVS = 4, 7

    def __init__(self, at, full, span, via_y, sends, recvs, index):
        self.at, self.full, self.span = at, full, span
        self.sends = [sends.at[self.SENDS * index + i] for i in range(self.SENDS)]
        self.recvs = [recvs.at[self.RECVS * index + i] for i in range(self.RECVS)]
        self.lanes = full.shape[-1] // 2
        self.cuts = ((0, via_y), (via_y, self.lanes - via_y))

    def piece(self, z, y, h, x, cut=None):
        start, size = cut or (0, self.lanes)
        lo = pl.multiple_of(x * self.lanes + start, 128)
        return self.full.at[self.span, z, y, h, :, pl.ds(lo, size)]

    def send(self, kind, slot, ref, peer):
        remote(ref, ref, self.sends[kind], self.recvs[slot], peer).start()

    def got(self, slot, ref):
        remote(ref, ref, self.sends[0], self.recvs[slot], self.at.sib).wait_recv()

    def sent(self, kind, ref):
        remote(ref, ref, self.sends[kind], self.recvs[0], self.at.sib).wait_send()

    def line(self, z):
        return self.piece(z, self.at.y, self.at.c, self.at.x)

    def begin(self):
        at = self.at
        own = self.line(at.z)
        self.send(2, 0, own, at.flip_peer)
        self.send(1, 2, own, at.xn)
        self.send(1, 3, own, at.yn)
        self.send(0, 6, own, at.sib)

    def spread(self, ref):
        at = self.at
        self.send(1, 2, ref, at.xn)
        self.send(1, 3, ref, at.yn)
        self.send(0, 6, ref, at.sib)

    def second(self, k):
        at = self.at
        if k == 1:
            self.got(0, self.line(at.flip))
            pl.when(at.inner)(lambda: self.send(3, 1, self.line(at.ours), at.across))
            self.spread(self.line(at.flip))
        elif k == 2:

            @pl.when(at.inner)
            def _():
                self.got(1, self.line(at.theirs))
                self.send(3, 1, self.line(at.theirs), at.flip_peer)
        else:
            pl.when(~at.inner)(lambda: self.got(1, self.line(at.theirs)))
            self.spread(self.line(at.theirs))

    def third(self, part):
        at, every = self.at, slice(None)
        x, y, peer = ((at.ox, at.y, at.yn), (at.x, at.oy, at.xn))[part]
        ref = self.piece(every, y, at.c, x)
        self.got(2 + part, ref)
        self.send(1, 4 + part, self.piece(every, y, at.c, x, self.cuts[part]), peer)
        self.send(0, 6, ref, at.sib)

    def fourth(self):
        at = self.at
        for part, cut in enumerate(self.cuts):
            ref = self.piece(slice(None), at.oy, at.c, at.ox, cut)
            self.got(4 + part, ref)
            self.send(0, 6, ref, at.sib)

    def last(self):
        self.got(6, self.full.at[self.span, :, :, self.at.oc])

    def drain(self):
        at = self.at
        self.sent(0, self.full.at[self.span, :, :, at.c])
        self.sent(1, self.full.at[self.span, pl.ds(0, 3), :, at.c])
        self.sent(2, self.line(at.z))
        pl.when(at.inner)(lambda: self.sent(3, self.line(slice(None))))


class GatherLast(Gather):
    def block(self, z):
        return self.full.at[self.span, z, :, self.at.c]

    def begin(self):
        self.spread(self.line(self.at.z))

    def third(self, part):
        at = self.at
        x, y, peer = ((at.ox, at.y, at.yn), (at.x, at.oy, at.xn))[part]
        ref = self.piece(at.z, y, at.c, x)
        self.got(2 + part, ref)
        self.send(1, 4 + part, self.piece(at.z, y, at.c, x, self.cuts[part]), peer)
        self.send(0, 6, ref, at.sib)

    def fourth(self):
        at = self.at
        for part, cut in enumerate(self.cuts):
            ref = self.piece(at.z, at.oy, at.c, at.ox, cut)
            self.got(4 + part, ref)
            self.send(0, 6, ref, at.sib)
        self.send(2, 0, self.block(at.z), at.flip_peer)

    def second(self, k):
        at = self.at
        if k == 1:
            ref = self.block(at.flip)
            self.got(0, ref)
            pl.when(at.inner)(lambda: self.send(3, 1, self.block(at.ours), at.across))
            self.send(0, 6, ref, at.sib)
        elif k == 2:

            @pl.when(at.inner)
            def _():
                self.got(1, self.block(at.theirs))
                self.send(3, 1, self.block(at.theirs), at.flip_peer)
        else:
            pl.when(~at.inner)(lambda: self.got(1, self.block(at.theirs)))
            self.send(0, 6, self.block(at.theirs), at.sib)

    def drain(self):
        at = self.at
        self.sent(0, self.full.at[self.span, :, :, at.c])
        self.sent(1, self.line(pl.ds(0, 3)))
        self.sent(2, self.block(at.z))
        pl.when(at.inner)(lambda: self.sent(3, self.full.at[self.span, :, :, at.c]))


class Reduce:
    RECVS = 9

    def __init__(self, at, full, span, bufs, sends, recvs, index):
        self.at, self.full, self.span = at, full, span
        (self.chip, self.via_y, self.via_x, self.rx, self.ry) = bufs[:5]
        (self.outer, self.middle, self.pair, self.fin) = bufs[5:]
        self.sends = sends.at[index]
        self.recvs = [recvs.at[self.RECVS * index + i] for i in range(self.RECVS)]
        self.count, self.lanes = self.chip.shape[0], full.shape[-1] // 2
        cut = self.via_y.shape[-1]
        self.cuts = (slice(0, cut), slice(cut, self.lanes))

    def send(self, slot, src, dst, peer):
        remote(src, dst, self.sends, self.recvs[slot], peer).start()

    def got(self, slot, ref):
        remote(ref, ref, self.sends, self.recvs[slot], self.at.sib).wait_recv()

    def begin(self):
        at = self.at
        for x in range(2):
            lanes = slice(x * self.lanes, (x + 1) * self.lanes)
            src = self.full.at[self.span, :, :, at.oc, :, lanes]
            self.send(0, src, self.chip.at[:, x], at.sib)

    def add_cores(self):
        at = self.at
        chip, full, lanes, w0 = self.chip, self.full, self.lanes, self.span.start
        self.got(0, chip)

        def add(i, carry):
            w, r = lax.div(i, 8), lax.rem(i, 8)
            z, y = lax.div(r, 2), lax.rem(r, 2)
            for x in range(2):
                mine = full[w0 + w, z, y, at.c, :, x * lanes : (x + 1) * lanes]
                chip[w, x, z, y] = (
                    chip[w, x, z, y].astype(F32) + mine.astype(F32)
                ).astype(BF)
            return carry

        lax.fori_loop(0, 8 * self.count, add, 0)

    def second(self):
        at, chip = self.at, self.chip
        self.add_cores()
        self.send(1, chip.at[:, at.ox, :, at.oy, :, self.cuts[0]], self.via_y, at.yn)
        self.send(2, chip.at[:, at.ox, :, at.oy, :, self.cuts[1]], self.via_x, at.xn)

    def third(self, part):
        at, chip = self.at, self.chip
        ref = (self.via_y, self.via_x)[part]
        x, y = ((at.ox, at.y), (at.x, at.oy))[part]
        cut = self.cuts[part]
        self.got(1 + part, ref)

        def add(i, carry):
            w, z = lax.div(i, 4), lax.rem(i, 4)
            chip[w, x, z, y, :, cut] = (
                chip[w, x, z, y, :, cut].astype(F32) + ref[w, z].astype(F32)
            ).astype(BF)
            return carry

        lax.fori_loop(0, 4 * self.count, add, 0)
        box, peer = ((self.rx, at.xn), (self.ry, at.yn))[part]
        self.send(3 + part, chip.at[:, x, :, y], box, peer)

    def fourth(self):
        at, chip = self.at, self.chip
        self.got(3, self.rx)
        self.got(4, self.ry)

        def add(i, carry):
            w, z = lax.div(i, 4), lax.rem(i, 4)
            chip[w, at.x, z, at.y] = (
                chip[w, at.x, z, at.y].astype(F32)
                + self.rx[w, z].astype(F32)
                + self.ry[w, z].astype(F32)
            ).astype(BF)
            return carry

        lax.fori_loop(0, 4 * self.count, add, 0)
        self.inward()

    def line(self, z):
        return self.chip.at[:, self.at.x, z, self.at.y]

    def inward(self):
        at = self.at
        pl.when(~at.inner)(
            lambda: self.send(5, self.line(at.theirs), self.outer, at.flip_peer)
        )

    def add_line(self, start, ref):
        at, chip = self.at, self.chip

        def add(i, carry):
            w, z = lax.div(i, 2), lax.rem(i, 2)
            chip[w, at.x, start + z, at.y] = (
                chip[w, at.x, start + z, at.y].astype(F32) + ref[w, z].astype(F32)
            ).astype(BF)
            return carry

        lax.fori_loop(0, 2 * self.count, add, 0)

    def relay(self, stage):
        at = self.at
        if stage == 0:

            @pl.when(at.inner)
            def _():
                self.got(5, self.outer)
                self.add_line(2 - 2 * at.side, self.outer)
                self.send(6, self.line(at.theirs), self.middle, at.across)

            return

        @pl.when(at.inner)
        def _():
            self.got(6, self.middle)
            self.add_line(2 * at.side, self.middle)

        self.send(7, self.line(at.flip), self.pair, at.flip_peer)

    def finish(self, terms):
        at = self.at

        def add(w, carry):
            total = self.chip[w, at.x, at.z, at.y].astype(F32)
            for term in terms:
                total = total + term[w].astype(F32)
            self.fin[w, at.c] = total.astype(BF)
            return carry

        lax.fori_loop(0, self.count, add, 0)
        mine = self.fin.at[:, at.c]
        self.send(8, mine, mine, at.sib)

    def fifth(self):
        self.got(7, self.pair)
        self.finish([self.pair])

    def last(self):
        self.got(8, self.fin.at[:, self.at.oc])

    def drain(self):
        ref = self.full.at[self.span]
        remote(ref, ref, self.sends, self.recvs[0], self.at.sib).wait_send()


class ReduceFirst(Reduce):
    def line(self, z):
        return self.chip.at[:, :, z]

    def second(self):
        self.add_cores()
        self.inward()

    def add_line(self, start, ref, n=2):
        chip = self.chip

        def add(i, carry):
            w, r = lax.div(i, 4 * n), lax.rem(i, 4 * n)
            z, r = lax.div(r, 4), lax.rem(r, 4)
            x, y = lax.div(r, 2), lax.rem(r, 2)
            chip[w, x, start + z, y] = (
                chip[w, x, start + z, y].astype(F32) + ref[w, x, z, y].astype(F32)
            ).astype(BF)
            return carry

        lax.fori_loop(0, 4 * n * self.count, add, 0)

    def fourth(self):
        at, chip = self.at, self.chip
        self.got(7, self.pair)

        def add(i, carry):
            w, r = lax.div(i, 4), lax.rem(i, 4)
            x, y = lax.div(r, 2), lax.rem(r, 2)
            chip[w, x, at.z, y] = (
                chip[w, x, at.z, y].astype(F32) + self.pair[w, x, y].astype(F32)
            ).astype(BF)
            return carry

        lax.fori_loop(0, 4 * self.count, add, 0)
        self.send(1, chip.at[:, at.ox, at.z, at.oy, :, self.cuts[0]], self.via_y, at.yn)
        self.send(2, chip.at[:, at.ox, at.z, at.oy, :, self.cuts[1]], self.via_x, at.xn)

    def third(self, part):
        at, chip = self.at, self.chip
        ref = (self.via_y, self.via_x)[part]
        x, y = ((at.ox, at.y), (at.x, at.oy))[part]
        cut = self.cuts[part]
        self.got(1 + part, ref)

        def add(w, carry):
            chip[w, x, at.z, y, :, cut] = (
                chip[w, x, at.z, y, :, cut].astype(F32) + ref[w].astype(F32)
            ).astype(BF)
            return carry

        lax.fori_loop(0, self.count, add, 0)
        box, peer = ((self.rx, at.xn), (self.ry, at.yn))[part]
        self.send(3 + part, chip.at[:, x, at.z, y], box, peer)

    def fifth(self):
        self.got(3, self.rx)
        self.got(4, self.ry)
        self.finish([self.rx, self.ry])


def reduce_bufs(count, rows, lanes, cut, z_first):
    one, line, block = (rows, lanes), (4, rows, lanes), (2, 2, 2, rows, lanes)
    if z_first:
        shapes = [(rows, cut), (rows, lanes - cut), one, one, block, block, block[1:]]
    else:
        pair = (2, rows, lanes)
        shapes = [(4, rows, cut), (4, rows, lanes - cut), line, line, pair, pair, one]
    shapes = [(2, 4, 2, rows, lanes)] + shapes + [(2, rows, lanes)]
    return [pltpu.VMEM((count,) + shape, BF) for shape in shapes]


def pick(rows, cols, start):
    col = lax.broadcasted_iota(jnp.int32, (rows, cols), 1)
    row = lax.broadcasted_iota(jnp.int32, (rows, cols), 0)
    return jnp.where(col == row + start, 1.0, 0.0).astype(BF)


def dot_nt(a, b):
    return lax.dot_general(a, b, (((1,), (1,)), ((), ())), preferred_element_type=F32)


def dot_nn(a, b):
    return lax.dot_general(a, b, (((1,), (0,)), ((), ())), preferred_element_type=F32)


def dot_tn(a, b):
    return lax.dot_general(a, b, (((0,), (0,)), ((), ())), preferred_element_type=F32)


def norm_stats(values):
    center = values - jnp.mean(values, axis=-1, keepdims=True)
    scale = lax.rsqrt(jnp.mean(center * center, axis=-1, keepdims=True) + EPS)
    return center * scale, scale


def gelu_both(value):
    c0, c1 = 0.7978845608028654, 0.044715
    square = value * value
    tanh = jnp.tanh(c0 * value * (1.0 + c1 * square))
    half = 0.5 + 0.5 * tanh
    slope = half + 0.5 * value * (1.0 - tanh * tanh) * (c0 + 3.0 * c0 * c1 * square)
    return value * half, slope


def softmax(scores):
    powered = jnp.exp(scores - jnp.max(scores, axis=-1, keepdims=True))
    return powered / jnp.sum(powered, axis=-1, keepdims=True)


class Layer:
    def __init__(self, **refs):
        self.__dict__.update(refs)
        self.tokens, self.dmodel = self.nrm.shape
        self.images = self.own_images
        self.txt = self.tokens // self.images
        self.mem_len = self.mkv.shape[1] // self.images
        lane = lax.broadcasted_iota(jnp.int32, (1, 4 * HEAD), 1)
        self.head_lanes = [
            jnp.where((lane >= HEAD * h) & (lane < HEAD * (h + 1)), 1.0, 0.0)
            for h in range(4)
        ]

    def weight(self, i):
        return self.full_s[i].reshape(self.dmodel, self.dmodel)

    def put_weight(self, i, value):
        self.full_s[i] = value.astype(BF).reshape(self.full_s.shape[1:])

    def blocks(self, size, fn, total=None):
        def step(i, carry):
            fn(pl.ds(pl.multiple_of(i * size, size), size))
            return carry

        lax.fori_loop(0, (total or self.tokens) // size, step, 0)

    def spread(self, value):
        return jnp.concatenate(
            [value * mask.astype(BF) for mask in self.head_lanes], axis=0
        )

    def gather_heads(self, value):
        n = value.shape[0] // 4
        out = value[:n] * self.head_lanes[0]
        for h in range(1, 4):
            out = out + value[h * n : (h + 1) * n] * self.head_lanes[h]
        return out

    def norm_into(self, source, index):
        gain, shift = self.norms[2 * index : 2 * index + 1], self.norms[2 * index + 1 : 2 * index + 2]

        def block(rows):
            hat, _ = norm_stats(source[rows, :].astype(F32))
            self.nrm[rows, :] = (hat * gain + shift).astype(BF)

        self.blocks(128, block)

    def norm_back(self, source, upstream, index, finish):
        gain = self.norms[2 * index : 2 * index + 1]

        def step(i, carry):
            rows = pl.ds(pl.multiple_of(i * 64, 64), 64)
            hat, scale = norm_stats(source[rows, :].astype(F32))
            up = upstream[rows, :]
            scaled = up * gain
            first = jnp.mean(scaled, axis=-1, keepdims=True)
            second = jnp.mean(scaled * hat, axis=-1, keepdims=True)
            finish(rows, scale * (scaled - first - hat * second))
            gains, shifts = carry
            return (
                gains + jnp.sum(up * hat, axis=0, keepdims=True),
                shifts + jnp.sum(up, axis=0, keepdims=True),
            )

        zero = jnp.zeros((1, self.dmodel), F32)
        gains, shifts = lax.fori_loop(0, self.tokens // 64, step, (zero, zero))
        self.norm_grads[2 * index : 2 * index + 1, :] = gains
        self.norm_grads[2 * index + 1 : 2 * index + 2, :] = shifts


    def project(self, outs, value, first):
        def step(i, carry):
            outs[i] = dot_nt(value(), self.weight(first + i)).astype(BF)
            return carry

        lax.fori_loop(0, outs.shape[0], step, 0)

    def allowed(self, p):
        n = 2 * self.txt
        row = lax.broadcasted_iota(jnp.int32, (n, n), 0)
        col = lax.broadcasted_iota(jnp.int32, (n, n), 1)
        late = col >= self.txt
        length = jnp.where(
            late, self.txt + self.lengths[2 * p + 1], self.lengths[2 * p]
        )
        return (col <= row) & (col < length) & (late == (row >= self.txt))

    def self_forward(self, start, stop):
        def pair(p, carry):
            rows = pl.ds(pl.multiple_of(p * 128, 128), 128)
            allow = self.allowed(p)
            for g in range(self.dmodel // 256):
                cols = slice(256 * g, 256 * g + 256)
                scores = dot_nt(self.spread(self.qkv[0, rows, cols]), self.qkv[1, rows, cols])
                scores = scores.reshape(4, 128, 128) * HEAD**-0.5
                scores = jnp.where(allow[None], scores, NEG)
                probs = softmax(scores).reshape(512, 128).astype(BF)
                self.ps[p, g] = probs
                mixed = dot_nn(probs, self.qkv[2, rows, cols])
                self.sm[rows, cols] = self.gather_heads(mixed).astype(BF)
            return carry

        lax.fori_loop(start, stop, pair, 0)

    def add_after_self(self):
        def block(rows):
            self.after_self[rows, :] = self.io[rows, :].astype(F32) + dot_nt(
                self.sm[rows, :], self.weight(3)
            )

        self.blocks(256, block)

    def memory_in(self):
        n, size = self.images, self.mem_len
        total = n * size

        def block(i, carry):
            row = lax.broadcasted_iota(jnp.int32, (size, total), 0)
            col = lax.broadcasted_iota(jnp.int32, (size, total), 1)
            hot = jnp.where(col == n * row + i, 1.0, 0.0).astype(BF)
            rows = pl.ds(pl.multiple_of(i * size, 32), size)
            self.mkv[0, rows, :] = dot_nn(hot, self.memory()).astype(BF)
            return carry

        lax.fori_loop(0, n, block, 0)
        self.rows[...] = self.mkv[0].reshape(self.rows.shape)

    def memory(self):
        return self.rows[...].reshape(self.mkv.shape[1:])

    def memory_out(self):
        n, size = self.images, self.mem_len
        short, total = size // n, n * size

        def block(b, carry):
            row = lax.broadcasted_iota(jnp.int32, (size, total), 0)
            col = lax.broadcasted_iota(jnp.int32, (size, total), 1)
            image = row & (n - 1)
            slot = lax.shift_right_logical(row, n.bit_length() - 1) + b * short
            hot = jnp.where(col == image * size + slot, 1.0, 0.0).astype(BF)
            low, high = self.cm[...], self.t2[: total - self.tokens, : self.dmodel]
            back = dot_nn(hot[:, : self.tokens], low) + dot_nn(hot[:, self.tokens :], high)
            self.rows[b] = back.astype(BF).reshape(self.rows.shape[1:])
            return carry

        lax.fori_loop(0, n, block, 0)

    def probs_at(self, i, g):
        size = 4 * self.txt
        start = pl.multiple_of(lax.rem(i, 2) * size, size)
        return lax.div(i, 2), g, pl.ds(start, size), slice(0, self.mem_len)

    def cross_forward(self, start, stop):
        def image(i, carry):
            rows = pl.ds(pl.multiple_of(i * self.txt, 64), self.txt)
            mems = pl.ds(pl.multiple_of(i * self.mem_len, 32), self.mem_len)
            for g in range(self.dmodel // 256):
                cols = slice(256 * g, 256 * g + 256)
                scores = dot_nt(self.spread(self.cq[0, rows, cols]), self.mkv[0, mems, cols])
                probs = softmax(scores * HEAD**-0.5).astype(BF)
                self.ps[self.probs_at(i, g)] = probs
                mixed = dot_nn(probs, self.mkv[1, mems, cols])
                self.cm[rows, cols] = self.gather_heads(mixed).astype(BF)
            return carry

        lax.fori_loop(start, stop, image, 0)

    def add_after_cross(self):
        def block(rows):
            self.after_cross[rows, :] = self.after_self[rows, :] + dot_nt(
                self.cm[rows, :], self.weight(7)
            )

        self.blocks(256, block)


    def mask_top(self):
        def block(rows):
            self.io[rows, :] = self.io[rows, :] * self.valid[rows, :1]

        self.blocks(128, block)

    def feed_start(self):
        def block(rows):
            self.acc_out[rows, :] = self.after_cross[rows, :]
            self.acc_up[rows, :] = jnp.zeros((128, self.dmodel), F32)

        self.blocks(128, block)

    def feed_chunk(self, s):
        dmodel = self.dmodel
        units = self.t2.shape[1]

        def w_in(lo=0, n=units):
            return self.full_in[s].reshape(units, dmodel)[lo : lo + n]

        def w_out(lo=0, n=units):
            return self.full_out[s, :, :, :, :, lo : lo + n].reshape(dmodel, n)

        def block(rows):
            for lo in range(0, units, 512):
                before = dot_nt(self.nrm[rows, :], w_in(lo, 512))
                act, slope = gelu_both(before)
                self.t2[rows, lo : lo + 512] = act.astype(BF)
                up = dot_nn(self.io[rows, :], w_out(lo, 512))
                self.t3[rows, lo : lo + 512] = (slope * up).astype(BF)

        self.blocks(256, block)

        def block(rows):
            self.acc_out[rows, :] += dot_nt(self.t2[rows, :], w_out())
            self.acc_up[rows, :] += dot_nn(self.t3[rows, :], w_in())

        self.blocks(256, block)
        shape = self.full_out.shape[1:5]
        for lo in range(0, units, 512):
            grad = dot_tn(self.io[...], self.t2[:, lo : lo + 512]).astype(BF)
            self.full_out[s, :, :, :, :, lo : lo + 512] = grad.reshape(shape + (512,))
        grad = dot_tn(self.t3[...], self.nrm[...]).astype(BF)
        self.full_in[s] = grad.reshape(self.full_in.shape[1:])

    def layer_out(self, out):
        def block(rows):
            out[rows, : self.dmodel] = (self.acc_out[rows, :] * self.valid[rows, :1].astype(F32)).astype(BF)

        self.blocks(128, block)


    def third_back(self):
        def finish(rows, grad):
            total = self.io[rows, :].astype(F32) + grad
            self.acc_up[rows, :] = total
            self.io[rows, :] = total.astype(BF)

        self.norm_back(self.after_cross, self.acc_up, 2, finish)

    def output_back(self, i, mixed, out):
        out[:, : self.dmodel] = dot_nn(self.io[...], self.weight(i)).astype(BF)
        self.put_weight(i, dot_tn(self.io[...], mixed[...]))

    def attend_back(self, probs, up, q, k, v, rows, mems, cols):
        low_q = self.spread(q[rows, cols])
        low_up = self.spread(up[rows, cols])
        keys, values = k[mems, cols], v[mems, cols]
        full = probs.astype(F32)
        prob_grad = dot_nt(low_up, values)
        score = full * (prob_grad - jnp.sum(prob_grad * full, axis=-1, keepdims=True))
        score = (score * HEAD**-0.5).astype(BF)
        v[mems, cols] = dot_tn(probs, low_up).astype(BF)
        k[mems, cols] = dot_tn(score, low_q).astype(BF)
        q[rows, cols] = self.gather_heads(dot_nn(score, keys)).astype(BF)

    def cross_back(self, start, stop):
        def image(i, carry):
            rows = pl.ds(pl.multiple_of(i * self.txt, 64), self.txt)
            mems = pl.ds(pl.multiple_of(i * self.mem_len, 32), self.mem_len)
            for g in range(self.dmodel // 256):
                cols = slice(256 * g, 256 * g + 256)
                probs = self.ps[self.probs_at(i, g)]
                self.attend_back(
                    probs,
                    self.t2,
                    self.cq.at[0],
                    self.mkv.at[0],
                    self.mkv.at[1],
                    rows,
                    mems,
                    cols,
                )
            return carry

        lax.fori_loop(start, stop, image, 0)

    def self_back(self, start, stop):
        def pair(p, carry):
            rows = pl.ds(pl.multiple_of(p * 128, 128), 128)
            for g in range(self.dmodel // 256):
                cols = slice(256 * g, 256 * g + 256)
                self.attend_back(
                    self.ps[p, g],
                    self.t2,
                    self.qkv.at[0],
                    self.qkv.at[1],
                    self.qkv.at[2],
                    rows,
                    rows,
                    cols,
                )
            return carry

        lax.fori_loop(start, stop, pair, 0)

    def memory_back(self):
        size = 256
        keys, values = self.mkv.at[0], self.mkv.at[1]

        def back(rows):
            total = dot_nn(keys[rows, :], self.weight(5)) + dot_nn(
                values[rows, :], self.weight(6)
            )
            return total.astype(BF)

        def block(rows):
            self.cm[rows, :] = back(rows)

        self.blocks(size, block)
        for start in range(self.tokens, self.mkv.shape[1], size):
            there = slice(start - self.tokens, start - self.tokens + size)
            self.t2[there, : self.dmodel] = back(slice(start, start + size))

    def weight_grads(self, lows, value, first):
        def step(i, carry):
            self.put_weight(first + i, dot_tn(lows[i], value()))
            return carry

        lax.fori_loop(0, lows.shape[0], step, 0)

    def second_up(self):
        def block(rows):
            self.acc_out[rows, :] = dot_nn(self.cq[0, rows, :], self.weight(4))

        self.blocks(256, block)

    def second_back(self):
        def finish(rows, grad):
            total = self.acc_up[rows, :] + grad
            self.acc_up[rows, :] = total
            self.io[rows, :] = total.astype(BF)

        self.norm_back(self.after_self, self.acc_out, 1, finish)

    def first_up(self):
        def block(rows):
            self.acc_out[rows, :] = (
                dot_nn(self.qkv[0, rows, :], self.weight(0))
                + dot_nn(self.qkv[1, rows, :], self.weight(1))
                + dot_nn(self.qkv[2, rows, :], self.weight(2))
            )

        self.blocks(256, block)

    def first_back(self, text, out):
        def finish(rows, grad):
            out[rows, : self.dmodel] = (self.acc_up[rows, :] + grad).astype(BF)

        self.norm_back(text, self.acc_out, 0, finish)


class NormSum:
    def __init__(self, at, sums, pair, plane, line, out, sends, recvs):
        self.at, self.sums, self.pair = at, sums, pair
        self.boxes = (plane, line)
        self.sends, self.recvs = sends, recvs
        self.me = (at.x * 2 + at.y, at.z)
        self.target = (line.at[at.z], out)
        self.peers = ((at.xn, at.yn, at.xyn), tuple(at.zpeer(k) for k in (1, 2, 3)))
        self.out = []

    def start(self, stage):
        if stage == 0:
            copy = remote(
                self.sums, self.pair, self.sends.at[0], self.recvs.at[0], self.at.sib
            )
            copy.start()
            self.out.append(copy)
            return
        box = self.boxes[stage - 1].at[self.me[stage - 1]]
        for k, peer in enumerate(self.peers[stage - 1]):
            i = 3 * stage - 2 + k
            copy = remote(box, box, self.sends.at[i], self.recvs.at[i], peer)
            copy.start()
            self.out.append(copy)

    def finish(self, stage):
        if stage == 0:
            self.out[0].wait_recv()
            self.boxes[0][self.me[0]] = self.sums[...] + self.pair[...]
            return
        for copy in self.out[3 * stage - 2 : 3 * stage + 1]:
            copy.wait_recv()
        box = self.boxes[stage - 1]
        total = box[0] + box[1] + box[2] + box[3]
        self.target[stage - 1][...] = total


SMALL = ((0, 2), (2, 3), (3, 5), (5, 7), (7, 8))
SMALL_BACK = ((7, 8), (4, 5), (3, 4), (0, 3), (5, 7))
THIRDS = 3
Z_LAST = (4, 9)
Z_FIRST_BACK = (0, 6)
NAMES = ("nrm", "io", "sm", "cm")
WIDE = ("after_self", "after_cross", "acc_out", "acc_up")


def whole_kernel(own_images, *refs):
    refs = list(refs)

    def take(n):
        out = refs[:n]
        del refs[:n]
        return out

    shards, (rows_in, text_in, top_in, lengths), vectors = take(10), take(4), take(6)
    fins, (layer_out, text_out, rows_out, norm_out, spill) = take(3), take(5)
    full_s, full_in, full_out, pair_s, pair_in, pair_out = take(6)
    bufs = [take(9) for _ in range(2 * THIRDS + len(SMALL_BACK))]
    narrow, wide = take(len(NAMES)), take(len(WIDE))
    qkv, cq, mkv, t2, t3, rows, ps, valid, norms = take(9)
    norm_sums, norm_pair, norm_plane, norm_line = take(4)
    (psend, precv, gsend, grecv, hsend, hrecv, rsend, rrecv, bsend, brecv, nsend, nrecv, local) = refs
    at = Place()
    greet(at)
    layer = Layer(
        own_images=own_images,
        full_s=full_s,
        full_in=full_in,
        full_out=full_out,
        rows=rows,
        qkv=qkv,
        cq=cq,
        mkv=mkv,
        ps=ps,
        t2=t2,
        t3=t3,
        lengths=lengths,
        valid=valid,
        norms=norms,
        norm_grads=norm_sums,
        **dict(zip(NAMES, narrow)),
        **dict(zip(WIDE, wide)),
    )
    half, dmodel = full_s.shape[4:]
    lanes, half_in, lanes_out = dmodel // 2, full_in.shape[4], full_out.shape[5] // 2

    pairs = [pair_s.at[i] for i in range(8)] + [pair_in]
    own, other = [], []
    for i in range(9):
        depth = shards[i].shape[0]
        mine = pairs[i].at[pl.ds(pl.multiple_of(at.c * depth, 8), depth), :]
        other.append(remote(shards[i], mine, psend.at[i], precv.at[i], at.sib))
        own.append(pltpu.make_async_copy(shards[i], mine, local.at[i]))
    for core, peer in ((at.c, None), (at.oc, at.sib)):
        src = shards[9].at[pl.ds(pl.multiple_of(core * half, 16), half), :]
        if peer is None:
            own.append(pltpu.make_async_copy(src, pair_out.at[at.c], local.at[9]))
        else:
            other.append(remote(src, pair_out.at[at.c], psend.at[9], precv.at[9], peer))
    for a, b in zip(other, own):
        a.start()
        b.start()
    load = pltpu.make_async_copy(text_in, layer.io, local.at[10])
    load.start()

    def ready(i):
        own[i].wait()
        if i < 9:
            depth = shards[i].shape[0]
            theirs = pairs[i].at[pl.ds(pl.multiple_of(at.oc * depth, 8), depth), :]
        else:
            theirs = pair_out.at[at.oc]
        remote(theirs, theirs, psend.at[i], precv.at[i], at.sib).wait_recv()

    x_lanes = pl.ds(pl.multiple_of(at.x * lanes, 128), lanes)

    def lay_small(w):
        ready(w)
        block = dot_nt(pick(half, 2 * half, at.c * half), pair_s[w])
        full_s[w, at.z, at.y, at.c, :, x_lanes] = block.astype(BF)

    def lay_third(s, part):
        if part == 0:
            start = 2 * half_in * s + at.c * half_in
            block = dot_nt(pick(half_in, pair_in.shape[1], start), pair_in[...])
            full_in[s, at.z, at.y, at.c, :, x_lanes] = block.astype(BF)
            return
        for b in range(4):
            lo = pl.multiple_of(at.x * lanes_out + 128 * b, 128)
            cut = (b % 2) * (128 * THIRDS) + 128 * s
            full_out[s, at.z, at.y, at.c, :, pl.ds(lo, 128)] = pair_out[
                b // 2, :, cut : cut + 128
            ]

    def gather(full, span, via_y, n):
        form = GatherLast if n in Z_LAST else Gather
        return form(at, full, span, via_y, gsend, grecv, n)

    g_small = [
        gather(full_s, slice(*span), 128, g)
        for g, span in enumerate(SMALL)
    ]
    g_feed = []
    for s in range(THIRDS):
        index = len(SMALL) + 2 * s
        span = slice(s, s + 1)
        g_feed.append(
            (
                gather(full_in, span, 128, index),
                gather(full_out, span, 256, index + 1),
            )
        )

    def begin(group):
        for w in range(group.span.start, group.span.stop):
            lay_small(w)
        group.begin()

    arrived = []

    def begin_third(s, part):
        if part not in arrived:
            arrived.append(part)
            ready(8 + part)
        lay_third(s, part)
        g_feed[s][part].begin()

    here = pl.ds(pl.multiple_of(at.m * own_images, 8), own_images)
    keep = pltpu.make_async_copy(rows_in.at[:, here, :], rows.at[at.m], local.at[11])

    def begin_memory():
        for k in range(1, 8):
            to = lax.rem(at.m + k, 8) * own_images
            src = rows_in.at[:, pl.ds(pl.multiple_of(to, 8), own_images), :]
            remote(src, rows.at[at.m], rsend.at[0], rrecv.at[k - 1], at.mpeer(k)).start()
        keep.start()

    for i, vector in enumerate(vectors):
        norms[i : i + 1, :] = vector[...].reshape(1, dmodel)
    row = lax.broadcasted_iota(jnp.int32, valid.shape, 0)
    limit = jnp.zeros(valid.shape, jnp.int32)
    for i in range(own_images):
        first = i * layer.txt
        limit = jnp.where(row >= first, first + lengths[i], limit)
    valid[...] = jnp.where(row < limit, 1.0, 0.0).astype(BF)

    def each(groups, name):
        for group in groups:
            getattr(group, name)()

    seven = rows.at[pl.ds(0, 7)]

    def end_memory():
        keep.wait()
        for k in range(1, 8):
            ref = rows.at[lax.rem(at.m + 8 - k, 8)]
            remote(ref, ref, rsend.at[0], rrecv.at[k - 1], at.sib).wait_recv()

    def drain_small():
        for copy in other:
            copy.wait_send()
        remote(seven, seven, rsend.at[0], rrecv.at[0], at.sib).wait_send()
        each(g_small, "drain")

    def send_memory():
        for k in range(1, 8):
            src, dst = rows.at[lax.rem(at.m + k, 8)], rows_out.at[:, here, :]
            remote(src, dst, bsend.at[0], brecv.at[k - 1], at.mpeer(k)).start()
        keep_back.start()

    def move(src, dst, i):
        return pltpu.make_async_copy(src, dst, local.at[i])

    top, text = move(top_in, layer.io, 10), move(text_in, layer.sm, 10)
    away, again = move(ps, spill, 13), move(spill, ps, 13)
    packed = t3.at[:, 0:dmodel]
    save_out, save_text = move(packed, layer_out, 12), move(packed, text_out, 12)
    keep_back = move(rows.at[at.m], rows_out.at[:, here, :], 11)
    norm = NormSum(at, norm_sums, norm_pair, norm_plane, norm_line, norm_out, nsend, nrecv)
    fin_s, fin_in, fin_out = fins
    stores = []

    def store(group, out):
        group.last()
        copy = move(group.fin, out.at[group.span], 14 + len(stores))
        copy.start()
        stores.append(copy)

    def reduce(full, span, n):
        form = ReduceFirst if n in Z_FIRST_BACK else Reduce
        return form(at, full, span, bufs[n], hsend, hrecv, n)

    r_feed, r_small = [], []
    for s in range(THIRDS):
        span = slice(s, s + 1)
        r_feed.append(
            [
                reduce(full, span, 2 * s + i)
                for i, full in enumerate((full_in, full_out))
            ]
        )
    for g, span in enumerate(SMALL_BACK):
        n = 2 * THIRDS + g
        r_small.append(reduce(full_s, slice(*span), n))

    begin(g_small[1])
    begin(g_small[2])
    begin_third(0, 1)
    begin(g_small[0])
    g_small[1].second(1)
    begin_third(2, 1)
    begin_third(2, 0)
    begin(g_small[4])
    begin_third(0, 0)
    g_small[2].second(1)
    begin(g_small[3])
    g_small[0].second(1)
    g_small[1].second(2)
    g_small[2].second(2)
    g_small[3].second(1)
    g_small[4].third(0)
    load.wait()
    layer.norm_into(layer.io, 0)
    g_small[4].third(1)
    g_small[0].second(2)
    g_feed[2][1].second(1)
    g_small[1].second(3)
    g_feed[0][0].second(1)
    g_feed[0][1].second(1)
    begin_third(1, 0)
    begin_third(1, 1)
    g_small[3].second(2)
    g_small[0].second(3)
    g_feed[0][0].second(2)
    g_feed[1][1].second(1)
    begin_memory()
    g_small[1].third(1)
    g_small[2].second(3)
    g_small[1].third(0)
    g_small[3].second(3)
    g_small[0].third(1)
    g_small[0].third(0)
    g_feed[2][0].third(0)
    g_small[4].fourth()
    g_small[2].third(1)
    g_small[2].third(0)
    g_feed[0][1].second(2)
    g_feed[0][0].second(3)
    g_small[3].third(0)
    g_small[0].fourth()
    g_feed[2][0].third(1)
    g_small[1].fourth()
    g_small[3].third(1)
    g_small[0].last()
    g_small[1].last()
    g_feed[1][0].second(1)
    g_feed[1][1].second(2)
    layer.project(layer.qkv, lambda: layer.nrm[...], 0)
    g_feed[0][1].second(3)
    g_feed[2][0].fourth()
    g_small[4].second(1)
    layer.self_forward(0, 2)
    g_small[2].fourth()
    g_feed[1][0].second(2)
    layer.self_forward(2, 4)
    away.start()
    g_feed[0][0].third(1)
    g_small[2].last()
    layer.add_after_self()
    top.start()
    g_feed[2][0].second(1)
    g_feed[2][1].second(2)
    layer.norm_into(layer.after_self, 1)
    layer.project(layer.cq, lambda: layer.nrm[...], 4)
    g_feed[1][0].second(3)
    g_feed[1][1].second(3)
    g_feed[0][1].third(0)
    g_small[3].fourth()
    g_small[4].second(2)
    end_memory()
    layer.memory_in()
    g_small[3].last()
    g_feed[2][1].second(3)
    g_feed[0][0].third(0)
    layer.project(layer.mkv, layer.memory, 5)
    g_feed[0][1].third(1)
    away.wait()
    layer.cross_forward(0, 4)
    g_feed[2][0].second(2)
    g_feed[1][0].third(0)
    g_feed[1][0].third(1)
    g_small[4].second(3)
    g_feed[1][1].third(1)
    g_feed[1][1].third(0)
    layer.cross_forward(4, 8)
    g_small[4].last()
    g_feed[0][1].fourth()
    layer.add_after_cross()
    g_feed[0][0].fourth()
    g_feed[2][1].third(1)
    layer.norm_into(layer.after_cross, 2)
    top.wait()
    layer.mask_top()
    layer.feed_start()
    drain_small()
    g_feed[0][1].last()
    g_feed[2][1].third(0)
    g_feed[0][0].last()
    g_feed[1][0].fourth()
    g_feed[1][1].fourth()
    each(g_feed[0], "drain")
    layer.feed_chunk(0)
    g_feed[2][0].second(3)
    g_feed[1][1].last()
    g_feed[2][1].fourth()
    r_feed[0][1].begin()
    g_feed[1][0].last()
    each(g_feed[1], "drain")
    layer.feed_chunk(1)
    g_feed[2][0].last()
    r_feed[0][1].second()
    r_feed[1][1].begin()
    r_feed[1][0].begin()
    g_feed[2][1].last()
    each(g_feed[2], "drain")
    layer.feed_chunk(2)
    r_feed[1][1].second()
    r_feed[2][1].begin()
    r_feed[0][1].third(1)
    r_feed[1][0].second()
    layer.third_back()
    layer.output_back(7, layer.cm, t2)
    r_feed[2][1].second()
    r_feed[2][0].begin()
    r_small[0].begin()
    layer.cross_back(0, 4)
    r_feed[2][0].second()
    r_feed[1][1].third(1)
    r_small[0].second()
    r_feed[1][0].third(1)
    r_feed[1][1].third(0)
    r_feed[0][1].third(0)
    r_feed[0][0].begin()
    layer.cross_back(4, 8)
    again.start()
    layer.memory_back()
    layer.weight_grads(layer.mkv, layer.memory, 5)
    r_feed[0][0].second()
    r_feed[2][1].third(1)
    r_small[4].begin()
    r_small[0].relay(0)
    r_feed[1][0].third(0)
    layer.memory_out()
    layer.layer_out(t3)
    save_out.start()
    layer.second_up()
    r_feed[2][1].third(0)
    r_small[4].second()
    r_feed[2][0].third(1)
    layer.second_back()
    send_memory()
    layer.output_back(3, layer.sm, t2)
    text.start()
    layer.norm_into(layer.after_self, 1)
    layer.weight_grads(layer.cq, lambda: layer.nrm[...], 4)
    r_feed[1][1].fourth()
    r_feed[0][1].fourth()
    r_small[2].begin()
    again.wait()
    layer.self_back(0, 2)
    r_small[4].third(0)
    r_small[1].begin()
    layer.self_back(2, 4)
    r_small[4].third(1)
    r_feed[2][1].fourth()
    text.wait()
    layer.norm_into(layer.sm, 0)
    layer.first_up()
    r_feed[2][0].third(0)
    layer.weight_grads(layer.qkv, lambda: layer.nrm[...], 0)
    r_small[1].second()
    r_small[3].begin()
    r_small[2].second()
    r_feed[0][0].relay(0)
    r_small[3].second()
    save_out.wait()
    layer.first_back(layer.sm, t3)
    save_text.start()
    r_feed[2][0].fourth()
    r_small[0].relay(1)
    r_feed[0][1].relay(0)
    r_small[1].third(0)
    r_small[4].fourth()
    r_small[1].third(1)
    r_small[3].third(0)
    r_feed[1][0].fourth()
    r_feed[2][0].relay(0)
    r_small[3].third(1)
    r_feed[2][1].relay(0)
    r_feed[1][1].relay(0)
    r_small[1].fourth()
    r_feed[0][0].relay(1)
    r_small[1].relay(0)
    r_small[3].fourth()
    r_feed[2][1].relay(1)
    r_small[0].fourth()
    r_small[2].third(1)
    r_feed[0][0].fourth()
    norm.start(0)
    r_feed[1][0].relay(0)
    r_small[4].relay(0)
    r_small[2].third(0)
    r_feed[2][0].relay(1)
    r_small[3].relay(0)
    r_feed[0][0].third(1)
    r_small[0].third(1)
    r_feed[1][0].relay(1)
    r_small[2].fourth()
    norm.finish(0)
    norm.start(1)
    r_feed[0][1].relay(1)
    r_small[1].relay(1)
    r_feed[0][0].third(0)
    r_small[4].relay(1)
    r_feed[1][1].relay(1)
    r_small[2].relay(0)
    norm.finish(1)
    norm.start(2)
    r_small[0].third(0)
    r_small[3].relay(1)
    r_small[2].relay(1)
    r_feed[0][1].fifth()
    r_feed[0][0].fifth()
    r_feed[1][1].fifth()
    r_feed[1][0].fifth()
    r_feed[2][0].fifth()
    r_feed[2][1].fifth()
    r_small[0].fifth()
    r_small[1].fifth()
    r_small[4].fifth()
    store(r_feed[2][1], fin_out)
    store(r_feed[0][1], fin_out)
    store(r_feed[0][0], fin_in)
    store(r_small[1], fin_s)
    store(r_feed[2][0], fin_in)
    store(r_feed[1][1], fin_out)
    store(r_small[0], fin_s)
    norm.finish(2)
    r_small[3].fifth()
    r_small[2].fifth()
    store(r_feed[1][0], fin_in)
    store(r_small[4], fin_s)
    store(r_small[3], fin_s)
    store(r_small[2], fin_s)
    save_text.wait()
    keep_back.wait()
    for k in range(1, 8):
        m = lax.rem(at.m + 8 - k, 8)
        there = pl.ds(pl.multiple_of(m * own_images, 8), own_images)
        ref = rows_out.at[:, there, :]
        remote(ref, ref, bsend.at[0], brecv.at[k - 1], at.sib).wait_recv()
    remote(seven, seven, bsend.at[0], brecv.at[0], at.sib).wait_send()
    for copy in norm.out:
        copy.wait_send()
    each(r_small, "drain")
    for groups in r_feed:
        each(groups, "drain")
    for copy in stores:
        copy.wait()


def whole(shards, rows, text, top, lengths, vectors):
    depth, width = shards[0].shape
    dmodel = depth * 4
    half = width // 2
    lanes = dmodel // 2
    ff = shards[8].shape[1] * 8
    units = ff // THIRDS
    half_in = units // 16
    shapes = [
        (8, 4, 2, 2, half, dmodel),
        (THIRDS, 4, 2, 2, half_in, dmodel),
        (THIRDS, 4, 2, 2, half, units),
    ]
    tokens = text.shape[0]
    images = lengths.shape[0]
    mem_rows = rows.shape[0] * rows.shape[1]
    groups = dmodel // 256
    any_ = pl.BlockSpec(memory_space=pl.ANY)
    vmem = pl.BlockSpec(memory_space=pltpu.VMEM)
    smem = pl.BlockSpec(memory_space=pltpu.SMEM)
    sems = pltpu.SemaphoreType.DMA
    scratch = [pltpu.VMEM(s, BF) for s in shapes]
    scratch += [
        pltpu.VMEM((8, 2 * depth, width), BF),
        pltpu.VMEM((2 * depth, 4 * width), BF),
        pltpu.VMEM((2, half, 4 * depth), BF),
    ]
    for s in range(THIRDS):
        n = 2 * s
        scratch += reduce_bufs(1, half_in, lanes, 128, n in Z_FIRST_BACK)
        scratch += reduce_bufs(1, half, units // 2, 256, n + 1 in Z_FIRST_BACK)
    for n, (a, b) in enumerate(SMALL_BACK, 2 * THIRDS):
        scratch += reduce_bufs(b - a, half, lanes, 128, n in Z_FIRST_BACK)
    scratch += [pltpu.VMEM((tokens, dmodel), BF) for _ in NAMES]
    scratch += [pltpu.VMEM((tokens, dmodel), F32) for _ in WIDE]
    stacks = [(3, tokens, dmodel), (1, tokens, dmodel), (2, mem_rows, dmodel)]
    scratch += [pltpu.VMEM(s, BF) for s in stacks]
    scratch += [
        pltpu.VMEM((tokens, units), BF),
        pltpu.VMEM((tokens, units), BF),
        pltpu.VMEM((8, rows.shape[0], images, dmodel), BF),
        pltpu.VMEM((images // 2, groups, 512, 128), BF),
        pltpu.VMEM((tokens, 128), BF),
        pltpu.VMEM((8, dmodel), F32),
        pltpu.VMEM((8, dmodel), F32),
        pltpu.VMEM((8, dmodel), F32),
        pltpu.VMEM((4, 8, dmodel), F32),
        pltpu.VMEM((4, 8, dmodel), F32),
    ]
    gathers = len(SMALL) + 2 * THIRDS
    reduces = len(SMALL_BACK) + 2 * THIRDS
    counts = (10, 10, Gather.SENDS * gathers, Gather.RECVS * gathers)
    counts += (reduces, Reduce.RECVS * reduces, 1, 7, 1, 7, 7, 7, 14 + reduces)
    scratch += [sems((n,)) for n in counts]
    return pl.pallas_call(
        functools.partial(whole_kernel, images),
        out_shape=[
            jax.ShapeDtypeStruct((8, 2, half, lanes), BF),
            jax.ShapeDtypeStruct((THIRDS, 2, half_in, lanes), BF),
            jax.ShapeDtypeStruct((THIRDS, 2, half, units // 2), BF),
            jax.ShapeDtypeStruct(text.shape, BF),
            jax.ShapeDtypeStruct(text.shape, BF),
            jax.ShapeDtypeStruct(rows.shape, BF),
            jax.ShapeDtypeStruct((8, dmodel), F32),
            jax.ShapeDtypeStruct((images // 2, groups, 512, 128), BF),
        ],
        in_specs=[any_] * 13 + [smem] + [vmem] * 6,
        out_specs=[any_] * 6 + [vmem, any_],
        scratch_shapes=scratch,
        compiler_params=pltpu.CompilerParams(
            collective_id=0, has_side_effects=True, vmem_limit_bytes=63 << 20
        ),
    )(*shards, rows, text, top, lengths, *vectors)


def finish_kernel(*refs):
    fin_s, fin_in, fin_out, norm, *moved = refs[:7]
    outs, norm_outs, targets, sem = refs[7:17], refs[17:23], refs[23:26], refs[26]
    copies = []
    for i, (a, b) in enumerate(zip(moved, targets)):
        copy = pltpu.make_async_copy(a, b, sem.at[i])
        copy.start()
        copies.append(copy)
    c = lax.rem(lax.axis_index("dp"), 2)
    depth = outs[0].shape[0]
    sel = pick(depth, 2 * depth, c * depth)
    for w in range(8):
        both = fin_s[w].reshape(outs[w].shape[1], 2 * depth)
        outs[w][...] = dot_nt(sel, both)
    outs[8][...] = dot_nt(sel, fin_in[...].reshape(outs[8].shape[1], 2 * depth))
    half = fin_out.shape[2]
    for s in range(THIRDS):
        for h in range(2):
            for b in range(2):
                lo = pl.multiple_of(c * 256 + 128 * b, 128)
                cut = b * (128 * THIRDS) + 128 * s
                outs[9][half * h : half * (h + 1), cut : cut + 128] = fin_out[
                    s, h, :, pl.ds(lo, 128)
                ].astype(F32)
    for i, out in enumerate(norm_outs):
        out[...] = norm[i : i + 1, :].reshape(out.shape)
    for copy in copies:
        copy.wait()


def finish(fin_s, fin_in, fin_out, norm, moved, shapes):
    any_ = pl.BlockSpec(memory_space=pl.ANY)
    vmem = pl.BlockSpec(memory_space=pltpu.VMEM)
    return pl.pallas_call(
        finish_kernel,
        out_shape=[jax.ShapeDtypeStruct(s, F32) for s in shapes]
        + [jax.ShapeDtypeStruct(norm.shape[1:], F32)] * 6
        + [jax.ShapeDtypeStruct(a.shape, a.dtype) for a in moved],
        in_specs=[vmem] * 7,
        out_specs=[vmem] * 16 + [any_] * 3,
        scratch_shapes=[pltpu.SemaphoreType.DMA((3,))],
    )(fin_s, fin_in, fin_out, norm, *moved)


def fits(mesh_shape, text, memory, mats):
    images, txt, dmodel = text.shape
    depth, width = mats[0].shape
    return (
        mesh_shape["dp"] == 4
        and mesh_shape["mem"] == 8
        and images == 8
        and txt == HEAD == 64
        and memory.shape[0] == 8 * images
        and (memory.shape[1] * 8) % 32 == 0
        and memory.shape[1] * 8 <= 128
        and dmodel == HEADS * HEAD == 4 * depth == 8 * width
        and dmodel % 256 == 0
        and width % 32 == 0
        and mats[8].shape == (depth, 4 * width)
        and 4 * width == 128 * THIRDS
        and mats[9].shape == (4 * depth, width)
    )


def shards_lean(text, lengths, memory, out_grad, *params):
    mats, vectors = params[:10], params[10:]
    images, txt, dmodel = text.shape
    tokens = images * txt
    mats = mats[:9] + (mats[9].T,)
    fin_s, fin_in, fin_out, layer_out, text_grad, back, norm_sums, _ = whole(
        mats,
        memory.transpose(1, 0, 2),
        text.reshape(tokens, dmodel),
        out_grad.reshape(tokens, dmodel),
        lengths,
        vectors,
    )
    *grads, layer_out, text_grad, back = finish(
        fin_s,
        fin_in,
        fin_out,
        norm_sums,
        (layer_out, text_grad, back),
        [mat.shape for mat in mats],
    )
    return (
        layer_out.reshape(text.shape),
        text_grad.reshape(text.shape),
        back.transpose(1, 0, 2),
        *grads[:9],
        grads[9].T,
        *grads[10:],
    )


def solution(mesh):
    def pick_form(text, lengths, memory, out_grad, *params):
        lean = fits(mesh.shape, text, memory, params[:10])
        form = shards_lean if lean else shards
        return form(text, lengths, memory, out_grad, *params)

    return jax.shard_map(
        pick_form,
        mesh=mesh,
        in_specs=(
            P(("dp", "mem"), None, None),
            P(("dp", "mem")),
            P("dp", "mem", None),
            P(("dp", "mem"), None, None),
            P("dp", "mem"),
            P("dp", "mem"),
            P("dp", "mem"),
            P("dp", "mem"),
            P("dp", "mem"),
            P("dp", "mem"),
            P("dp", "mem"),
            P("dp", "mem"),
            P("dp", "mem"),
            P("dp", "mem"),
            P(),
            P(),
            P(),
            P(),
            P(),
            P(),
        ),
        out_specs=(
            P(("dp", "mem"), None, None),
            P(("dp", "mem"), None, None),
            P("dp", "mem", None),
            P("dp", "mem"),
            P("dp", "mem"),
            P("dp", "mem"),
            P("dp", "mem"),
            P("dp", "mem"),
            P("dp", "mem"),
            P("dp", "mem"),
            P("dp", "mem"),
            P("dp", "mem"),
            P("dp", "mem"),
            P(),
            P(),
            P(),
            P(),
            P(),
            P(),
        ),
        check_vma=False,
    )
```
